32 devices in a mesh: row: 8 (over y, x, core), col: 4 (over z).
Axes of the slice: x: 2, y: 2, z: 4, core: 2. Of those that a mesh axis runs over, the one named last changes fastest.
Arguments:
- col_samples: float32 [16, 2, 2048, 128], P('row', None, 'col'), may hold values from -6 to 6
- row_samples: float32 [16, 2, 128, 2048], P('row', None, None, 'col'), may hold values from -6 to 6
- pivot_rows: int32 [16, 128], P('row'), may hold values from 0 to 2047
- rank_blocks: int32 [16], P('row'), may hold values from 1 to 8
- upper_inverse: float32 [2, 2048, 2048], P(None, 'col', 'row'), as said below
- upanel_left: float32 [4, 2, 2048, 128], P('col'), may hold values from -0.125 to 0.125
Outputs:
- panel_right: float32 [16, 2, 128, 2048], P('row', None, None, 'col')
- cores: float32 [16, 4, 2, 128, 128], P('row', 'col')
The draws below stay inside these ranges and needn't reach their ends.
Inputs may be any that keep to these rules, and one draw needn't show every extreme that they name: `rank_blocks`: the tile's rank is 16 times this. `upper_inverse`: zero below the diagonal in both parts.
All inputs are finite; a program needn't handle non-finite values.
Results may differ from the reference program's by a relative error of at most 0.00007.
Values sent between devices are 32-bit elements; how exact they have to be, the bound alone decides.
A program may use at most 64 MiB of HBM per device.

```python
import jax
import jax.numpy as jnp
from jax import lax

B = 2048
R = 128
RANK_STEP = 16
NT = 16
NJ = 4


def draw_upper_inverse(key, part):
    first_key, second_key = jax.random.split(key)
    base = jax.random.normal(first_key, (2, B, B), jnp.float32)
    rows_index = lax.broadcasted_iota(jnp.int32, (2, B, B), 1)
    cols_index = lax.broadcasted_iota(jnp.int32, (2, B, B), 2)
    component = lax.broadcasted_iota(jnp.int32, (2, B, B), 0)
    upper = jnp.where(cols_index >= rows_index, base * (1.0 / B ** 0.5), 0.0)
    diagonal = jax.random.uniform(second_key, (2, B, B), jnp.float32, 0.5, 1.5)
    on_diagonal = (cols_index == rows_index) & (component == 0)
    return upper + jnp.where(on_diagonal, diagonal, 0.0)


def plant(drawn, rng, low, top_value):
    dims = drawn.shape
    spot = [jax.random.randint(jax.random.fold_in(rng, axis), (), 0, dims[axis]) for axis in range(len(dims))]
    drawn = drawn.at[tuple(spot)].set(low)
    longest = dims.index(max(dims))
    spot[longest] = (spot[longest] + 1) % dims[longest]
    return drawn.at[tuple(spot)].set(top_value)


def block_levels(rng, shape, cuts, least, largest):
    gain = 1.0
    for position, blocks in cuts:
        heights = jax.random.uniform(jax.random.fold_in(jax.random.fold_in(rng, 6), position), (blocks,), jnp.float32, least / len(cuts), largest / len(cuts))
        gain = gain * jnp.repeat(jnp.exp(heights), shape[position] // blocks).reshape((-1,) + (1,) * (len(shape) - 1 - position))
    return gain


def normal_values(rng, dims, deviation, limit, shards=(), kind=jnp.bfloat16):
    values = deviation * jax.random.normal(rng, dims, jnp.float32)
    if shards:
        values = values * block_levels(rng, dims, shards, -0.22, 0.18)
    return jnp.clip(values, -limit, limit).astype(kind)


def setup_inputs(seed: int = 0) -> dict:
    streams_of = jax.random.split(jax.random.key(seed), 7)
    col_samples = normal_values(streams_of[0], (NT, 2, B, R), 1.0, 6.0, ((0, 8), (2, 4)), jnp.float32)
    row_samples = normal_values(streams_of[1], (NT, 2, R, B), 1.0, 6.0, ((0, 8), (3, 4)), jnp.float32)
    pivot_rows = plant(jax.random.randint(streams_of[2], (NT, R), 0, B), jax.random.fold_in(streams_of[2], 1), 0, B - 1).astype(jnp.int32)
    rank_blocks = plant(jax.random.randint(streams_of[3], (NT,), 1, R // RANK_STEP + 1), jax.random.fold_in(streams_of[3], 1), 1, (R // RANK_STEP + 1) - 1).astype(jnp.int32)
    upper_inverse = draw_upper_inverse(jax.random.fold_in(streams_of[6], 71), 0)
    upanel_left = normal_values(streams_of[5], (NJ, 2, B, R), B ** -0.5, 0.125, ((0, 4),), jnp.float32)
    return {"col_samples": col_samples, "row_samples": row_samples, "pivot_rows": pivot_rows, "rank_blocks": rank_blocks, "upper_inverse": upper_inverse, "upanel_left": upanel_left}


def complex_product(pattern, left_real, left_imag, right_real, right_imag):
    def single(left, right):
        return jnp.einsum(pattern, left, right, precision=lax.Precision.HIGHEST, preferred_element_type=jnp.float32)
    real_part = single(left_real, right_real) - single(left_imag, right_imag)
    imag_part = single(left_real, right_imag) + single(left_imag, right_real)
    return real_part, imag_part


def scale_rows(values, weight_real, weight_imag):
    wr = weight_real[:, :, None]
    wi = weight_imag[:, :, None]
    real_part = values[:, 0] * wr - values[:, 1] * wi
    imag_part = values[:, 0] * wi + values[:, 1] * wr
    return jnp.stack((real_part, imag_part), axis=1)


def reference(col_samples, row_samples, pivot_rows, rank_blocks, upper_inverse, upanel_left):
    count = col_samples.shape[0]
    index = jnp.broadcast_to(pivot_rows[:, None, None, :], (count, 2, 1, R)).astype(jnp.int32)
    entries = jnp.take_along_axis(col_samples, index, axis=2)[:, :, 0, :]
    levels = lax.broadcasted_iota(jnp.int32, (1, R), 1)
    keeping = (levels < RANK_STEP * rank_blocks[:, None]).astype(jnp.float32)
    magnitude = jnp.maximum(entries[:, 0] * entries[:, 0] + entries[:, 1] * entries[:, 1], 1.0)
    factor_real = keeping * entries[:, 0] / magnitude
    factor_imag = -keeping * entries[:, 1] / magnitude
    scaled = scale_rows(row_samples, factor_real, factor_imag)
    real_part, imag_part = complex_product("trk,kn->trn", scaled[:, 0], scaled[:, 1], upper_inverse[0], upper_inverse[1])
    panel_right = jnp.stack((real_part, imag_part), axis=1)
    core_real, core_imag = complex_product("trn,jns->tjrs", panel_right[:, 0], panel_right[:, 1], upanel_left[:, 0], upanel_left[:, 1])
    cores = jnp.stack((core_real, core_imag), axis=2)
    return panel_right, cores
```

```python
import functools
import math

import jax
import jax.numpy as jnp
from jax import lax
from jax.experimental import pallas as pl
from jax.experimental.pallas import tpu as pltpu
from jax.sharding import PartitionSpec as P

RANK_STEP = 16
MESH = pl.DeviceIdType.MESH


def split(x):
    high = x.astype(jnp.bfloat16)
    low = (x - high.astype(jnp.float32)).astype(jnp.bfloat16)
    return high, low


def dot3(xh, xl, uh, ul):
    def single(a, b):
        return jnp.dot(a, b, preferred_element_type=jnp.float32)

    return single(xh, uh) + (single(xh, ul) + single(xl, uh))


def kernel(
    n_rows, n_cols,
    row_ref, u_ref, up_ref, col_ref, piv_ref, rank_ref,
    panel_ref, cores_ref,
    xh, xl, ch, cl, us, ps, pr, fin, lz, lg, ks, kr, eb,
    u_loc, u_send, u_sib, u_fwd, u_recv,
    p_send, p_recv,
    lz_loc, lz_send, lz_recv, lg_loc, lg_send, lg_sib, lg_fwd, lg_recv,
    k_send, k_recv, e_send, e_recv,
):
    r, c = lax.axis_index("row"), lax.axis_index("col")
    chips = n_rows // 2
    nx = math.isqrt(chips)
    ny = chips // nx
    q, h = r // 2, r % 2
    qy, qx = q // nx, q % nx
    tiles, _, ranks, wc = row_ref.shape
    nsub, sw = us.shape[1], us.shape[4]
    wq = lz.shape[1]
    half = tiles * ranks
    sib = (q * 2 + 1 - h, c)

    def ahead(d):
        return ((qy + d // nx) % ny) * nx + (qx + d % nx) % nx

    def behind(d):
        return ((qy + ny - d // nx) % ny) * nx + (qx + nx - d % nx) % nx

    def rcopy(src, dst, ssem, rsem, dev):
        return pltpu.make_async_remote_copy(
            src_ref=src, dst_ref=dst, send_sem=ssem, recv_sem=rsem, device_id=dev, device_id_type=MESH
        )

    def u_out(d, s):
        return rcopy(
            u_ref.at[:, :, s * sw:(s + 1) * sw], us.at[r, s], u_send.at[d, s], u_recv.at[r, s],
            (behind(d) * 2 + h, c),
        )

    def u_side(s):
        return rcopy(u_ref.at[:, :, s * sw:(s + 1) * sw], us.at[r, s], u_sib.at[s], u_recv.at[r, s], sib)

    def u_forward(t, s, b):
        return rcopy(us.at[b, s], us.at[b, s], u_fwd.at[t, s], u_recv.at[b, s], sib)

    def p_up(b, s):
        return rcopy(ps.at[b, s], pr.at[b, s], p_send.at[b, s], p_recv.at[b, s], (r, c + 1))

    def lz_out(k):
        to = (c + k) % n_cols
        start = pl.multiple_of(to * wc + q * wq, wq)
        return rcopy(up_ref.at[0, h, pl.ds(start, wq), :], lz.at[c], lz_send.at[k], lz_recv.at[c], (r, to))

    def lg_out(d):
        return rcopy(lz, lg.at[h, q], lg_send.at[d], lg_recv.at[h, q], (behind(d) * 2 + h, c))

    def lg_side():
        return rcopy(lz, lg.at[h, q], lg_sib.at[0], lg_recv.at[h, q], sib)

    def lg_forward(d):
        b = ahead(d)
        return rcopy(lg.at[h, b], lg.at[h, b], lg_fwd.at[d], lg_recv.at[h, b], sib)

    def k_out(k):
        to = (c + k) % n_cols
        return rcopy(ks.at[k], kr.at[c], k_send.at[k], k_recv.at[c], (r, to))

    def e_out(k):
        return rcopy(eb.at[c], eb.at[c], e_send.at[k], e_recv.at[c], (r, (c + k) % n_cols))

    def each(first, last, body):
        lax.fori_loop(first, last, lambda i, z: (body(i), z)[1], 0)

    own = [
        pltpu.make_async_copy(u_ref.at[:, :, s * sw:(s + 1) * sw], us.at[r, s], u_loc.at[s]) for s in range(nsub)
    ]
    for copy in own:
        copy.start()
    mine = pl.multiple_of(c * wc + q * wq, wq)
    lz_own = pltpu.make_async_copy(up_ref.at[0, h, pl.ds(mine, wq), :], lz.at[c], lz_loc.at[0])
    lz_own.start()
    barrier = pltpu.get_barrier_semaphore()

    def signal(dev):
        pl.semaphore_signal(barrier, inc=1, device_id=dev, device_id_type=MESH)

    signal(sib)
    each(1, chips, lambda d: signal((behind(d) * 2 + h, c)))
    each(1, n_cols, lambda k: signal((r, (c + k) % n_cols)))
    pl.semaphore_wait(barrier, 1 + (chips - 1) + (n_cols - 1))

    @pl.when(q >= c)
    def _():
        for s in range(nsub):
            u_side(s).start()

        @pl.when(q > 0)
        def _():
            for s in range(nsub):
                each(1, chips, lambda d: u_out(d, s).start())

    each(1, n_cols, lambda k: lz_out(k).start())

    for i in range(tiles):
        for p in range(2):
            a, b = split(row_ref[i, p])
            at = pl.ds(p * half + i * ranks, ranks)
            xh[at, :] = a
            xl[at, :] = b

    pos = c * wc + lax.broadcasted_iota(jnp.int32, (wc, ranks), 0)
    parts = []
    for i in range(tiles):
        hit = pos == piv_ref[i:i + 1, :]
        for p in range(2):
            parts.append(jnp.sum(jnp.where(hit, col_ref[i, p], 0.0), axis=0, keepdims=True))
    parts.append(jnp.zeros((eb.shape[1] - 2 * tiles, ranks), jnp.float32))
    eb[c] = jnp.concatenate(parts, axis=0)
    each(1, n_cols, lambda k: e_out(k).start())
    for copy in own:
        copy.wait()

    near = chips * (nsub - 1)
    total = 2 * (near + chips + nsub - 1)
    spread_at = jnp.where(c == 0, 2, 0)
    final_at = jnp.where(c == 0, total - 1, 2 * (near + chips - 1 - c) + 1)

    def finish():
        def pass_on(d2):
            o = ahead(d2)
            rcopy(lz, lg.at[h, o], lg_send.at[d2], lg_recv.at[h, o], sib).wait_recv()
            lg_forward(d2).start()

        each(1, chips, pass_on)

        each(1, n_cols, lambda k: rcopy(
            eb.at[(c + k) % n_cols], eb.at[(c + k) % n_cols], e_send.at[k], e_recv.at[(c + k) % n_cols], sib
        ).wait_recv())
        entries = jnp.sum(eb[...], axis=0)
        lines = []
        levels = lax.broadcasted_iota(jnp.int32, (1, ranks), 1)
        for i in range(tiles):
            er, ei = entries[2 * i:2 * i + 1], entries[2 * i + 1:2 * i + 2]
            keep = (levels < RANK_STEP * rank_ref[i]).astype(jnp.float32)
            mag = jnp.maximum(er * er + ei * ei, 1.0)
            lines.append(keep * er / mag)
            lines.append(-keep * ei / mag)
        lines.append(jnp.zeros((128 - 2 * tiles, ranks), jnp.float32))
        turned = jnp.concatenate(lines, axis=0).T
        for i in range(tiles):
            fr, fi = turned[:, 2 * i:2 * i + 1], turned[:, 2 * i + 1:2 * i + 2]
            lr, li = i * ranks, half + i * ranks
            vr, vi = [], []
            for hh in range(2):
                for s in range(nsub):
                    vr.append(ps[2 * c + hh, s, lr:lr + ranks, :])
                    vi.append(ps[2 * c + hh, s, li:li + ranks, :])
            vr, vi = jnp.concatenate(vr, axis=1), jnp.concatenate(vi, axis=1)
            wr = vr * fr - vi * fi
            wi = vr * fi + vi * fr
            panel_ref[i, 0] = wr
            panel_ref[i, 1] = wi
            a, b = split(wr)
            ch[lr:lr + ranks, :] = a
            cl[lr:lr + ranks, :] = b
            a, b = split(wi)
            ch[li:li + ranks, :] = a
            cl[li:li + ranks, :] = b

        pltpu.make_async_copy(lz, lg.at[h, q], lg_loc.at[0]).wait()
        each(0, chips, lambda o: rcopy(
            lz, lg.at[1 - h, o], lg_sib.at[0], lg_recv.at[1 - h, o], sib
        ).wait_recv())

        def core(k0, carry):
            k = jnp.where(c == 0, n_cols - 1 - k0, (k0 + 1) % n_cols)
            j = (c + k) % n_cols
            lr = lg[0, :, j].reshape(wc, lz.shape[2])
            li = lg[1, :, j].reshape(wc, lz.shape[2])
            rank2 = lz.shape[2]
            uh, ul = split(jnp.concatenate([lr, li], axis=1))
            prod = dot3(ch[...], cl[...], uh, ul)
            real = prod[:half, :rank2] - prod[half:, rank2:]
            imag = prod[:half, rank2:] + prod[half:, :rank2]
            for i in range(tiles):
                ks[k, i, 0] = real[i * ranks:(i + 1) * ranks]
                ks[k, i, 1] = imag[i * ranks:(i + 1) * ranks]

            @pl.when(k > 0)
            def _():
                k_out(k).start()

            return carry

        lax.fori_loop(0, n_cols, core, 0)

    def unit(u, carry):
        slot = u // 2
        t = jnp.where(slot < near, ahead(slot % chips), jnp.maximum(near + chips - 1 - slot, 0))
        s = jnp.where(slot < near, slot // chips, jnp.where(slot < near + chips, nsub - 1, slot - near - chips))
        live = jnp.logical_and(t >= c, jnp.logical_or(slot >= near, t > 0))
        e = u % 2
        b = t * 2 + (h + e) % 2

        @pl.when(u == spread_at)
        def _():
            lz_own.wait()
            each(1, n_cols, lambda k: rcopy(
                lz.at[(c + k) % n_cols], lz.at[(c + k) % n_cols], lz_send.at[k], lz_recv.at[(c + k) % n_cols], sib
            ).wait_recv())
            lg_side().start()
            pltpu.make_async_copy(lz, lg.at[h, q], lg_loc.at[0]).start()
            each(1, chips, lambda d2: lg_out(d2).start())

            @pl.when(jnp.logical_and(q == 0, q >= c))
            def _():
                for s2 in range(nsub):
                    each(1, chips, lambda d2: u_out(d2, s2).start())

        @pl.when(live)
        def _():
            @pl.when(jnp.logical_or(t != q, e > 0))
            def _():
                u_forward(t, s, b).wait_recv()

            @pl.when(jnp.logical_and(t != q, e == 0))
            def _():
                u_forward(t, s, b).start()

            ur, ui = us[b, s, 0], us[b, s, 1]
            uh, ul = split(jnp.concatenate([ur, ui], axis=1))
            prod = dot3(xh[...], xl[...], uh, ul)
            fin[0:half] = prod[:half, :sw] - prod[half:, sw:]
            fin[half:2 * half] = prod[:half, sw:] + prod[half:, :sw]

            @pl.when(c > 0)
            def _():
                rcopy(ps.at[b, s], pr.at[b, s], p_send.at[b, s], p_recv.at[b, s], sib).wait_recv()
                ps[b, s] = fin[...] + pr[b, s]

            @pl.when(c == 0)
            def _():
                ps[b, s] = fin[...]

            @pl.when(t > c)
            def _():
                p_up(b, s).start()

        @pl.when(u == final_at)
        def _():
            finish()

        return carry

    lax.fori_loop(0, total, unit, 0)
    cores_ref[:, 0] = ks[0]

    def gather(k):
        o = (c + k) % n_cols
        rcopy(ks.at[k], kr.at[o], k_send.at[k], k_recv.at[o], sib).wait_recv()
        cores_ref[:, 0] = cores_ref[:, 0] + kr[o]

    each(1, n_cols, gather)

    @pl.when(q >= c)
    def _():
        for s in range(nsub):
            u_side(s).wait_send()

        def left(d):
            for s in range(nsub):
                u_out(d, s).wait_send()

        each(1, chips, left)

    def rest(d):
        t = ahead(d)

        @pl.when(jnp.logical_and(t >= c, d > 0))
        def _():
            for s in range(nsub):
                u_forward(t, s, t * 2 + h).wait_send()

        @pl.when(t > c)
        def _():
            for s in range(nsub):
                for e in range(2):
                    p_up(t * 2 + e, s).wait_send()

        @pl.when(d > 0)
        def _():
            lg_out(d).wait_send()
            lg_forward(d).wait_send()

    each(0, chips, rest)
    lg_side().wait_send()

    def tail(k):
        lz_out(k).wait_send()
        k_out(k).wait_send()
        e_out(k).wait_send()

    each(1, n_cols, tail)


def paired_kernel(
    n_rows, n_cols,
    row_ref, u_ref, up_ref, col_ref, piv_ref, rank_ref,
    panel_ref, cores_ref,
    xh, xl, x0, ch, cl, us, ps, pr, lz, lg, ks, ku, kd, eb,
    u_loc, nat_x, nat_y, nat_fwd, full1, half1,
    lift, full0, half0, lift_x, lift_y, lift_fx, lift_fy,
    side_send, side_recv, x_send, x_recv, p_send, p_recv,
    lz_loc, lz_send, lz_recv, lg_loc, lg_send, lg_sib, lg_fwd, lg_recv,
    ku_send, ku_recv, kd_send, kd_recv, e_send, e_recv,
):
    r, c = lax.axis_index("row"), lax.axis_index("col")
    chips = n_rows // 2
    nx = math.isqrt(chips)
    q, h = r // 2, r % 2
    qy, qx = q // nx, q % nx
    xn, yn, dn = qy * nx + 1 - qx, (1 - qy) * nx + qx, (1 - qy) * nx + 1 - qx
    tiles, _, ranks, wc = row_ref.shape
    nsub, sw = us.shape[1], us.shape[5]
    wq = lz.shape[1]
    sib = (q * 2 + 1 - h, c)
    to_x, to_y = (xn * 2 + h, c), (yn * 2 + h, c)
    stages = nsub * (n_cols - 1)
    early = nsub * (n_cols - 2)

    def ahead(d):
        return ((qy + d // nx) % nx) * nx + (qx + d % nx) % nx

    def rcopy(src, dst, ssem, rsem, dev):
        return pltpu.make_async_remote_copy(
            src_ref=src, dst_ref=dst, send_sem=ssem, recv_sem=rsem, device_id=dev, device_id_type=MESH
        )

    def each(first, last, body):
        lax.fori_loop(first, last, lambda i, z: (body(i), z)[1], 0)

    def ts(i):
        return jnp.where(c == 0, 0, n_cols - 1 - i // nsub), i % nsub

    def active(i):
        t, _ = ts(i)
        return jnp.logical_and(i < stages, jnp.where(c == 0, i < nsub, t >= c))

    def ucols(s):
        return u_ref.at[:, :, pl.ds(pl.multiple_of(s * sw, sw), sw)]

    def local_u(s):
        return pltpu.make_async_copy(ucols(s), us.at[r, s, 1], u_loc.at[s])

    def nat_out(s, dev, sem):
        return rcopy(ucols(s), us.at[r, s, 1], sem.at[s], full1.at[q, s], dev)

    def nat_full(t, s):
        b = 2 * t + h
        return rcopy(us.at[b, s, 1], us.at[b, s, 1], nat_fwd.at[t, s], full1.at[t, s], sib)

    def nat_half(t, s, k, dev):
        b = 2 * t + h
        part = us.at[b, s, 1, :, k * (wc // 2):(k + 1) * (wc // 2), :]
        return rcopy(part, part, nat_fwd.at[t, s], half1.at[t, s, k], dev)

    def piece(b, s, g):
        return us.at[b, s, 0, :, pl.ds(pl.multiple_of(g * wq, wq), wq), :]

    def lift_out(s, g):
        rows = pl.ds(pl.multiple_of(g * wq, wq), wq)
        src = u_ref.at[:, rows, pl.ds(pl.multiple_of(s * sw, sw), sw)]
        return rcopy(src, piece(r, s, g), lift.at[s, g], full0.at[q, s, g], (g * 2 + h, 1))

    def lift_full(t, s, g, sem, dev):
        p = piece(2 * t + h, s, g)
        return rcopy(p, p, sem.at[t, s], full0.at[t, s, g], dev)

    def lift_half(t, s, g, k, sem, dev):
        rows = pl.ds(pl.multiple_of(g * wq + k * (wq // 2), wq // 2), wq // 2)
        p = us.at[2 * t + h, s, 0, :, rows, :]
        return rcopy(p, p, sem.at[t, s], half0.at[t, s, k], dev)

    def side(t, s, kk, b):
        return rcopy(us.at[b, s, kk], us.at[b, s, kk], side_send.at[t, s, kk], side_recv.at[t, s, kk], sib)

    def x_up(m):
        return rcopy(row_ref.at[m], x0.at[m], x_send.at[m], x_recv.at[m], (r, c + 1))

    def p_up(b, s, m):
        return rcopy(ps.at[b, s, m], pr.at[b, s, m], p_send.at[b, s, m], p_recv.at[b, s, m], (r, c + 1))

    def lz_out(k):
        to = (c + k) % n_cols
        start = pl.multiple_of(to * wc + q * wq, wq)
        return rcopy(up_ref.at[0, h, pl.ds(start, wq), :], lz.at[c], lz_send.at[k], lz_recv.at[c], (r, to))

    def lg_out(d):
        return rcopy(lz, lg.at[h, q], lg_send.at[d], lg_recv.at[h, q], (ahead(d) * 2 + h, c))

    def lg_side():
        return rcopy(lz, lg.at[h, q], lg_sib.at[0], lg_recv.at[h, q], sib)

    def lg_forward(d):
        b = ahead(d)
        return rcopy(lg.at[h, b], lg.at[h, b], lg_fwd.at[d], lg_recv.at[h, b], sib)

    def k_up(j, m):
        return rcopy(ks.at[j, m], ku.at[j, m], ku_send.at[j, m], ku_recv.at[j, m], (r, c + 1))

    def k_down(j, m):
        return rcopy(ks.at[j, m], kd.at[c, m], kd_send.at[j, m], kd_recv.at[c, m], (r, j))

    def e_out(k):
        return rcopy(eb.at[c], eb.at[c], e_send.at[k], e_recv.at[c], (r, (c + k) % n_cols))

    mine = pl.multiple_of(c * wc + q * wq, wq)
    lz_own = pltpu.make_async_copy(up_ref.at[0, h, pl.ds(mine, wq), :], lz.at[c], lz_loc.at[0])
    lz_own.start()
    barrier = pltpu.get_barrier_semaphore()

    def signal(dev):
        pl.semaphore_signal(barrier, inc=1, device_id=dev, device_id_type=MESH)

    signal(sib)
    each(1, chips, lambda d: signal((ahead(d) * 2 + h, c)))
    each(1, n_cols, lambda k: signal((r, (c + k) % n_cols)))

    @pl.when(c < 2)
    def _():
        each(1, chips, lambda d: signal((ahead(d) * 2 + h, 1 - c)))

    pl.semaphore_wait(barrier, 1 + (chips - 1) + (n_cols - 1) + jnp.where(c < 2, chips - 1, 0))

    def native_out(i):
        t, s = ts(i)

        @pl.when(jnp.logical_and(active(i), q == t))
        def _():
            nat_out(s, to_x, nat_x).start()
            nat_out(s, to_y, nat_y).start()
            local_u(s).start()

    def lift_in(i):
        t, s = ts(i)

        @pl.when(jnp.logical_and(active(i), c == 1))
        def _():
            lift_full(t, s, q, lift_x, sib).wait_recv()
            lift_full(t, s, q, lift_x, to_x).start()
            lift_full(t, s, q, lift_y, to_y).start()

    def relay(i):
        t, s = ts(i)

        @pl.when(active(i))
        def _():
            @pl.when(xn == t)
            def _():
                nat_full(t, s).wait_recv()
                nat_half(t, s, 0, to_y).start()

            @pl.when(yn == t)
            def _():
                nat_full(t, s).wait_recv()
                nat_half(t, s, 1, to_x).start()

            @pl.when(c == 1)
            def _():
                lift_full(t, s, xn, lift_x, sib).wait_recv()
                lift_half(t, s, xn, 0, lift_fy, to_y).start()
                lift_full(t, s, yn, lift_x, sib).wait_recv()
                lift_half(t, s, yn, 1, lift_fx, to_x).start()

    def collect(i):
        t, s = ts(i)

        @pl.when(active(i))
        def _():
            @pl.when(dn == t)
            def _():
                nat_half(t, s, 0, sib).wait_recv()
                nat_half(t, s, 1, sib).wait_recv()

            @pl.when(q == t)
            def _():
                local_u(s).wait()

            side(t, s, 1, 2 * t + h).start()

            @pl.when(c == 1)
            def _():
                lift_half(t, s, dn, 0, lift_fy, sib).wait_recv()
                lift_half(t, s, dn, 1, lift_fx, sib).wait_recv()
                side(t, s, 0, 2 * t + h).start()

    def pump(i):
        @pl.when(i >= early)
        def _():
            lift_in(i)

        relay(i)
        native_out(i + 2)

        @pl.when(i + 1 < early)
        def _():
            lift_in(i + 1)

        collect(i)

    def lifts():
        for s in range(nsub):
            each(0, chips, lambda g: lift_out(s, g).start())

    @pl.when(jnp.logical_and(c == 0, q == chips - 1))
    def _():
        lifts()

    @pl.when(c == 0)
    def _():
        x_up(0).start()

    native_out(0)
    native_out(1)
    each(1, n_cols, lambda k: lz_out(k).start())

    @pl.when(c == 0)
    def _():
        for m in range(1, tiles):
            x_up(m).start()

    for m in range(tiles):
        for p in range(2):
            a, b = split(row_ref[m, p])
            xh[1, m, p * ranks:(p + 1) * ranks, :] = a
            xl[1, m, p * ranks:(p + 1) * ranks, :] = b

    pos = c * wc + lax.broadcasted_iota(jnp.int32, (wc, ranks), 0)
    parts = []
    for i in range(tiles):
        hit = pos == piv_ref[i:i + 1, :]
        for p in range(2):
            parts.append(jnp.sum(jnp.where(hit, col_ref[i, p], 0.0), axis=0, keepdims=True))
    parts.append(jnp.zeros((eb.shape[1] - 2 * tiles, ranks), jnp.float32))
    eb[c] = jnp.concatenate(parts, axis=0)
    each(1, n_cols, lambda k: e_out(k).start())

    def spread():
        lz_own.wait()
        each(1, n_cols, lambda k: rcopy(
            lz.at[(c + k) % n_cols], lz.at[(c + k) % n_cols], lz_send.at[k], lz_recv.at[(c + k) % n_cols], sib
        ).wait_recv())
        lg_side().start()
        pltpu.make_async_copy(lz, lg.at[h, q], lg_loc.at[0]).start()
        each(1, chips, lambda d: lg_out(d).start())

    lift_in(0)

    @pl.when(c == 1)
    def _():
        pump(0)

    @pl.when(c != 1)
    def _():
        each(0, early, pump)

    @pl.when(c == 0)
    def _():
        for m in range(tiles):
            x_up(m).wait_send()

            @pl.when(q == chips - 2 - m)
            def _():
                lifts()

        @pl.when(jnp.logical_and(q > 0, q < chips - 1 - tiles))
        def _():
            lifts()

    @pl.when(c != 1)
    def _():
        spread()

    def gather():
        def pass_on(d):
            o = ahead(d)
            rcopy(lz, lg.at[h, o], lg_send.at[d], lg_recv.at[h, o], sib).wait_recv()
            lg_forward(d).start()

        each(1, chips, pass_on)
        each(1, n_cols, lambda k: rcopy(
            eb.at[(c + k) % n_cols], eb.at[(c + k) % n_cols], e_send.at[k], e_recv.at[(c + k) % n_cols], sib
        ).wait_recv())
        pltpu.make_async_copy(lz, lg.at[h, q], lg_loc.at[0]).wait()
        each(0, chips, lambda o: rcopy(
            lz, lg.at[1 - h, o], lg_sib.at[0], lg_recv.at[1 - h, o], sib
        ).wait_recv())

    def finish(m):
        @pl.when(m == 0)
        def _():
            gather()

        entries = jnp.sum(eb[...], axis=0)
        lines = []
        levels = lax.broadcasted_iota(jnp.int32, (1, ranks), 1)
        for i in range(tiles):
            er, ei = entries[2 * i:2 * i + 1], entries[2 * i + 1:2 * i + 2]
            keep = (levels < RANK_STEP * rank_ref[i]).astype(jnp.float32)
            mag = jnp.maximum(er * er + ei * ei, 1.0)
            lines.append(keep * er / mag)
            lines.append(-keep * ei / mag)
        factor_r, factor_i = lines[0], lines[1]
        for i in range(1, tiles):
            factor_r = jnp.where(m == i, lines[2 * i], factor_r)
            factor_i = jnp.where(m == i, lines[2 * i + 1], factor_i)
        pad = jnp.zeros((126, ranks), jnp.float32)
        turned = jnp.concatenate([factor_r, factor_i, pad], axis=0).T
        fr, fi = turned[:, 0:1], turned[:, 1:2]
        vr, vi = [], []
        for hh in range(2):
            for s in range(nsub):
                vr.append(ps[2 * c + hh, s, m, 0])
                vi.append(ps[2 * c + hh, s, m, 1])
        vr, vi = jnp.concatenate(vr, axis=1), jnp.concatenate(vi, axis=1)
        wr = vr * fr - vi * fi
        wi = vr * fi + vi * fr
        panel_ref[m, 0] = wr
        panel_ref[m, 1] = wi
        a, b = split(wr)
        ch[0:ranks, :] = a
        cl[0:ranks, :] = b
        a, b = split(wi)
        ch[ranks:2 * ranks, :] = a
        cl[ranks:2 * ranks, :] = b

        def core(j, carry):
            rank2 = lz.shape[2]
            lr = lg[0, :, j].reshape(wc, rank2)
            li = lg[1, :, j].reshape(wc, rank2)
            uh, ul = split(jnp.concatenate([lr, li], axis=1))
            prod = dot3(ch[...], cl[...], uh, ul)
            ks[j, m, 0] = prod[:ranks, :rank2] - prod[ranks:, rank2:]
            ks[j, m, 1] = prod[:ranks, rank2:] + prod[ranks:, :rank2]

            @pl.when(j < c)
            def _():
                k_down(j, m).start()

            @pl.when(jnp.logical_and(c == 0, j > 0))
            def _():
                k_up(j, m).start()

            return carry

        lax.fori_loop(0, n_cols, core, 0)

    head = early * tiles
    tail = stages - early
    total = head + tail * tiles
    first_final = jnp.where(c == 0, nsub, (n_cols - c) * nsub)
    final0 = jnp.where(c == 1, head + tail - 1, first_final - 1)
    final1 = jnp.where(c == 1, tail, early)

    def unit(u, carry):
        i = jnp.where(u < head, u % early, early + (u - head) % tail)
        m = jnp.where(u < head, u // early, (u - head) // tail)
        t, s = ts(i)

        @pl.when(active(i))
        def _():
            @pl.when(jnp.logical_and(c == 1, jnp.logical_and(u < head, u % early == 0)))
            def _():
                x_up(m).wait_recv()
                for p in range(2):
                    a, b = split(x0[m, p])
                    xh[0, m, p * ranks:(p + 1) * ranks, :] = a
                    xl[0, m, p * ranks:(p + 1) * ranks, :] = b

            for e in range(2):
                b = 2 * t + (h + e) % 2

                if e == 1:
                    @pl.when(m == 0)
                    def _():
                        side(t, s, 1, b).wait_recv()

                        @pl.when(c == 1)
                        def _():
                            side(t, s, 0, b).wait_recv()

                def product(kk):
                    uh, ul = split(jnp.concatenate([us[b, s, kk, 0], us[b, s, kk, 1]], axis=1))
                    prod = dot3(xh[kk, m], xl[kk, m], uh, ul)
                    real = prod[:ranks, :sw] - prod[ranks:, sw:]
                    imag = prod[:ranks, sw:] + prod[ranks:, :sw]
                    return real, imag

                real, imag = product(1)

                @pl.when(c == 1)
                def _():
                    real0, imag0 = product(0)
                    ps[b, s, m, 0] = real + real0
                    ps[b, s, m, 1] = imag + imag0

                @pl.when(c == 0)
                def _():
                    ps[b, s, m, 0] = real
                    ps[b, s, m, 1] = imag

                @pl.when(c > 1)
                def _():
                    p_up(b, s, m).wait_recv()
                    ps[b, s, m, 0] = real + pr[b, s, m, 0]
                    ps[b, s, m, 1] = imag + pr[b, s, m, 1]

                @pl.when(t > c)
                def _():
                    p_up(b, s, m).start()

        @pl.when(jnp.logical_or(u == final0, u == final0 + final1))
        def _():
            finish(m)

        @pl.when(c == 1)
        def _():
            @pl.when(u + 1 < early)
            def _():
                pump(u + 1)

            @pl.when(u == early - 1)
            def _():
                spread()

            @pl.when(jnp.logical_and(u >= early + 1, u < early + 1 + tail))
            def _():
                pump(u - 1)

        return carry

    lax.fori_loop(0, total, unit, 0)

    @pl.when(c > 0)
    def _():
        for m in range(tiles):
            def lower(j):
                k_up(j, m).wait_recv()
                ks[j, m] = ks[j, m] + ku[j, m]

                @pl.when(j > c)
                def _():
                    k_up(j, m).start()

            each(c, n_cols, lower)

    for m in range(tiles):
        cores_ref[m, 0] = ks[c, m]

        def upper(o):
            rcopy(ks.at[c, m], kd.at[o, m], kd_send.at[c, m], kd_recv.at[o, m], sib).wait_recv()
            cores_ref[m, 0] = cores_ref[m, 0] + kd[o, m]

        each(c + 1, n_cols, upper)

    @pl.when(jnp.logical_and(c == 0, q > 0))
    def _():
        for s in range(nsub):
            each(0, chips, lambda g: lift_out(s, g).wait_send())

    def drain(i):
        t, s = ts(i)

        @pl.when(active(i))
        def _():
            @pl.when(q == t)
            def _():
                nat_out(s, to_x, nat_x).wait_send()
                nat_out(s, to_y, nat_y).wait_send()

            @pl.when(jnp.logical_or(xn == t, yn == t))
            def _():
                nat_half(t, s, 0, sib).wait_send()

            side(t, s, 1, 2 * t + h).wait_send()

            @pl.when(c == 1)
            def _():
                lift_full(t, s, q, lift_x, sib).wait_send()
                lift_full(t, s, q, lift_y, sib).wait_send()
                lift_half(t, s, xn, 0, lift_fy, sib).wait_send()
                lift_half(t, s, yn, 1, lift_fx, sib).wait_send()
                side(t, s, 0, 2 * t + h).wait_send()

            @pl.when(t > c)
            def _():
                for m in range(tiles):
                    for e in range(2):
                        p_up(2 * t + e, s, m).wait_send()

    each(0, stages, drain)

    def tail_l(d):
        lg_out(d).wait_send()
        lg_forward(d).wait_send()

    each(1, chips, tail_l)
    lg_side().wait_send()

    def tail_z(k):
        lz_out(k).wait_send()
        e_out(k).wait_send()

    each(1, n_cols, tail_z)
    for m in range(tiles):
        each(0, c, lambda j: k_down(j, m).wait_send())
        each(c + 1, n_cols, lambda j: k_up(j, m).wait_send())


def paired(n_rows, n_cols, col_samples, row_samples, pivot_rows, rank_blocks, upper_inverse, upanel_left):
    tiles, _, ranks, wc = row_samples.shape
    wr = upper_inverse.shape[2]
    left_ranks = upanel_left.shape[3]
    chips = n_rows // 2
    nsub = wr // 128
    sw = wr // nsub
    wq = wc // chips
    f32, bf16 = jnp.float32, jnp.bfloat16
    dma = pltpu.SemaphoreType.DMA
    vmem = pl.BlockSpec(memory_space=pltpu.VMEM)
    hbm = pl.BlockSpec(memory_space=pl.ANY)
    sums = pltpu.VMEM((n_rows, nsub, tiles, 2, ranks, sw), f32)
    return pl.pallas_call(
        functools.partial(paired_kernel, n_rows, n_cols),
        out_shape=(
            jax.ShapeDtypeStruct((tiles, 2, ranks, wc), f32),
            jax.ShapeDtypeStruct((tiles, 1, 2, ranks, left_ranks), f32),
        ),
        in_specs=[vmem, hbm, hbm, vmem, vmem, pl.BlockSpec(memory_space=pltpu.SMEM)],
        out_specs=(vmem, vmem),
        scratch_shapes=[
            pltpu.VMEM((2, tiles, 2 * ranks, wc), bf16),
            pltpu.VMEM((2, tiles, 2 * ranks, wc), bf16),
            pltpu.VMEM((tiles, 2, ranks, wc), f32),
            pltpu.VMEM((2 * ranks, wc), bf16),
            pltpu.VMEM((2 * ranks, wc), bf16),
            pltpu.VMEM((n_rows, nsub, 2, 2, wc, sw), f32),
            sums,
            sums,
            pltpu.VMEM((n_cols, wq, left_ranks), f32),
            pltpu.VMEM((2, chips, n_cols, wq, left_ranks), f32),
            pltpu.VMEM((n_cols, tiles, 2, ranks, left_ranks), f32),
            pltpu.VMEM((n_cols, tiles, 2, ranks, left_ranks), f32),
            pltpu.VMEM((n_cols, tiles, 2, ranks, left_ranks), f32),
            pltpu.VMEM((n_cols, -(-2 * tiles // 8) * 8, ranks), f32),
            dma((nsub,)), dma((nsub,)), dma((nsub,)), dma((n_cols, nsub)), dma((n_cols, nsub)),
            dma((n_cols, nsub, 2)),
            dma((nsub, chips)), dma((n_cols, nsub, chips)), dma((n_cols, nsub, 2)),
            dma((n_cols, nsub)), dma((n_cols, nsub)), dma((n_cols, nsub)), dma((n_cols, nsub)),
            dma((n_cols, nsub, 2)), dma((n_cols, nsub, 2)), dma((tiles,)), dma((tiles,)),
            dma((n_rows, nsub, tiles)), dma((n_rows, nsub, tiles)),
            dma((1,)), dma((n_cols,)), dma((n_cols,)), dma((1,)), dma((chips,)), dma((1,)), dma((chips,)),
            dma((2, chips)),
            dma((n_cols, tiles)), dma((n_cols, tiles)), dma((n_cols, tiles)), dma((n_cols, tiles)),
            dma((n_cols,)), dma((n_cols,)),
        ],
        compiler_params=pltpu.CompilerParams(
            collective_id=0, has_side_effects=True, vmem_limit_bytes=56 * 1024 * 1024
        ),
    )(row_samples, upper_inverse, upanel_left, col_samples, pivot_rows, rank_blocks)


def on_device(n_rows, n_cols, col_samples, row_samples, pivot_rows, rank_blocks, upper_inverse, upanel_left):
    tiles, _, ranks, wc = row_samples.shape
    wr = upper_inverse.shape[2]
    left_ranks = upanel_left.shape[3]
    chips = n_rows // 2
    if chips != n_cols or wc != 2 * wr:
        raise ValueError("unsupported mesh")
    if chips == 4 and wr % 128 == 0:
        return paired(
            n_rows, n_cols, col_samples, row_samples, pivot_rows, rank_blocks, upper_inverse, upanel_left
        )
    nsub = max(wr // 128, 1)
    sw = wr // nsub
    wq = wc // chips
    m = 2 * tiles * ranks
    f32, bf16 = jnp.float32, jnp.bfloat16
    dma = pltpu.SemaphoreType.DMA
    vmem = pl.BlockSpec(memory_space=pltpu.VMEM)
    hbm = pl.BlockSpec(memory_space=pl.ANY)
    return pl.pallas_call(
        functools.partial(kernel, n_rows, n_cols),
        out_shape=(
            jax.ShapeDtypeStruct((tiles, 2, ranks, wc), f32),
            jax.ShapeDtypeStruct((tiles, 1, 2, ranks, left_ranks), f32),
        ),
        in_specs=[vmem, hbm, hbm, vmem, vmem, pl.BlockSpec(memory_space=pltpu.SMEM)],
        out_specs=(vmem, vmem),
        scratch_shapes=[
            pltpu.VMEM((m, wc), bf16),
            pltpu.VMEM((m, wc), bf16),
            pltpu.VMEM((m, wc), bf16),
            pltpu.VMEM((m, wc), bf16),
            pltpu.VMEM((n_rows, nsub, 2, wc, sw), f32),
            pltpu.VMEM((n_rows, nsub, m, sw), f32),
            pltpu.VMEM((n_rows, nsub, m, sw), f32),
            pltpu.VMEM((m, sw), f32),
            pltpu.VMEM((n_cols, wq, left_ranks), f32),
            pltpu.VMEM((2, chips, n_cols, wq, left_ranks), f32),
            pltpu.VMEM((n_cols, tiles, 2, ranks, left_ranks), f32),
            pltpu.VMEM((n_cols, tiles, 2, ranks, left_ranks), f32),
            pltpu.VMEM((n_cols, -(-2 * tiles // 8) * 8, ranks), f32),
            dma((nsub,)), dma((chips, nsub)), dma((nsub,)), dma((chips, nsub)), dma((n_rows, nsub)),
            dma((n_rows, nsub)), dma((n_rows, nsub)),
            dma((1,)), dma((n_cols,)), dma((n_cols,)), dma((1,)), dma((chips,)), dma((1,)), dma((chips,)),
            dma((2, chips)),
            dma((n_cols,)), dma((n_cols,)), dma((n_cols,)), dma((n_cols,)),
        ],
        compiler_params=pltpu.CompilerParams(
            collective_id=0, has_side_effects=True, vmem_limit_bytes=56 * 1024 * 1024
        ),
    )(row_samples, upper_inverse, upanel_left, col_samples, pivot_rows, rank_blocks)


def solution(mesh):
    in_specs = (
        P("row", None, "col", None),
        P("row", None, None, "col"),
        P("row", None),
        P("row"),
        P(None, "col", "row"),
        P("col", None, None, None),
    )
    out_specs = (P("row", None, None, "col"), P("row", "col", None, None, None))
    body = functools.partial(on_device, mesh.shape["row"], mesh.shape["col"])
    return jax.shard_map(body, mesh=mesh, in_specs=in_specs, out_specs=out_specs, check_vma=False)
```

```python
import functools
import math

import jax
import jax.numpy as jnp
from jax import lax
from jax.experimental import pallas as pl
from jax.experimental.pallas import tpu as pltpu
from jax.sharding import PartitionSpec as P

RANK_STEP = 16
MESH = pl.DeviceIdType.MESH


def split(x):
    high = x.astype(jnp.bfloat16)
    low = (x - high.astype(jnp.float32)).astype(jnp.bfloat16)
    return high, low


def dot3(xh, xl, uh, ul):
    def single(a, b):
        return jnp.dot(a, b, preferred_element_type=jnp.float32)

    return single(xh, uh) + (single(xh, ul) + single(xl, uh))


def kernel(
    n_rows, n_cols,
    row_ref, u_ref, up_ref, col_ref, piv_ref, rank_ref,
    panel_ref, cores_ref,
    xh, xl, ch, cl, us, ps, pr, fin, lz, lg, ks, kr, eb,
    u_loc, u_send, u_sib, u_fwd, u_recv,
    p_send, p_recv,
    lz_loc, lz_send, lz_recv, lg_loc, lg_send, lg_sib, lg_fwd, lg_recv,
    k_send, k_recv, e_send, e_recv,
):
    r, c = lax.axis_index("row"), lax.axis_index("col")
    chips = n_rows // 2
    nx = math.isqrt(chips)
    ny = chips // nx
    q, h = r // 2, r % 2
    qy, qx = q // nx, q % nx
    tiles, _, ranks, wc = row_ref.shape
    nsub, sw = us.shape[1], us.shape[4]
    wq = lz.shape[1]
    half = tiles * ranks
    sib = (q * 2 + 1 - h, c)

    def ahead(d):
        return ((qy + d // nx) % ny) * nx + (qx + d % nx) % nx

    def behind(d):
        return ((qy + ny - d // nx) % ny) * nx + (qx + nx - d % nx) % nx

    def rcopy(src, dst, ssem, rsem, dev):
        return pltpu.make_async_remote_copy(
            src_ref=src, dst_ref=dst, send_sem=ssem, recv_sem=rsem, device_id=dev, device_id_type=MESH
        )

    def u_out(d, s):
        return rcopy(
            u_ref.at[:, :, s * sw:(s + 1) * sw], us.at[r, s], u_send.at[d, s], u_recv.at[r, s],
            (behind(d) * 2 + h, c),
        )

    def u_side(s):
        return rcopy(u_ref.at[:, :, s * sw:(s + 1) * sw], us.at[r, s], u_sib.at[s], u_recv.at[r, s], sib)

    def u_forward(t, s, b):
        return rcopy(us.at[b, s], us.at[b, s], u_fwd.at[t, s], u_recv.at[b, s], sib)

    def p_up(b, s):
        return rcopy(ps.at[b, s], pr.at[b, s], p_send.at[b, s], p_recv.at[b, s], (r, c + 1))

    def lz_out(k):
        to = (c + k) % n_cols
        start = pl.multiple_of(to * wc + q * wq, wq)
        return rcopy(up_ref.at[0, h, pl.ds(start, wq), :], lz.at[c], lz_send.at[k], lz_recv.at[c], (r, to))

    def lg_out(d):
        return rcopy(lz, lg.at[h, q], lg_send.at[d], lg_recv.at[h, q], (behind(d) * 2 + h, c))

    def lg_side():
        return rcopy(lz, lg.at[h, q], lg_sib.at[0], lg_recv.at[h, q], sib)

    def lg_forward(d):
        b = ahead(d)
        return rcopy(lg.at[h, b], lg.at[h, b], lg_fwd.at[d], lg_recv.at[h, b], sib)

    def k_out(k):
        to = (c + k) % n_cols
        return rcopy(ks.at[k], kr.at[c], k_send.at[k], k_recv.at[c], (r, to))

    def e_out(k):
        return rcopy(eb.at[c], eb.at[c], e_send.at[k], e_recv.at[c], (r, (c + k) % n_cols))

    def each(first, last, body):
        lax.fori_loop(first, last, lambda i, z: (body(i), z)[1], 0)

    own = [
        pltpu.make_async_copy(u_ref.at[:, :, s * sw:(s + 1) * sw], us.at[r, s], u_loc.at[s]) for s in range(nsub)
    ]
    for copy in own:
        copy.start()
    mine = pl.multiple_of(c * wc + q * wq, wq)
    lz_own = pltpu.make_async_copy(up_ref.at[0, h, pl.ds(mine, wq), :], lz.at[c], lz_loc.at[0])
    lz_own.start()
    barrier = pltpu.get_barrier_semaphore()

    def signal(dev):
        pl.semaphore_signal(barrier, inc=1, device_id=dev, device_id_type=MESH)

    signal(sib)
    each(1, chips, lambda d: signal((behind(d) * 2 + h, c)))
    each(1, n_cols, lambda k: signal((r, (c + k) % n_cols)))
    pl.semaphore_wait(barrier, 1 + (chips - 1) + (n_cols - 1))

    @pl.when(q >= c)
    def _():
        for s in range(nsub):
            u_side(s).start()

        @pl.when(q > 0)
        def _():
            for s in range(nsub):
                each(1, chips, lambda d: u_out(d, s).start())

    each(1, n_cols, lambda k: lz_out(k).start())

    for i in range(tiles):
        for p in range(2):
            a, b = split(row_ref[i, p])
            at = pl.ds(p * half + i * ranks, ranks)
            xh[at, :] = a
            xl[at, :] = b

    pos = c * wc + lax.broadcasted_iota(jnp.int32, (wc, ranks), 0)
    parts = []
    for i in range(tiles):
        hit = pos == piv_ref[i:i + 1, :]
        for p in range(2):
            parts.append(jnp.sum(jnp.where(hit, col_ref[i, p], 0.0), axis=0, keepdims=True))
    parts.append(jnp.zeros((eb.shape[1] - 2 * tiles, ranks), jnp.float32))
    eb[c] = jnp.concatenate(parts, axis=0)
    each(1, n_cols, lambda k: e_out(k).start())
    for copy in own:
        copy.wait()

    near = chips * (nsub - 1)
    total = 2 * (near + chips + nsub - 1)
    spread_at = jnp.where(c == 0, 2, 0)
    final_at = jnp.where(c == 0, total - 1, 2 * (near + chips - 1 - c) + 1)

    def finish():
        def pass_on(d2):
            o = ahead(d2)
            rcopy(lz, lg.at[h, o], lg_send.at[d2], lg_recv.at[h, o], sib).wait_recv()
            lg_forward(d2).start()

        each(1, chips, pass_on)

        each(1, n_cols, lambda k: rcopy(
            eb.at[(c + k) % n_cols], eb.at[(c + k) % n_cols], e_send.at[k], e_recv.at[(c + k) % n_cols], sib
        ).wait_recv())
        entries = jnp.sum(eb[...], axis=0)
        lines = []
        levels = lax.broadcasted_iota(jnp.int32, (1, ranks), 1)
        for i in range(tiles):
            er, ei = entries[2 * i:2 * i + 1], entries[2 * i + 1:2 * i + 2]
            keep = (levels < RANK_STEP * rank_ref[i]).astype(jnp.float32)
            mag = jnp.maximum(er * er + ei * ei, 1.0)
            lines.append(keep * er / mag)
            lines.append(-keep * ei / mag)
        lines.append(jnp.zeros((128 - 2 * tiles, ranks), jnp.float32))
        turned = jnp.concatenate(lines, axis=0).T
        for i in range(tiles):
            fr, fi = turned[:, 2 * i:2 * i + 1], turned[:, 2 * i + 1:2 * i + 2]
            lr, li = i * ranks, half + i * ranks
            vr, vi = [], []
            for hh in range(2):
                for s in range(nsub):
                    vr.append(ps[2 * c + hh, s, lr:lr + ranks, :])
                    vi.append(ps[2 * c + hh, s, li:li + ranks, :])
            vr, vi = jnp.concatenate(vr, axis=1), jnp.concatenate(vi, axis=1)
            wr = vr * fr - vi * fi
            wi = vr * fi + vi * fr
            panel_ref[i, 0] = wr
            panel_ref[i, 1] = wi
            a, b = split(wr)
            ch[lr:lr + ranks, :] = a
            cl[lr:lr + ranks, :] = b
            a, b = split(wi)
            ch[li:li + ranks, :] = a
            cl[li:li + ranks, :] = b

        pltpu.make_async_copy(lz, lg.at[h, q], lg_loc.at[0]).wait()
        each(0, chips, lambda o: rcopy(
            lz, lg.at[1 - h, o], lg_sib.at[0], lg_recv.at[1 - h, o], sib
        ).wait_recv())

        def core(k0, carry):
            k = jnp.where(c == 0, n_cols - 1 - k0, (k0 + 1) % n_cols)
            j = (c + k) % n_cols
            lr = lg[0, :, j].reshape(wc, lz.shape[2])
            li = lg[1, :, j].reshape(wc, lz.shape[2])
            rank2 = lz.shape[2]
            uh, ul = split(jnp.concatenate([lr, li], axis=1))
            prod = dot3(ch[...], cl[...], uh, ul)
            real = prod[:half, :rank2] - prod[half:, rank2:]
            imag = prod[:half, rank2:] + prod[half:, :rank2]
            for i in range(tiles):
                ks[k, i, 0] = real[i * ranks:(i + 1) * ranks]
                ks[k, i, 1] = imag[i * ranks:(i + 1) * ranks]

            @pl.when(k > 0)
            def _():
                k_out(k).start()

            return carry

        lax.fori_loop(0, n_cols, core, 0)

    def unit(u, carry):
        slot = u // 2
        t = jnp.where(slot < near, ahead(slot % chips), jnp.maximum(near + chips - 1 - slot, 0))
        s = jnp.where(slot < near, slot // chips, jnp.where(slot < near + chips, nsub - 1, slot - near - chips))
        live = jnp.logical_and(t >= c, jnp.logical_or(slot >= near, t > 0))
        e = u % 2
        b = t * 2 + (h + e) % 2

        @pl.when(u == spread_at)
        def _():
            lz_own.wait()
            each(1, n_cols, lambda k: rcopy(
                lz.at[(c + k) % n_cols], lz.at[(c + k) % n_cols], lz_send.at[k], lz_recv.at[(c + k) % n_cols], sib
            ).wait_recv())
            lg_side().start()
            pltpu.make_async_copy(lz, lg.at[h, q], lg_loc.at[0]).start()
            each(1, chips, lambda d2: lg_out(d2).start())

            @pl.when(jnp.logical_and(q == 0, q >= c))
            def _():
                for s2 in range(nsub):
                    each(1, chips, lambda d2: u_out(d2, s2).start())

        @pl.when(live)
        def _():
            @pl.when(jnp.logical_or(t != q, e > 0))
            def _():
                u_forward(t, s, b).wait_recv()

            @pl.when(jnp.logical_and(t != q, e == 0))
            def _():
                u_forward(t, s, b).start()

            ur, ui = us[b, s, 0], us[b, s, 1]
            uh, ul = split(jnp.concatenate([ur, ui], axis=1))
            prod = dot3(xh[...], xl[...], uh, ul)
            fin[0:half] = prod[:half, :sw] - prod[half:, sw:]
            fin[half:2 * half] = prod[:half, sw:] + prod[half:, :sw]

            @pl.when(c > 0)
            def _():
                rcopy(ps.at[b, s], pr.at[b, s], p_send.at[b, s], p_recv.at[b, s], sib).wait_recv()
                ps[b, s] = fin[...] + pr[b, s]

            @pl.when(c == 0)
            def _():
                ps[b, s] = fin[...]

            @pl.when(t > c)
            def _():
                p_up(b, s).start()

        @pl.when(u == final_at)
        def _():
            finish()

        return carry

    lax.fori_loop(0, total, unit, 0)
    cores_ref[:, 0] = ks[0]

    def gather(k):
        o = (c + k) % n_cols
        rcopy(ks.at[k], kr.at[o], k_send.at[k], k_recv.at[o], sib).wait_recv()
        cores_ref[:, 0] = cores_ref[:, 0] + kr[o]

    each(1, n_cols, gather)

    @pl.when(q >= c)
    def _():
        for s in range(nsub):
            u_side(s).wait_send()

        def left(d):
            for s in range(nsub):
                u_out(d, s).wait_send()

        each(1, chips, left)

    def rest(d):
        t = ahead(d)

        @pl.when(jnp.logical_and(t >= c, d > 0))
        def _():
            for s in range(nsub):
                u_forward(t, s, t * 2 + h).wait_send()

        @pl.when(t > c)
        def _():
            for s in range(nsub):
                for e in range(2):
                    p_up(t * 2 + e, s).wait_send()

        @pl.when(d > 0)
        def _():
            lg_out(d).wait_send()
            lg_forward(d).wait_send()

    each(0, chips, rest)
    lg_side().wait_send()

    def tail(k):
        lz_out(k).wait_send()
        k_out(k).wait_send()
        e_out(k).wait_send()

    each(1, n_cols, tail)


def paired_kernel(
    n_rows, n_cols,
    row_ref, u_ref, up_ref, col_ref, piv_ref, rank_ref,
    panel_ref, cores_ref,
    xh, xl, x0, ch, cl, us, ps, pr, pq, pin, lg, ks, kd, eb,
    u_loc, nat_x, nat_y, nat_fwd, full1, near1, half1,
    lift, full0, half0, lift_x, lift_y, lift_fx, lift_fy,
    side_send, side_recv, x_send, x_recv, p_send, p_recv, q_send, q_recv,
    l_loc, l_send, l_recv, g_send, g_recv, l_side, l_got,
    k_send, k_recv, e_send, e_recv,
):
    r, c = lax.axis_index("row"), lax.axis_index("col")
    chips = n_rows // 2
    nx = math.isqrt(chips)
    q, h = r // 2, r % 2
    qy, qx = q // nx, q % nx
    xn, yn, dn = qy * nx + 1 - qx, (1 - qy) * nx + qx, (1 - qy) * nx + 1 - qx
    tiles, _, ranks, wc = row_ref.shape
    nsub, sw = us.shape[1], us.shape[5]
    wq = wc // chips
    rank2 = lg.shape[4]
    width = n_cols - 2
    sib = (q * 2 + 1 - h, c)
    to_x, to_y = (xn * 2 + h, c), (yn * 2 + h, c)
    stages = 2 * nsub

    def ahead(d):
        return ((qy + d // nx) % nx) * nx + (qx + d % nx) % nx

    def rcopy(src, dst, ssem, rsem, dev):
        return pltpu.make_async_remote_copy(
            src_ref=src, dst_ref=dst, send_sem=ssem, recv_sem=rsem, device_id=dev, device_id_type=MESH
        )

    def each(first, last, body):
        lax.fori_loop(first, last, lambda i, z: (body(i), z)[1], 0)

    def ts(i):
        t = jnp.where(c == 0, 1 - i // nsub, n_cols - 1 - i % width)
        return t, jnp.where(c == 0, i % nsub, i // width)

    def active(i):
        return ts(i)[0] >= c

    def lifted(i):
        return jnp.logical_and(c < 2, ts(i)[0] > 0)

    def ucols(s):
        return u_ref.at[:, :, pl.ds(pl.multiple_of(s * sw, sw), sw)]

    def local_u(s):
        return pltpu.make_async_copy(ucols(s), us.at[r, s, 1], u_loc.at[s])

    def nat_out(s):
        return rcopy(ucols(s), us.at[r, s, 1], nat_x.at[s], full1.at[q, s], to_x)

    def nat_near(s, k):
        rows = slice(k * (wc // 2), (k + 1) * (wc // 2))
        src = u_ref.at[:, rows, pl.ds(pl.multiple_of(s * sw, sw), sw)]
        return rcopy(src, us.at[r, s, 1, :, rows, :], nat_y.at[s, k], near1.at[q, s, k], to_y)

    def nat_full(t, s):
        b = 2 * t + h
        return rcopy(us.at[b, s, 1], us.at[b, s, 1], nat_fwd.at[t, s, 0], full1.at[t, s], sib)

    def nat_half(t, s, k, got):
        part = us.at[2 * t + h, s, 1, :, k * (wc // 2):(k + 1) * (wc // 2), :]
        return rcopy(part, part, nat_fwd.at[t, s, k], got.at[t, s, k], to_x)

    def piece(b, s, g):
        return us.at[b, s, 0, :, pl.ds(pl.multiple_of(g * wq, wq), wq), :]

    def lift_out(s, g):
        rows = pl.ds(pl.multiple_of(g * wq, wq), wq)
        src = u_ref.at[:, rows, pl.ds(pl.multiple_of(s * sw, sw), sw)]
        return rcopy(src, piece(r, s, g), lift.at[s, g], full0.at[q, s, g], (g * 2 + h, 1 - c))

    def lift_full(t, s, g, sem, dev):
        p = piece(2 * t + h, s, g)
        return rcopy(p, p, sem.at[t, s], full0.at[t, s, g], dev)

    def lift_half(t, s, g, k, sem, dev):
        rows = pl.ds(pl.multiple_of(g * wq + k * (wq // 2), wq // 2), wq // 2)
        p = us.at[2 * t + h, s, 0, :, rows, :]
        return rcopy(p, p, sem.at[t, s], half0.at[t, s, k], dev)

    def side(t, s, kk, b):
        return rcopy(us.at[b, s, kk], us.at[b, s, kk], side_send.at[t, s, kk], side_recv.at[t, s, kk], sib)

    def x_swap(m):
        return rcopy(row_ref.at[m], x0.at[m], x_send.at[m], x_recv.at[m], (r, 1 - c))

    def p_up(b, s, m):
        return rcopy(ps.at[b, s, m], pr.at[b, s, m], p_send.at[b, s, m], p_recv.at[b, s, m], (r, c + 1))

    def l_part(j, nb, g):
        return lg.at[h, nb, j, pl.ds(pl.multiple_of(g * wq, wq), wq), :]

    def l_out(o, nb):
        rows = pl.ds(pl.multiple_of((o + nb) * wc + q * wq, wq), wq)
        return rcopy(up_ref.at[0, h, rows, :], l_part(c, nb, q), l_send.at[o, nb], l_recv.at[c, nb], (r, o))

    def g_out(j, nb, d):
        p = l_part(j, nb, q)
        return rcopy(p, p, g_send.at[j, nb, d], g_recv.at[j, nb, q], (ahead(d) * 2 + h, c))

    def l_sib(j, nb, comp):
        return rcopy(lg.at[comp, nb, j], lg.at[comp, nb, j], l_side.at[j, nb], l_got.at[j, nb], sib)

    def l_own(nb):
        rows = pl.ds(pl.multiple_of((c + nb) * wc, wc), wc)
        return pltpu.make_async_copy(up_ref.at[0, :, rows, :], lg.at[:, nb, c], l_loc.at[nb])

    def blocks(o, body):
        @pl.when(o != 1)
        def _():
            body(0)

        @pl.when(o == 0)
        def _():
            body(1)

    def others(body):
        each(1, n_cols, lambda k: body((c + k) % n_cols))

    def q_up(m):
        return rcopy(pq.at[m], pin.at[m], q_send.at[m], q_recv.at[m], (r, 1))

    def k_out(j, m):
        return rcopy(ks.at[j, m], kd.at[c, m], k_send.at[j, m], k_recv.at[c, m], (r, j))

    def e_out(k):
        return rcopy(eb.at[c], eb.at[c], e_send.at[k], e_recv.at[c], (r, (c + k) % n_cols))

    blocks(c, lambda nb: l_own(nb).start())
    barrier = pltpu.get_barrier_semaphore()

    def signal(dev):
        pl.semaphore_signal(barrier, inc=1, device_id=dev, device_id_type=MESH)

    signal(sib)
    each(1, chips, lambda d: signal((ahead(d) * 2 + h, c)))
    each(1, n_cols, lambda k: signal((r, (c + k) % n_cols)))

    @pl.when(c < 2)
    def _():
        each(1, chips, lambda d: signal((ahead(d) * 2 + h, 1 - c)))

    pl.semaphore_wait(barrier, 1 + (chips - 1) + (n_cols - 1) + jnp.where(c < 2, chips - 1, 0))

    def native_out(i):
        t, s = ts(i)

        @pl.when(jnp.logical_and(active(i), q == t))
        def _():
            nat_out(s).start()
            for k in range(2):
                nat_near(s, k).start()
            local_u(s).start()

    def lift_in(i):
        t, s = ts(i)

        @pl.when(lifted(i))
        def _():
            lift_full(t, s, q, lift_x, sib).wait_recv()
            lift_full(t, s, q, lift_x, to_x).start()
            lift_full(t, s, q, lift_y, to_y).start()

    def relay_native(i):
        t, s = ts(i)

        @pl.when(jnp.logical_and(active(i), yn == t))
        def _():
            for k in range(2):
                nat_half(t, s, k, near1).wait_recv()
                nat_half(t, s, k, half1).start()

    def relay_lift(i):
        t, s = ts(i)

        @pl.when(lifted(i))
        def _():
            lift_full(t, s, xn, lift_x, sib).wait_recv()
            lift_half(t, s, xn, 0, lift_fy, to_y).start()
            lift_full(t, s, yn, lift_x, sib).wait_recv()
            lift_half(t, s, yn, 1, lift_fx, to_x).start()

    def collect(i):
        t, s = ts(i)

        @pl.when(active(i))
        def _():
            @pl.when(dn == t)
            def _():
                for k in range(2):
                    nat_half(t, s, k, half1).wait_recv()

            @pl.when(q == t)
            def _():
                local_u(s).wait()

            @pl.when(xn == t)
            def _():
                nat_full(t, s).wait_recv()

            side(t, s, 1, 2 * t + h).start()

        @pl.when(lifted(i))
        def _():
            lift_half(t, s, dn, 0, lift_fy, sib).wait_recv()
            lift_half(t, s, dn, 1, lift_fx, sib).wait_recv()
            side(t, s, 0, 2 * t + h).start()

    def lifts(s):
        each(0, chips, lambda g: lift_out(s, g).start())

    sender = jnp.where(c == 0, q > 1, jnp.logical_and(c == 1, q == 1))

    @pl.when(sender)
    def _():
        lifts(0)

    @pl.when(jnp.logical_and(sender, c == 1))
    def _():
        for s in range(1, nsub):
            lifts(s)

    @pl.when(c < 2)
    def _():
        for m in range(tiles):
            x_swap(m).start()

    each(0, stages, lambda i: pl.when(jnp.logical_or(c > 1, i < width))(lambda: native_out(i)))
    others(lambda o: blocks(o, lambda nb: l_out(o, nb).start()))

    for m in range(tiles):
        for p in range(2):
            a, b = split(row_ref[m, p])
            xh[1, m, p * ranks:(p + 1) * ranks, :] = a
            xl[1, m, p * ranks:(p + 1) * ranks, :] = b

    pos = c * wc + lax.broadcasted_iota(jnp.int32, (wc, ranks), 0)
    parts = []
    for i in range(tiles):
        hit = pos == piv_ref[i:i + 1, :]
        for p in range(2):
            parts.append(jnp.sum(jnp.where(hit, col_ref[i, p], 0.0), axis=0, keepdims=True))
    parts.append(jnp.zeros((eb.shape[1] - 2 * tiles, ranks), jnp.float32))
    eb[c] = jnp.concatenate(parts, axis=0)
    each(1, n_cols, lambda k: e_out(k).start())

    def spread(j):
        def share(nb):
            p = l_part(j, nb, q)
            rcopy(p, p, l_send.at[j, nb], l_recv.at[j, nb], sib).wait_recv()
            each(1, chips, lambda d: g_out(j, nb, d).start())

        blocks(c, share)

    @pl.when(c < 2)
    def _():
        for i in range(width):
            lift_in(i)
        for i in range(width):
            relay_native(i)
            relay_lift(i)
        for i in range(width, stages):
            native_out(i)

        @pl.when(c == 0)
        def _():
            x_swap(0).wait_send()

            @pl.when(sender)
            def _():
                for s in range(1, nsub):
                    lifts(s)

        for i in range(width, stages):
            lift_in(i)
        for i in range(width):
            collect(i)

    @pl.when(c > 1)
    def _():
        each(0, stages, relay_native)
        each(0, stages, collect)
        others(spread)

    def gather():
        blocks(c, lambda nb: l_own(nb).wait())

        def pieces(j, nb):
            def got(d):
                p = l_part(j, nb, ahead(d))
                rcopy(p, p, g_send.at[j, nb, d], g_recv.at[j, nb, ahead(d)], sib).wait_recv()

            each(1, chips, got)
            l_sib(j, nb, h).start()

        others(lambda j: blocks(c, lambda nb: pieces(j, nb)))
        others(lambda j: blocks(c, lambda nb: l_sib(j, nb, 1 - h).wait_recv()))

    def entries_in():
        each(1, n_cols, lambda k: rcopy(
            eb.at[(c + k) % n_cols], eb.at[(c + k) % n_cols], e_send.at[k], e_recv.at[(c + k) % n_cols], sib
        ).wait_recv())

    def scaled(t, m, nb):
        entries = jnp.sum(eb[...], axis=0)
        lines = []
        levels = lax.broadcasted_iota(jnp.int32, (1, ranks), 1)
        for i in range(tiles):
            er, ei = entries[2 * i:2 * i + 1], entries[2 * i + 1:2 * i + 2]
            keep = (levels < RANK_STEP * rank_ref[i]).astype(jnp.float32)
            mag = jnp.maximum(er * er + ei * ei, 1.0)
            lines.append(keep * er / mag)
            lines.append(-keep * ei / mag)
        factor_r, factor_i = lines[0], lines[1]
        for i in range(1, tiles):
            factor_r = jnp.where(m == i, lines[2 * i], factor_r)
            factor_i = jnp.where(m == i, lines[2 * i + 1], factor_i)
        pad = jnp.zeros((126, ranks), jnp.float32)
        turned = jnp.concatenate([factor_r, factor_i, pad], axis=0).T
        fr, fi = turned[:, 0:1], turned[:, 1:2]
        vr, vi = [], []
        for hh in range(2):
            for s in range(nsub):
                vr.append(ps[2 * t + hh, s, m, 0])
                vi.append(ps[2 * t + hh, s, m, 1])
        vr, vi = jnp.concatenate(vr, axis=1), jnp.concatenate(vi, axis=1)
        wr = vr * fr - vi * fi
        wi = vr * fi + vi * fr
        a, b = split(wr)
        ch[nb, m, 0:ranks, :] = a
        cl[nb, m, 0:ranks, :] = b
        a, b = split(wi)
        ch[nb, m, ranks:2 * ranks, :] = a
        cl[nb, m, ranks:2 * ranks, :] = b
        return wr, wi

    def finish_next(m):
        @pl.when(m == 0)
        def _():
            entries_in()

        wr, wi = scaled(c + 1, m, 1)
        pq[m, 0] = wr
        pq[m, 1] = wi
        q_up(m).start()

    def finish(m):
        @pl.when(m == 0)
        def _():
            gather()

            @pl.when(c > 0)
            def _():
                entries_in()

        wr, wi = scaled(c, m, 0)
        panel_ref[m, 0] = wr
        panel_ref[m, 1] = wi

        def core(j, carry):
            def product(nb):
                uh, ul = split(jnp.concatenate([lg[0, nb, j], lg[1, nb, j]], axis=1))
                prod = dot3(ch[nb, m], cl[nb, m], uh, ul)
                real = prod[:ranks, :rank2] - prod[ranks:, rank2:]
                imag = prod[:ranks, rank2:] + prod[ranks:, :rank2]
                return real, imag

            real, imag = product(0)

            @pl.when(c > 0)
            def _():
                ks[j, m, 0] = real
                ks[j, m, 1] = imag

            @pl.when(c == 0)
            def _():
                real1, imag1 = product(1)
                ks[j, m, 0] = real + real1
                ks[j, m, 1] = imag + imag1

            @pl.when(j != c)
            def _():
                k_out(j, m).start()

            return carry

        lax.fori_loop(0, n_cols, core, 0)

    half = width * tiles
    total = 2 * half
    final0 = jnp.where(c == 0, half + nsub - 1, (nsub - 1) * half + n_cols - 1 - c)

    def unit(u, carry):
        i = u // half * width + u % width
        m = u // width % tiles
        t, s = ts(i)

        @pl.when(active(i))
        def _():
            @pl.when(jnp.logical_and(c < 2, jnp.logical_and(u < half, u % width == 0)))
            def _():
                x_swap(m).wait_recv()
                for p in range(2):
                    a, b = split(x0[m, p])
                    xh[0, m, p * ranks:(p + 1) * ranks, :] = a
                    xl[0, m, p * ranks:(p + 1) * ranks, :] = b

            for e in range(2):
                b = 2 * t + (h + e) % 2

                if e == 1:
                    @pl.when(m == 0)
                    def _():
                        side(t, s, 1, b).wait_recv()

                        @pl.when(lifted(i))
                        def _():
                            side(t, s, 0, b).wait_recv()

                def product(kk):
                    uh, ul = split(jnp.concatenate([us[b, s, kk, 0], us[b, s, kk, 1]], axis=1))
                    prod = dot3(xh[kk, m], xl[kk, m], uh, ul)
                    real = prod[:ranks, :sw] - prod[ranks:, sw:]
                    imag = prod[:ranks, sw:] + prod[ranks:, :sw]
                    return real, imag

                real, imag = product(1)

                @pl.when(lifted(i))
                def _():
                    real0, imag0 = product(0)
                    ps[b, s, m, 0] = real + real0
                    ps[b, s, m, 1] = imag + imag0

                @pl.when(jnp.logical_and(c == 0, t == 0))
                def _():
                    ps[b, s, m, 0] = real
                    ps[b, s, m, 1] = imag

                @pl.when(c > 1)
                def _():
                    p_up(b, s, m).wait_recv()
                    ps[b, s, m, 0] = real + pr[b, s, m, 0]
                    ps[b, s, m, 1] = imag + pr[b, s, m, 1]

                @pl.when(jnp.logical_and(t > c, c > 0))
                def _():
                    p_up(b, s, m).start()

        @pl.when(jnp.logical_and(c == 0, jnp.logical_and(u < half, u % width == width - 1)))
        def _():
            finish_next(m)

        @pl.when(jnp.logical_and(c != 1, jnp.logical_or(u == final0, u == final0 + width)))
        def _():
            finish(m)

        @pl.when(jnp.logical_and(c < 2, u == width - 1))
        def _():
            for i in range(width, stages):
                relay_native(i)
                relay_lift(i)

        @pl.when(jnp.logical_and(c < 2, u == half - 1))
        def _():
            for i in range(width, stages):
                collect(i)

            @pl.when(c == 0)
            def _():
                others(spread)

        return carry

    lax.fori_loop(0, total, unit, 0)

    @pl.when(c == 1)
    def _():
        entries_in()
        for m in range(tiles):
            q_up(m).wait_recv()
            panel_ref[m] = pin[m]

    for m in range(tiles):
        @pl.when(c != 1)
        def _():
            cores_ref[m, 0] = ks[c, m]

        @pl.when(c == 1)
        def _():
            cores_ref[m, 0] = jnp.zeros_like(ks[c, m])

        def add(o):
            @pl.when(o != 1)
            def _():
                rcopy(ks.at[c, m], kd.at[o, m], k_send.at[c, m], k_recv.at[o, m], sib).wait_recv()
                cores_ref[m, 0] = cores_ref[m, 0] + kd[o, m]

        others(add)

    @pl.when(sender)
    def _():
        for s in range(nsub):
            each(0, chips, lambda g: lift_out(s, g).wait_send())

    @pl.when(c < 2)
    def _():
        for m in range(tiles):
            @pl.when(jnp.logical_or(c == 1, m > 0))
            def _():
                x_swap(m).wait_send()

    @pl.when(c == 0)
    def _():
        for m in range(tiles):
            q_up(m).wait_send()

    def drain(i):
        t, s = ts(i)

        @pl.when(active(i))
        def _():
            @pl.when(q == t)
            def _():
                nat_out(s).wait_send()
                for k in range(2):
                    nat_near(s, k).wait_send()

            @pl.when(yn == t)
            def _():
                for k in range(2):
                    nat_half(t, s, k, half1).wait_send()

            side(t, s, 1, 2 * t + h).wait_send()

            @pl.when(lifted(i))
            def _():
                lift_full(t, s, q, lift_x, sib).wait_send()
                lift_full(t, s, q, lift_y, sib).wait_send()
                lift_half(t, s, xn, 0, lift_fy, sib).wait_send()
                lift_half(t, s, yn, 1, lift_fx, sib).wait_send()
                side(t, s, 0, 2 * t + h).wait_send()

            @pl.when(jnp.logical_and(t > c, c > 0))
            def _():
                for m in range(tiles):
                    for e in range(2):
                        p_up(2 * t + e, s, m).wait_send()

    each(0, stages, drain)

    def tail_l(j):
        def left(nb):
            each(1, chips, lambda d: g_out(j, nb, d).wait_send())
            l_sib(j, nb, h).wait_send()

        blocks(c, left)
        blocks(j, lambda nb: l_out(j, nb).wait_send())

        @pl.when(c != 1)
        def _():
            for m in range(tiles):
                k_out(j, m).wait_send()

    others(tail_l)
    each(1, n_cols, lambda k: e_out(k).wait_send())


def paired(n_rows, n_cols, col_samples, row_samples, pivot_rows, rank_blocks, upper_inverse, upanel_left):
    tiles, _, ranks, wc = row_samples.shape
    wr = upper_inverse.shape[2]
    left_ranks = upanel_left.shape[3]
    chips = n_rows // 2
    nsub = wr // 128
    sw = wr // nsub
    f32, bf16 = jnp.float32, jnp.bfloat16
    dma = pltpu.SemaphoreType.DMA
    vmem = pl.BlockSpec(memory_space=pltpu.VMEM)
    hbm = pl.BlockSpec(memory_space=pl.ANY)
    sums = pltpu.VMEM((n_rows, nsub, tiles, 2, ranks, sw), f32)
    return pl.pallas_call(
        functools.partial(paired_kernel, n_rows, n_cols),
        out_shape=(
            jax.ShapeDtypeStruct((tiles, 2, ranks, wc), f32),
            jax.ShapeDtypeStruct((tiles, 1, 2, ranks, left_ranks), f32),
        ),
        in_specs=[vmem, hbm, hbm, vmem, vmem, pl.BlockSpec(memory_space=pltpu.SMEM)],
        out_specs=(vmem, vmem),
        scratch_shapes=[
            pltpu.VMEM((2, tiles, 2 * ranks, wc), bf16),
            pltpu.VMEM((2, tiles, 2 * ranks, wc), bf16),
            pltpu.VMEM((tiles, 2, ranks, wc), f32),
            pltpu.VMEM((2, tiles, 2 * ranks, wc), bf16),
            pltpu.VMEM((2, tiles, 2 * ranks, wc), bf16),
            pltpu.VMEM((n_rows, nsub, 2, 2, wc, sw), f32),
            sums,
            sums,
            pltpu.VMEM((tiles, 2, ranks, wc), f32),
            pltpu.VMEM((tiles, 2, ranks, wc), f32),
            pltpu.VMEM((2, 2, n_cols, wc, left_ranks), f32),
            pltpu.VMEM((n_cols, tiles, 2, ranks, left_ranks), f32),
            pltpu.VMEM((n_cols, tiles, 2, ranks, left_ranks), f32),
            pltpu.VMEM((n_cols, -(-2 * tiles // 8) * 8, ranks), f32),
            dma((nsub,)), dma((nsub,)), dma((nsub, 2)), dma((n_cols, nsub, 2)), dma((n_cols, nsub)),
            dma((n_cols, nsub, 2)), dma((n_cols, nsub, 2)),
            dma((nsub, chips)), dma((n_cols, nsub, chips)), dma((n_cols, nsub, 2)),
            dma((n_cols, nsub)), dma((n_cols, nsub)), dma((n_cols, nsub)), dma((n_cols, nsub)),
            dma((n_cols, nsub, 2)), dma((n_cols, nsub, 2)), dma((tiles,)), dma((tiles,)),
            dma((n_rows, nsub, tiles)), dma((n_rows, nsub, tiles)), dma((tiles,)), dma((tiles,)),
            dma((2,)), dma((n_cols, 2)), dma((n_cols, 2)), dma((n_cols, 2, chips)), dma((n_cols, 2, chips)),
            dma((n_cols, 2)), dma((n_cols, 2)),
            dma((n_cols, tiles)), dma((n_cols, tiles)), dma((n_cols,)), dma((n_cols,)),
        ],
        compiler_params=pltpu.CompilerParams(
            collective_id=0, has_side_effects=True, vmem_limit_bytes=56 * 1024 * 1024
        ),
    )(row_samples, upper_inverse, upanel_left, col_samples, pivot_rows, rank_blocks)


def on_device(n_rows, n_cols, col_samples, row_samples, pivot_rows, rank_blocks, upper_inverse, upanel_left):
    tiles, _, ranks, wc = row_samples.shape
    wr = upper_inverse.shape[2]
    left_ranks = upanel_left.shape[3]
    chips = n_rows // 2
    if chips != n_cols or wc != 2 * wr:
        raise ValueError("unsupported mesh")
    if chips == 4 and wr == 128 * (n_cols - 2):
        return paired(
            n_rows, n_cols, col_samples, row_samples, pivot_rows, rank_blocks, upper_inverse, upanel_left
        )
    nsub = max(wr // 128, 1)
    sw = wr // nsub
    wq = wc // chips
    m = 2 * tiles * ranks
    f32, bf16 = jnp.float32, jnp.bfloat16
    dma = pltpu.SemaphoreType.DMA
    vmem = pl.BlockSpec(memory_space=pltpu.VMEM)
    hbm = pl.BlockSpec(memory_space=pl.ANY)
    return pl.pallas_call(
        functools.partial(kernel, n_rows, n_cols),
        out_shape=(
            jax.ShapeDtypeStruct((tiles, 2, ranks, wc), f32),
            jax.ShapeDtypeStruct((tiles, 1, 2, ranks, left_ranks), f32),
        ),
        in_specs=[vmem, hbm, hbm, vmem, vmem, pl.BlockSpec(memory_space=pltpu.SMEM)],
        out_specs=(vmem, vmem),
        scratch_shapes=[
            pltpu.VMEM((m, wc), bf16),
            pltpu.VMEM((m, wc), bf16),
            pltpu.VMEM((m, wc), bf16),
            pltpu.VMEM((m, wc), bf16),
            pltpu.VMEM((n_rows, nsub, 2, wc, sw), f32),
            pltpu.VMEM((n_rows, nsub, m, sw), f32),
            pltpu.VMEM((n_rows, nsub, m, sw), f32),
            pltpu.VMEM((m, sw), f32),
            pltpu.VMEM((n_cols, wq, left_ranks), f32),
            pltpu.VMEM((2, chips, n_cols, wq, left_ranks), f32),
            pltpu.VMEM((n_cols, tiles, 2, ranks, left_ranks), f32),
            pltpu.VMEM((n_cols, tiles, 2, ranks, left_ranks), f32),
            pltpu.VMEM((n_cols, -(-2 * tiles // 8) * 8, ranks), f32),
            dma((nsub,)), dma((chips, nsub)), dma((nsub,)), dma((chips, nsub)), dma((n_rows, nsub)),
            dma((n_rows, nsub)), dma((n_rows, nsub)),
            dma((1,)), dma((n_cols,)), dma((n_cols,)), dma((1,)), dma((chips,)), dma((1,)), dma((chips,)),
            dma((2, chips)),
            dma((n_cols,)), dma((n_cols,)), dma((n_cols,)), dma((n_cols,)),
        ],
        compiler_params=pltpu.CompilerParams(
            collective_id=0, has_side_effects=True, vmem_limit_bytes=56 * 1024 * 1024
        ),
    )(row_samples, upper_inverse, upanel_left, col_samples, pivot_rows, rank_blocks)


def solution(mesh):
    in_specs = (
        P("row", None, "col", None),
        P("row", None, None, "col"),
        P("row", None),
        P("row"),
        P(None, "col", "row"),
        P("col", None, None, None),
    )
    out_specs = (P("row", None, None, "col"), P("row", "col", None, None, None))
    body = functools.partial(on_device, mesh.shape["row"], mesh.shape["col"])
    return jax.shard_map(body, mesh=mesh, in_specs=in_specs, out_specs=out_specs, check_vma=False)
```

```python
import functools
import math

import jax
import jax.numpy as jnp
from jax import lax
from jax.experimental import pallas as pl
from jax.experimental.pallas import tpu as pltpu
from jax.sharding import PartitionSpec as P

RANK_STEP = 16
MESH = pl.DeviceIdType.MESH


def split(x):
    high = x.astype(jnp.bfloat16)
    low = (x - high.astype(jnp.float32)).astype(jnp.bfloat16)
    return high, low


def dot3(xh, xl, uh, ul):
    def single(a, b):
        return jnp.dot(a, b, preferred_element_type=jnp.float32)

    return single(xh, uh) + (single(xh, ul) + single(xl, uh))


def kernel(
    n_rows, n_cols,
    row_ref, u_ref, up_ref, col_ref, piv_ref, rank_ref,
    panel_ref, cores_ref,
    xh, xl, ch, cl, us, ps, pr, fin, lz, lg, ks, kr, eb,
    u_loc, u_send, u_sib, u_fwd, u_recv,
    p_send, p_recv,
    lz_loc, lz_send, lz_recv, lg_loc, lg_send, lg_sib, lg_fwd, lg_recv,
    k_send, k_recv, e_send, e_recv,
):
    r, c = lax.axis_index("row"), lax.axis_index("col")
    chips = n_rows // 2
    nx = math.isqrt(chips)
    ny = chips // nx
    q, h = r // 2, r % 2
    qy, qx = q // nx, q % nx
    tiles, _, ranks, wc = row_ref.shape
    nsub, sw = us.shape[1], us.shape[4]
    wq = lz.shape[1]
    half = tiles * ranks
    sib = (q * 2 + 1 - h, c)

    def ahead(d):
        return ((qy + d // nx) % ny) * nx + (qx + d % nx) % nx

    def behind(d):
        return ((qy + ny - d // nx) % ny) * nx + (qx + nx - d % nx) % nx

    def rcopy(src, dst, ssem, rsem, dev):
        return pltpu.make_async_remote_copy(
            src_ref=src, dst_ref=dst, send_sem=ssem, recv_sem=rsem, device_id=dev, device_id_type=MESH
        )

    def u_out(d, s):
        return rcopy(
            u_ref.at[:, :, s * sw:(s + 1) * sw], us.at[r, s], u_send.at[d, s], u_recv.at[r, s],
            (behind(d) * 2 + h, c),
        )

    def u_side(s):
        return rcopy(u_ref.at[:, :, s * sw:(s + 1) * sw], us.at[r, s], u_sib.at[s], u_recv.at[r, s], sib)

    def u_forward(t, s, b):
        return rcopy(us.at[b, s], us.at[b, s], u_fwd.at[t, s], u_recv.at[b, s], sib)

    def p_up(b, s):
        return rcopy(ps.at[b, s], pr.at[b, s], p_send.at[b, s], p_recv.at[b, s], (r, c + 1))

    def lz_out(k):
        to = (c + k) % n_cols
        start = pl.multiple_of(to * wc + q * wq, wq)
        return rcopy(up_ref.at[0, h, pl.ds(start, wq), :], lz.at[c], lz_send.at[k], lz_recv.at[c], (r, to))

    def lg_out(d):
        return rcopy(lz, lg.at[h, q], lg_send.at[d], lg_recv.at[h, q], (behind(d) * 2 + h, c))

    def lg_side():
        return rcopy(lz, lg.at[h, q], lg_sib.at[0], lg_recv.at[h, q], sib)

    def lg_forward(d):
        b = ahead(d)
        return rcopy(lg.at[h, b], lg.at[h, b], lg_fwd.at[d], lg_recv.at[h, b], sib)

    def k_out(k):
        to = (c + k) % n_cols
        return rcopy(ks.at[k], kr.at[c], k_send.at[k], k_recv.at[c], (r, to))

    def e_out(k):
        return rcopy(eb.at[c], eb.at[c], e_send.at[k], e_recv.at[c], (r, (c + k) % n_cols))

    def each(first, last, body):
        lax.fori_loop(first, last, lambda i, z: (body(i), z)[1], 0)

    own = [
        pltpu.make_async_copy(u_ref.at[:, :, s * sw:(s + 1) * sw], us.at[r, s], u_loc.at[s]) for s in range(nsub)
    ]
    for copy in own:
        copy.start()
    mine = pl.multiple_of(c * wc + q * wq, wq)
    lz_own = pltpu.make_async_copy(up_ref.at[0, h, pl.ds(mine, wq), :], lz.at[c], lz_loc.at[0])
    lz_own.start()
    barrier = pltpu.get_barrier_semaphore()

    def signal(dev):
        pl.semaphore_signal(barrier, inc=1, device_id=dev, device_id_type=MESH)

    signal(sib)
    each(1, chips, lambda d: signal((behind(d) * 2 + h, c)))
    each(1, n_cols, lambda k: signal((r, (c + k) % n_cols)))
    pl.semaphore_wait(barrier, 1 + (chips - 1) + (n_cols - 1))

    @pl.when(q >= c)
    def _():
        for s in range(nsub):
            u_side(s).start()

        @pl.when(q > 0)
        def _():
            for s in range(nsub):
                each(1, chips, lambda d: u_out(d, s).start())

    each(1, n_cols, lambda k: lz_out(k).start())

    for i in range(tiles):
        for p in range(2):
            a, b = split(row_ref[i, p])
            at = pl.ds(p * half + i * ranks, ranks)
            xh[at, :] = a
            xl[at, :] = b

    pos = c * wc + lax.broadcasted_iota(jnp.int32, (wc, ranks), 0)
    parts = []
    for i in range(tiles):
        hit = pos == piv_ref[i:i + 1, :]
        for p in range(2):
            parts.append(jnp.sum(jnp.where(hit, col_ref[i, p], 0.0), axis=0, keepdims=True))
    parts.append(jnp.zeros((eb.shape[1] - 2 * tiles, ranks), jnp.float32))
    eb[c] = jnp.concatenate(parts, axis=0)
    each(1, n_cols, lambda k: e_out(k).start())
    for copy in own:
        copy.wait()

    near = chips * (nsub - 1)
    total = 2 * (near + chips + nsub - 1)
    spread_at = jnp.where(c == 0, 2, 0)
    final_at = jnp.where(c == 0, total - 1, 2 * (near + chips - 1 - c) + 1)

    def finish():
        def pass_on(d2):
            o = ahead(d2)
            rcopy(lz, lg.at[h, o], lg_send.at[d2], lg_recv.at[h, o], sib).wait_recv()
            lg_forward(d2).start()

        each(1, chips, pass_on)

        each(1, n_cols, lambda k: rcopy(
            eb.at[(c + k) % n_cols], eb.at[(c + k) % n_cols], e_send.at[k], e_recv.at[(c + k) % n_cols], sib
        ).wait_recv())
        entries = jnp.sum(eb[...], axis=0)
        lines = []
        levels = lax.broadcasted_iota(jnp.int32, (1, ranks), 1)
        for i in range(tiles):
            er, ei = entries[2 * i:2 * i + 1], entries[2 * i + 1:2 * i + 2]
            keep = (levels < RANK_STEP * rank_ref[i]).astype(jnp.float32)
            mag = jnp.maximum(er * er + ei * ei, 1.0)
            lines.append(keep * er / mag)
            lines.append(-keep * ei / mag)
        lines.append(jnp.zeros((128 - 2 * tiles, ranks), jnp.float32))
        turned = jnp.concatenate(lines, axis=0).T
        for i in range(tiles):
            fr, fi = turned[:, 2 * i:2 * i + 1], turned[:, 2 * i + 1:2 * i + 2]
            lr, li = i * ranks, half + i * ranks
            vr, vi = [], []
            for hh in range(2):
                for s in range(nsub):
                    vr.append(ps[2 * c + hh, s, lr:lr + ranks, :])
                    vi.append(ps[2 * c + hh, s, li:li + ranks, :])
            vr, vi = jnp.concatenate(vr, axis=1), jnp.concatenate(vi, axis=1)
            wr = vr * fr - vi * fi
            wi = vr * fi + vi * fr
            panel_ref[i, 0] = wr
            panel_ref[i, 1] = wi
            a, b = split(wr)
            ch[lr:lr + ranks, :] = a
            cl[lr:lr + ranks, :] = b
            a, b = split(wi)
            ch[li:li + ranks, :] = a
            cl[li:li + ranks, :] = b

        pltpu.make_async_copy(lz, lg.at[h, q], lg_loc.at[0]).wait()
        each(0, chips, lambda o: rcopy(
            lz, lg.at[1 - h, o], lg_sib.at[0], lg_recv.at[1 - h, o], sib
        ).wait_recv())

        def core(k0, carry):
            k = jnp.where(c == 0, n_cols - 1 - k0, (k0 + 1) % n_cols)
            j = (c + k) % n_cols
            lr = lg[0, :, j].reshape(wc, lz.shape[2])
            li = lg[1, :, j].reshape(wc, lz.shape[2])
            rank2 = lz.shape[2]
            uh, ul = split(jnp.concatenate([lr, li], axis=1))
            prod = dot3(ch[...], cl[...], uh, ul)
            real = prod[:half, :rank2] - prod[half:, rank2:]
            imag = prod[:half, rank2:] + prod[half:, :rank2]
            for i in range(tiles):
                ks[k, i, 0] = real[i * ranks:(i + 1) * ranks]
                ks[k, i, 1] = imag[i * ranks:(i + 1) * ranks]

            @pl.when(k > 0)
            def _():
                k_out(k).start()

            return carry

        lax.fori_loop(0, n_cols, core, 0)

    def unit(u, carry):
        slot = u // 2
        t = jnp.where(slot < near, ahead(slot % chips), jnp.maximum(near + chips - 1 - slot, 0))
        s = jnp.where(slot < near, slot // chips, jnp.where(slot < near + chips, nsub - 1, slot - near - chips))
        live = jnp.logical_and(t >= c, jnp.logical_or(slot >= near, t > 0))
        e = u % 2
        b = t * 2 + (h + e) % 2

        @pl.when(u == spread_at)
        def _():
            lz_own.wait()
            each(1, n_cols, lambda k: rcopy(
                lz.at[(c + k) % n_cols], lz.at[(c + k) % n_cols], lz_send.at[k], lz_recv.at[(c + k) % n_cols], sib
            ).wait_recv())
            lg_side().start()
            pltpu.make_async_copy(lz, lg.at[h, q], lg_loc.at[0]).start()
            each(1, chips, lambda d2: lg_out(d2).start())

            @pl.when(jnp.logical_and(q == 0, q >= c))
            def _():
                for s2 in range(nsub):
                    each(1, chips, lambda d2: u_out(d2, s2).start())

        @pl.when(live)
        def _():
            @pl.when(jnp.logical_or(t != q, e > 0))
            def _():
                u_forward(t, s, b).wait_recv()

            @pl.when(jnp.logical_and(t != q, e == 0))
            def _():
                u_forward(t, s, b).start()

            ur, ui = us[b, s, 0], us[b, s, 1]
            uh, ul = split(jnp.concatenate([ur, ui], axis=1))
            prod = dot3(xh[...], xl[...], uh, ul)
            fin[0:half] = prod[:half, :sw] - prod[half:, sw:]
            fin[half:2 * half] = prod[:half, sw:] + prod[half:, :sw]

            @pl.when(c > 0)
            def _():
                rcopy(ps.at[b, s], pr.at[b, s], p_send.at[b, s], p_recv.at[b, s], sib).wait_recv()
                ps[b, s] = fin[...] + pr[b, s]

            @pl.when(c == 0)
            def _():
                ps[b, s] = fin[...]

            @pl.when(t > c)
            def _():
                p_up(b, s).start()

        @pl.when(u == final_at)
        def _():
            finish()

        return carry

    lax.fori_loop(0, total, unit, 0)
    cores_ref[:, 0] = ks[0]

    def gather(k):
        o = (c + k) % n_cols
        rcopy(ks.at[k], kr.at[o], k_send.at[k], k_recv.at[o], sib).wait_recv()
        cores_ref[:, 0] = cores_ref[:, 0] + kr[o]

    each(1, n_cols, gather)

    @pl.when(q >= c)
    def _():
        for s in range(nsub):
            u_side(s).wait_send()

        def left(d):
            for s in range(nsub):
                u_out(d, s).wait_send()

        each(1, chips, left)

    def rest(d):
        t = ahead(d)

        @pl.when(jnp.logical_and(t >= c, d > 0))
        def _():
            for s in range(nsub):
                u_forward(t, s, t * 2 + h).wait_send()

        @pl.when(t > c)
        def _():
            for s in range(nsub):
                for e in range(2):
                    p_up(t * 2 + e, s).wait_send()

        @pl.when(d > 0)
        def _():
            lg_out(d).wait_send()
            lg_forward(d).wait_send()

    each(0, chips, rest)
    lg_side().wait_send()

    def tail(k):
        lz_out(k).wait_send()
        k_out(k).wait_send()
        e_out(k).wait_send()

    each(1, n_cols, tail)


def stacked(x, uh, ul):
    rows = x.shape[0] // 2
    high = jnp.dot(x, uh, preferred_element_type=jnp.float32)
    low = jnp.dot(x[:rows], ul, preferred_element_type=jnp.float32)
    return high[:rows] + (high[rows:] + low)


def paired_kernel(
    n_rows, n_cols,
    row_ref, u_ref, up_ref, col_ref, piv_ref, rank_ref,
    panel_ref, cores_ref,
    xs, x0, cs, us, uc, lc, stg, ps, pr, pq, pin, lg, ks, ku, kd, eb,
    u_loc, nat_x, nat_y, nat_fwd, full1, near1, half1,
    lift, sc_send, sc_recv, full0, half0, lift_x, lift_y, lift_fx, lift_fy,
    side_send, side_recv, x_send, x_recv, p_send, p_recv, q_send, q_recv,
    l_loc, l_send, l_recv, g_send, g_recv, l_side, l_got,
    k_send, ku_recv, k_recv, e_send, e_recv,
):
    r, c = lax.axis_index("row"), lax.axis_index("col")
    chips = n_rows // 2
    nx = math.isqrt(chips)
    q, h = r // 2, r % 2
    qy, qx = q // nx, q % nx
    xn, yn, dn = qy * nx + 1 - qx, (1 - qy) * nx + qx, (1 - qy) * nx + 1 - qx
    tiles, _, ranks, wc = row_ref.shape
    nsub, sw = us.shape[1], us.shape[5]
    wq = wc // chips
    rank2 = lg.shape[3]
    width = n_cols - 2
    sib = (q * 2 + 1 - h, c)
    to_x, to_y = (xn * 2 + h, c), (yn * 2 + h, c)
    stages = 2 * nsub

    def ahead(d):
        return ((qy + d // nx) % nx) * nx + (qx + d % nx) % nx

    def rcopy(src, dst, ssem, rsem, dev):
        return pltpu.make_async_remote_copy(
            src_ref=src, dst_ref=dst, send_sem=ssem, recv_sem=rsem, device_id=dev, device_id_type=MESH
        )

    def each(first, last, body):
        lax.fori_loop(first, last, lambda i, z: (body(i), z)[1], 0)

    def ts(i):
        t = jnp.where(c == 0, 1 - i // nsub, n_cols - 1 - i % width)
        return t, jnp.where(c == 0, i % nsub, i // width)

    def active(i):
        return ts(i)[0] >= c

    def lifted(i):
        return jnp.logical_and(c < 2, ts(i)[0] > 0)

    def ucols(s):
        return u_ref.at[:, :, pl.ds(pl.multiple_of(s * sw, sw), sw)]

    def local_u(s):
        return pltpu.make_async_copy(ucols(s), us.at[r, s, 1], u_loc.at[s])

    def nat_out(s):
        return rcopy(ucols(s), us.at[r, s, 1], nat_x.at[s], full1.at[q, s], to_x)

    def nat_near(s, k):
        rows = slice(k * (wc // 2), (k + 1) * (wc // 2))
        src = u_ref.at[:, rows, pl.ds(pl.multiple_of(s * sw, sw), sw)]
        return rcopy(src, us.at[r, s, 1, :, rows, :], nat_y.at[s, k], near1.at[q, s, k], to_y)

    def nat_full(t, s):
        b = 2 * t + h
        return rcopy(us.at[b, s, 1], us.at[b, s, 1], nat_fwd.at[t, s, 0], full1.at[t, s], sib)

    def nat_half(t, s, k, got, dev=None):
        part = us.at[2 * t + h, s, 1, :, k * (wc // 2):(k + 1) * (wc // 2), :]
        return rcopy(part, part, nat_fwd.at[t, s, k], got.at[t, s, k], dev or to_x)

    def piece(b, s, g):
        return us.at[b, s, 0, :, pl.ds(pl.multiple_of(g * wq, wq), wq), :]

    def upiece(s, g):
        rows = pl.ds(pl.multiple_of(g * wq, wq), wq)
        return u_ref.at[:, rows, pl.ds(pl.multiple_of(s * sw, sw), sw)]

    def scatter(s, g):
        slot = stg.at[q % width, s]
        return rcopy(upiece(s, g), slot, sc_send.at[s, g], sc_recv.at[q % width, s], (g * 2 + h, c))

    def raised(t, s, src):
        return rcopy(src, piece(2 * t + h, s, q), lift.at[s, t], full0.at[t, s, q], (r, 1 - c))

    def lift_full(t, s, g, sem, dev):
        p = piece(2 * t + h, s, g)
        return rcopy(p, p, sem.at[t, s], full0.at[t, s, g], dev)

    def lift_half(t, s, g, k, sem, dev):
        rows = pl.ds(pl.multiple_of(g * wq + k * (wq // 2), wq // 2), wq // 2)
        p = us.at[2 * t + h, s, 0, :, rows, :]
        return rcopy(p, p, sem.at[t, s], half0.at[t, s, k], dev)

    def side(t, s, kk, b):
        return rcopy(us.at[b, s, kk], us.at[b, s, kk], side_send.at[t, s, kk], side_recv.at[t, s, kk], sib)

    def x_swap(m, p):
        return rcopy(row_ref.at[m, p], x0.at[m, p], x_send.at[m, p], x_recv.at[m, p], (r, 1 - c))

    def p_up(b, s, m):
        return rcopy(ps.at[b, s, m], pr.at[b, s, m], p_send.at[b, s, m], p_recv.at[b, s, m], (r, c + 1))

    def l_down(o):
        rows = pl.ds(pl.multiple_of(o * wc, wc), wc)
        return rcopy(up_ref.at[0, h, rows, :], lg.at[h, c], l_send.at[o], l_recv.at[c], (r, o))

    def l_part(j, g):
        return lg.at[h, j, pl.ds(pl.multiple_of(g * wq, wq), wq), :]

    def l_up(o):
        rows = pl.ds(pl.multiple_of(o * wc + q * wq, wq), wq)
        return rcopy(up_ref.at[0, h, rows, :], l_part(c, q), l_send.at[o], l_recv.at[c], (r, o))

    def g_out(j, d):
        return rcopy(l_part(j, q), l_part(j, q), g_send.at[j, d], g_recv.at[j, q], (ahead(d) * 2 + h, c))

    def l_sib(j, comp):
        return rcopy(lg.at[comp, j], lg.at[comp, j], l_side.at[j], l_got.at[j], sib)

    def l_own():
        rows = pl.ds(pl.multiple_of(c * wc, wc), wc)
        return pltpu.make_async_copy(up_ref.at[0, :, rows, :], lg.at[:, c], l_loc.at[0])

    def others(body):
        each(1, n_cols, lambda k: body((c + k) % n_cols))

    def q_up(m):
        return rcopy(pq.at[m], pin.at[m], q_send.at[m], q_recv.at[m], (r, 1))

    def k_out(j, m):
        return rcopy(ks.at[j, m], kd.at[c, m], k_send.at[j, m], k_recv.at[c, m], (r, j))

    def k_next(j, m):
        return rcopy(ks.at[j, m], ku.at[j, m], k_send.at[j, m], ku_recv.at[j, m], (r, 1))

    def e_out(k):
        return rcopy(eb.at[c], eb.at[c], e_send.at[k], e_recv.at[c], (r, (c + k) % n_cols))

    l_own().start()
    barrier = pltpu.get_barrier_semaphore()

    def signal(dev):
        pl.semaphore_signal(barrier, inc=1, device_id=dev, device_id_type=MESH)

    signal(sib)
    each(1, chips, lambda d: signal((ahead(d) * 2 + h, c)))
    each(1, n_cols, lambda k: signal((r, (c + k) % n_cols)))

    @pl.when(c < 2)
    def _():
        each(1, chips, lambda d: signal((ahead(d) * 2 + h, 1 - c)))

    pl.semaphore_wait(barrier, 1 + (chips - 1) + (n_cols - 1) + jnp.where(c < 2, chips - 1, 0))

    def native_x(i):
        t, s = ts(i)

        @pl.when(jnp.logical_and(active(i), q == t))
        def _():
            nat_out(s).start()
            local_u(s).start()

    def native_y(i):
        t, s = ts(i)

        @pl.when(jnp.logical_and(active(i), q == t))
        def _():
            for k in range(2):
                nat_near(s, k).start()

    def native_out(i):
        native_x(i)
        native_y(i)

    def lift_in(i):
        t, s = ts(i)

        @pl.when(lifted(i))
        def _():
            lift_full(t, s, q, lift_x, sib).wait_recv()
            lift_full(t, s, q, lift_x, to_x).start()
            lift_full(t, s, q, lift_y, to_y).start()

    def relay_native(i):
        t, s = ts(i)

        @pl.when(jnp.logical_and(active(i), yn == t))
        def _():
            nat_half(t, s, 0, near1).wait_recv()

            @pl.when(c > 0)
            def _():
                nat_half(t, s, 0, half1).start()

            nat_half(t, s, 1, near1).wait_recv()
            nat_half(t, s, 1, half1).start()

        @pl.when(jnp.logical_and(c == 0, xn == t))
        def _():
            nat_full(t, s).wait_recv()
            nat_half(t, s, 0, half1, to_y).start()

    def relay_lift(i):
        t, s = ts(i)

        @pl.when(lifted(i))
        def _():
            lift_full(t, s, xn, lift_x, sib).wait_recv()
            lift_half(t, s, xn, 0, lift_fy, to_y).start()
            lift_full(t, s, yn, lift_x, sib).wait_recv()
            lift_half(t, s, yn, 1, lift_fx, to_x).start()

    def collect(i):
        t, s = ts(i)

        @pl.when(active(i))
        def _():
            @pl.when(dn == t)
            def _():
                for k in range(2):
                    nat_half(t, s, k, half1).wait_recv()

            @pl.when(q == t)
            def _():
                local_u(s).wait()

            @pl.when(jnp.logical_and(c > 0, xn == t))
            def _():
                nat_full(t, s).wait_recv()

            side(t, s, 1, 2 * t + h).start()

        @pl.when(lifted(i))
        def _():
            lift_half(t, s, dn, 0, lift_fy, sib).wait_recv()
            lift_half(t, s, dn, 1, lift_fx, sib).wait_recv()
            side(t, s, 0, 2 * t + h).start()

    source = jnp.where(c == 0, q > 1, jnp.logical_and(c == 1, q == 1))

    def scatters(s):
        @pl.when(source)
        def _():
            each(1, chips, lambda d: scatter(s, ahead(d)).start())

    for s in range(nsub):
        scatters(s)

    each(0, stages, lambda i: pl.when(jnp.logical_or(c > 1, i < width))(lambda: native_out(i)))
    def climb(t, s):
        @pl.when(q == t)
        def _():
            raised(t, s, upiece(s, q)).start()

        @pl.when(q != t)
        def _():
            rcopy(stg.at[t % width, s], stg.at[t % width, s], lift.at[s, t], sc_recv.at[t % width, s], sib).wait_recv()
            raised(t, s, stg.at[t % width, s]).start()

    @pl.when(c == 0)
    def _():
        for s in range(nsub):
            for t in range(n_cols - 1, 1, -1):
                climb(t, s)
            for p in range(2):
                x_swap(s, p).start()

    @pl.when(c == 1)
    def _():
        for s in range(nsub):
            climb(1, s)
        for m in range(tiles):
            for p in range(2):
                x_swap(m, p).start()

    each(c + 1, n_cols, lambda o: l_up(o).start())

    @pl.when(c == 1)
    def _():
        l_down(0).start()

    pos = c * wc + lax.broadcasted_iota(jnp.int32, (wc, ranks), 0)
    parts = []
    for i in range(tiles):
        hit = pos == piv_ref[i:i + 1, :]
        for p in range(2):
            parts.append(jnp.sum(jnp.where(hit, col_ref[i, p], 0.0), axis=0, keepdims=True))
    parts.append(jnp.zeros((eb.shape[1] - 2 * tiles, ranks), jnp.float32))
    eb[c] = jnp.concatenate(parts, axis=0)
    each(1, n_cols, lambda k: e_out(k).start())

    def spread(j):
        rcopy(l_part(j, q), l_part(j, q), l_send.at[c], l_recv.at[j], sib).wait_recv()
        each(1, chips, lambda d: g_out(j, d).start())

    @pl.when(c < 2)
    def _():
        for i in range(width):
            lift_in(i)

            @pl.when(c == 0)
            def _():
                native_x(width + i)

        relay_native(0)

        @pl.when(c == 1)
        def _():
            relay_lift(0)

        @pl.when(c == 0)
        def _():
            native_y(width)
            relay_lift(0)
            relay_lift(1)
            relay_native(1)
            for i in range(width + 1, stages):
                native_y(i)

        @pl.when(c == 1)
        def _():
            for i in range(1, width):
                relay_native(i)
                relay_lift(i)
            for i in range(width, stages):
                native_out(i)

        for i in range(width):
            collect(i)

    @pl.when(c > 1)
    def _():
        each(0, stages, relay_native)
        each(0, c, lambda o: l_down(o).start())
        each(0, stages, collect)
        each(0, c, spread)


    for m in range(tiles):
        for p in range(2):
            a, b = split(row_ref[m, p])
            xs[1, m, p * ranks:(p + 1) * ranks, :] = a
            xs[1, m, (p + 2) * ranks:(p + 3) * ranks, :] = b

    def gather():
        l_own().wait()

        def low(j):
            each(1, chips, lambda d: rcopy(
                l_part(j, ahead(d)), l_part(j, ahead(d)), g_send.at[j, d], g_recv.at[j, ahead(d)], sib
            ).wait_recv())
            l_sib(j, h).start()

        def high(j):
            rcopy(lg.at[h, j], lg.at[h, j], l_send.at[c], l_recv.at[j], sib).wait_recv()
            l_sib(j, h).start()

        each(0, c, low)
        each(c + 1, n_cols, high)

    def gathered():
        each(0, c, lambda j: l_sib(j, 1 - h).wait_recv())
        each(c + 1, n_cols, lambda j: l_sib(j, 1 - h).wait_recv())

    def entries_in():
        each(1, n_cols, lambda k: rcopy(
            eb.at[(c + k) % n_cols], eb.at[(c + k) % n_cols], e_send.at[k], e_recv.at[(c + k) % n_cols], sib
        ).wait_recv())

    def scaled(t, m):
        entries = jnp.sum(eb[...], axis=0)
        lines = []
        levels = lax.broadcasted_iota(jnp.int32, (1, ranks), 1)
        for i in range(tiles):
            er, ei = entries[2 * i:2 * i + 1], entries[2 * i + 1:2 * i + 2]
            keep = (levels < RANK_STEP * rank_ref[i]).astype(jnp.float32)
            mag = jnp.maximum(er * er + ei * ei, 1.0)
            lines.append(keep * er / mag)
            lines.append(-keep * ei / mag)
        factor_r, factor_i = lines[0], lines[1]
        for i in range(1, tiles):
            factor_r = jnp.where(m == i, lines[2 * i], factor_r)
            factor_i = jnp.where(m == i, lines[2 * i + 1], factor_i)
        pad = jnp.zeros((126, ranks), jnp.float32)
        turned = jnp.concatenate([factor_r, factor_i, pad], axis=0).T
        fr, fi = turned[:, 0:1], turned[:, 1:2]
        vr, vi = [], []
        for hh in range(2):
            for s in range(nsub):
                vr.append(ps[2 * t + hh, s, m, 0])
                vi.append(ps[2 * t + hh, s, m, 1])
        vr, vi = jnp.concatenate(vr, axis=1), jnp.concatenate(vi, axis=1)
        wr = vr * fr - vi * fi
        wi = vr * fi + vi * fr
        return wr, wi

    def finish_next(m):
        @pl.when(m == 0)
        def _():
            entries_in()

        wr, wi = scaled(c + 1, m)
        pq[m, 0] = wr
        pq[m, 1] = wi
        q_up(m).start()

    def finish(m):
        @pl.when(m == 0)
        def _():
            gathered()

            @pl.when(c > 0)
            def _():
                entries_in()

        @pl.when(c == 1)
        def _():
            q_up(m).wait_recv()
            panel_ref[m] = pin[m]

        @pl.when(c != 1)
        def _():
            wr, wi = scaled(c, m)
            panel_ref[m, 0] = wr
            panel_ref[m, 1] = wi

        for p in range(2):
            a, b = split(panel_ref[m, p])
            cs[p * ranks:(p + 1) * ranks, :] = a
            cs[(p + 2) * ranks:(p + 3) * ranks, :] = b

        def core(j, carry):
            @pl.when(m == 0)
            def _():
                for p in range(2):
                    uh, ul = split(lg[p, j])
                    lc[j, 0, :, p * rank2:(p + 1) * rank2] = uh
                    lc[j, 1, :, p * rank2:(p + 1) * rank2] = ul

            prod = stacked(cs[...], lc[j, 0], lc[j, 1])
            ks[j, m, 0] = prod[:ranks, :rank2] - prod[ranks:, rank2:]
            ks[j, m, 1] = prod[:ranks, rank2:] + prod[ranks:, :rank2]

            @pl.when(jnp.logical_and(c == 1, j > 0))
            def _():
                k_next(j, m).wait_recv()
                ks[j, m] = ks[j, m] + ku[j, m]

            @pl.when(jnp.logical_and(c == 0, j > 0))
            def _():
                k_next(j, m).start()

            @pl.when(jnp.logical_and(c > 0, j != c))
            def _():
                k_out(j, m).start()

            return carry

        lax.fori_loop(0, n_cols, core, 0)

    half = width * tiles
    total = 2 * half
    final0 = jnp.where(c == 0, half + nsub - 1, (nsub - 1) * half + n_cols - 1 - c)
    final0 = jnp.where(c == 1, total, final0)

    def unit(u, carry):
        i = u // half * width + u % width
        m = u // width % tiles
        t, s = ts(i)

        @pl.when(jnp.logical_and(active(i), u < total))
        def _():
            @pl.when(jnp.logical_and(c < 2, jnp.logical_and(u < half, u % width == 0)))
            def _():
                for p in range(2):
                    x_swap(m, p).wait_recv()
                    a, b = split(x0[m, p])
                    xs[0, m, p * ranks:(p + 1) * ranks, :] = a
                    xs[0, m, (p + 2) * ranks:(p + 3) * ranks, :] = b

            for e in range(2):
                b = 2 * t + (h + e) % 2

                if e == 1:
                    @pl.when(m == 0)
                    def _():
                        side(t, s, 1, b).wait_recv()

                        @pl.when(lifted(i))
                        def _():
                            side(t, s, 0, b).wait_recv()

                def product(kk):
                    @pl.when(m == 0)
                    def _():
                        for p in range(2):
                            uh, ul = split(us[b, s, kk, p])
                            uc[i, e, kk, 0, :, p * sw:(p + 1) * sw] = uh
                            uc[i, e, kk, 1, :, p * sw:(p + 1) * sw] = ul

                    prod = stacked(xs[kk, m], uc[i, e, kk, 0], uc[i, e, kk, 1])
                    real = prod[:ranks, :sw] - prod[ranks:, sw:]
                    imag = prod[:ranks, sw:] + prod[ranks:, :sw]
                    return real, imag

                real, imag = product(1)

                @pl.when(lifted(i))
                def _():
                    real0, imag0 = product(0)
                    ps[b, s, m, 0] = real + real0
                    ps[b, s, m, 1] = imag + imag0

                @pl.when(jnp.logical_and(c == 0, t == 0))
                def _():
                    ps[b, s, m, 0] = real
                    ps[b, s, m, 1] = imag

                @pl.when(c > 1)
                def _():
                    p_up(b, s, m).wait_recv()
                    ps[b, s, m, 0] = real + pr[b, s, m, 0]
                    ps[b, s, m, 1] = imag + pr[b, s, m, 1]

                @pl.when(jnp.logical_and(t > c, c > 0))
                def _():
                    p_up(b, s, m).start()

        @pl.when(jnp.logical_and(c == 0, jnp.logical_and(u < half, u % width == width - 1)))
        def _():
            finish_next(m)

        @pl.when(jnp.logical_or(u == final0, u == final0 + width))
        def _():
            finish(m)

        @pl.when(jnp.logical_and(c == 0, u < width))
        def _():
            relay_native(width + u)

        @pl.when(u == jnp.where(c == 0, half - 1, jnp.where(c == 1, total - 1, width - 1)))
        def _():
            gather()

        @pl.when(jnp.logical_and(c == 1, u == 0))
        def _():
            for i in range(width, stages):
                lift_in(i)

        @pl.when(jnp.logical_and(c == 1, u == width - 1))
        def _():
            for i in range(width, stages):
                relay_native(i)
                relay_lift(i)

        @pl.when(jnp.logical_and(c < 2, u == half - 1))
        def _():
            for i in range(width, stages):
                collect(i)
            each(0, jnp.where(c == 1, 1, 0), spread)

        return carry

    lax.fori_loop(0, jnp.where(c == 1, total + 2 * width - 1, total), unit, 0)

    for m in range(tiles):
        cores_ref[m, 0] = ks[c, m]

        def add(o):
            @pl.when(o > 0)
            def _():
                rcopy(ks.at[c, m], kd.at[o, m], k_send.at[c, m], k_recv.at[o, m], sib).wait_recv()
                cores_ref[m, 0] = cores_ref[m, 0] + kd[o, m]

        others(add)

    @pl.when(c < 2)
    def _():
        for m in range(tiles):
            for p in range(2):
                x_swap(m, p).wait_send()
        for s in range(nsub):
            for t in range(1, n_cols):
                @pl.when(c == (0 if t > 1 else 1))
                def _():
                    raised(t, s, stg.at[t % width, s]).wait_send()

    @pl.when(c == 0)
    def _():
        for m in range(tiles):
            q_up(m).wait_send()

    @pl.when(source)
    def _():
        for s in range(nsub):
            each(1, chips, lambda d: scatter(s, ahead(d)).wait_send())

    def drain(i):
        t, s = ts(i)

        @pl.when(active(i))
        def _():
            @pl.when(q == t)
            def _():
                nat_out(s).wait_send()
                for k in range(2):
                    nat_near(s, k).wait_send()

            @pl.when(yn == t)
            def _():
                nat_half(t, s, 1, half1).wait_send()

            @pl.when(jnp.where(c == 0, xn == t, yn == t))
            def _():
                nat_half(t, s, 0, half1).wait_send()

            side(t, s, 1, 2 * t + h).wait_send()

            @pl.when(lifted(i))
            def _():
                lift_full(t, s, q, lift_x, sib).wait_send()
                lift_full(t, s, q, lift_y, sib).wait_send()
                lift_half(t, s, xn, 0, lift_fy, sib).wait_send()
                lift_half(t, s, yn, 1, lift_fx, sib).wait_send()
                side(t, s, 0, 2 * t + h).wait_send()

            @pl.when(jnp.logical_and(t > c, c > 0))
            def _():
                for m in range(tiles):
                    for e in range(2):
                        p_up(2 * t + e, s, m).wait_send()

    each(0, stages, drain)

    def tail_l(j):
        each(1, chips, lambda d: g_out(j, d).wait_send())
        l_down(j).wait_send()

    each(0, c, tail_l)
    each(c + 1, n_cols, lambda o: l_up(o).wait_send())

    def tail_k(j):
        l_sib(j, h).wait_send()
        for m in range(tiles):
            k_out(j, m).wait_send()

    others(tail_k)
    each(1, n_cols, lambda k: e_out(k).wait_send())


def paired(n_rows, n_cols, col_samples, row_samples, pivot_rows, rank_blocks, upper_inverse, upanel_left):
    tiles, _, ranks, wc = row_samples.shape
    wr = upper_inverse.shape[2]
    left_ranks = upanel_left.shape[3]
    chips = n_rows // 2
    nsub = wr // 128
    sw = wr // nsub
    f32, bf16 = jnp.float32, jnp.bfloat16
    dma = pltpu.SemaphoreType.DMA
    vmem = pl.BlockSpec(memory_space=pltpu.VMEM)
    hbm = pl.BlockSpec(memory_space=pl.ANY)
    sums = pltpu.VMEM((n_rows, nsub, tiles, 2, ranks, sw), f32)
    return pl.pallas_call(
        functools.partial(paired_kernel, n_rows, n_cols),
        out_shape=(
            jax.ShapeDtypeStruct((tiles, 2, ranks, wc), f32),
            jax.ShapeDtypeStruct((tiles, 1, 2, ranks, left_ranks), f32),
        ),
        in_specs=[vmem, hbm, hbm, vmem, vmem, pl.BlockSpec(memory_space=pltpu.SMEM)],
        out_specs=(vmem, vmem),
        scratch_shapes=[
            pltpu.VMEM((2, tiles, 4 * ranks, wc), bf16),
            pltpu.VMEM((tiles, 2, ranks, wc), f32),
            pltpu.VMEM((4 * ranks, wc), bf16),
            pltpu.VMEM((n_rows, nsub, 2, 2, wc, sw), f32),
            pltpu.VMEM((2 * nsub, 2, 2, 2, wc, 2 * sw), bf16),
            pltpu.VMEM((n_cols, 2, wc, 2 * left_ranks), bf16),
            pltpu.VMEM((n_cols - 2, nsub, 2, wc // chips, sw), f32),
            sums,
            sums,
            pltpu.VMEM((tiles, 2, ranks, wc), f32),
            pltpu.VMEM((tiles, 2, ranks, wc), f32),
            pltpu.VMEM((2, n_cols, wc, left_ranks), f32),
            pltpu.VMEM((n_cols, tiles, 2, ranks, left_ranks), f32),
            pltpu.VMEM((n_cols, tiles, 2, ranks, left_ranks), f32),
            pltpu.VMEM((n_cols, tiles, 2, ranks, left_ranks), f32),
            pltpu.VMEM((n_cols, -(-2 * tiles // 8) * 8, ranks), f32),
            dma((nsub,)), dma((nsub,)), dma((nsub, 2)), dma((n_cols, nsub, 2)), dma((n_cols, nsub)),
            dma((n_cols, nsub, 2)), dma((n_cols, nsub, 2)),
            dma((nsub, n_cols)), dma((nsub, chips)), dma((n_cols - 2, nsub)),
            dma((n_cols, nsub, chips)), dma((n_cols, nsub, 2)),
            dma((n_cols, nsub)), dma((n_cols, nsub)), dma((n_cols, nsub)), dma((n_cols, nsub)),
            dma((n_cols, nsub, 2)), dma((n_cols, nsub, 2)), dma((tiles, 2)), dma((tiles, 2)),
            dma((n_rows, nsub, tiles)), dma((n_rows, nsub, tiles)), dma((tiles,)), dma((tiles,)),
            dma((1,)), dma((n_cols,)), dma((n_cols,)), dma((n_cols, chips)), dma((n_cols, chips)),
            dma((n_cols,)), dma((n_cols,)),
            dma((n_cols, tiles)), dma((n_cols, tiles)), dma((n_cols, tiles)), dma((n_cols,)), dma((n_cols,)),
        ],
        compiler_params=pltpu.CompilerParams(
            collective_id=0, has_side_effects=True, vmem_limit_bytes=60 * 1024 * 1024
        ),
    )(row_samples, upper_inverse, upanel_left, col_samples, pivot_rows, rank_blocks)


def on_device(n_rows, n_cols, col_samples, row_samples, pivot_rows, rank_blocks, upper_inverse, upanel_left):
    tiles, _, ranks, wc = row_samples.shape
    wr = upper_inverse.shape[2]
    left_ranks = upanel_left.shape[3]
    chips = n_rows // 2
    if chips != n_cols or wc != 2 * wr:
        raise ValueError("unsupported mesh")
    if chips == 4 and wr == 128 * (n_cols - 2):
        return paired(
            n_rows, n_cols, col_samples, row_samples, pivot_rows, rank_blocks, upper_inverse, upanel_left
        )
    nsub = max(wr // 128, 1)
    sw = wr // nsub
    wq = wc // chips
    m = 2 * tiles * ranks
    f32, bf16 = jnp.float32, jnp.bfloat16
    dma = pltpu.SemaphoreType.DMA
    vmem = pl.BlockSpec(memory_space=pltpu.VMEM)
    hbm = pl.BlockSpec(memory_space=pl.ANY)
    return pl.pallas_call(
        functools.partial(kernel, n_rows, n_cols),
        out_shape=(
            jax.ShapeDtypeStruct((tiles, 2, ranks, wc), f32),
            jax.ShapeDtypeStruct((tiles, 1, 2, ranks, left_ranks), f32),
        ),
        in_specs=[vmem, hbm, hbm, vmem, vmem, pl.BlockSpec(memory_space=pltpu.SMEM)],
        out_specs=(vmem, vmem),
        scratch_shapes=[
            pltpu.VMEM((m, wc), bf16),
            pltpu.VMEM((m, wc), bf16),
            pltpu.VMEM((m, wc), bf16),
            pltpu.VMEM((m, wc), bf16),
            pltpu.VMEM((n_rows, nsub, 2, wc, sw), f32),
            pltpu.VMEM((n_rows, nsub, m, sw), f32),
            pltpu.VMEM((n_rows, nsub, m, sw), f32),
            pltpu.VMEM((m, sw), f32),
            pltpu.VMEM((n_cols, wq, left_ranks), f32),
            pltpu.VMEM((2, chips, n_cols, wq, left_ranks), f32),
            pltpu.VMEM((n_cols, tiles, 2, ranks, left_ranks), f32),
            pltpu.VMEM((n_cols, tiles, 2, ranks, left_ranks), f32),
            pltpu.VMEM((n_cols, -(-2 * tiles // 8) * 8, ranks), f32),
            dma((nsub,)), dma((chips, nsub)), dma((nsub,)), dma((chips, nsub)), dma((n_rows, nsub)),
            dma((n_rows, nsub)), dma((n_rows, nsub)),
            dma((1,)), dma((n_cols,)), dma((n_cols,)), dma((1,)), dma((chips,)), dma((1,)), dma((chips,)),
            dma((2, chips)),
            dma((n_cols,)), dma((n_cols,)), dma((n_cols,)), dma((n_cols,)),
        ],
        compiler_params=pltpu.CompilerParams(
            collective_id=0, has_side_effects=True, vmem_limit_bytes=56 * 1024 * 1024
        ),
    )(row_samples, upper_inverse, upanel_left, col_samples, pivot_rows, rank_blocks)


def solution(mesh):
    in_specs = (
        P("row", None, "col", None),
        P("row", None, None, "col"),
        P("row", None),
        P("row"),
        P(None, "col", "row"),
        P("col", None, None, None),
    )
    out_specs = (P("row", None, None, "col"), P("row", "col", None, None, None))
    body = functools.partial(on_device, mesh.shape["row"], mesh.shape["col"])
    return jax.shard_map(body, mesh=mesh, in_specs=in_specs, out_specs=out_specs, check_vma=False)
```

```python
import functools
import math

import jax
import jax.numpy as jnp
from jax import lax
from jax.experimental import pallas as pl
from jax.experimental.pallas import tpu as pltpu
from jax.sharding import PartitionSpec as P

RANK_STEP = 16
MESH = pl.DeviceIdType.MESH


def split(x):
    high = x.astype(jnp.bfloat16)
    low = (x - high.astype(jnp.float32)).astype(jnp.bfloat16)
    return high, low


def dot3(xh, xl, uh, ul):
    def single(a, b):
        return jnp.dot(a, b, preferred_element_type=jnp.float32)

    return single(xh, uh) + (single(xh, ul) + single(xl, uh))


def kernel(
    n_rows, n_cols,
    row_ref, u_ref, up_ref, col_ref, piv_ref, rank_ref,
    panel_ref, cores_ref,
    xh, xl, ch, cl, us, ps, pr, fin, lz, lg, ks, kr, eb,
    u_loc, u_send, u_sib, u_fwd, u_recv,
    p_send, p_recv,
    lz_loc, lz_send, lz_recv, lg_loc, lg_send, lg_sib, lg_fwd, lg_recv,
    k_send, k_recv, e_send, e_recv,
):
    r, c = lax.axis_index("row"), lax.axis_index("col")
    chips = n_rows // 2
    nx = math.isqrt(chips)
    ny = chips // nx
    q, h = r // 2, r % 2
    qy, qx = q // nx, q % nx
    tiles, _, ranks, wc = row_ref.shape
    nsub, sw = us.shape[1], us.shape[4]
    wq = lz.shape[1]
    half = tiles * ranks
    sib = (q * 2 + 1 - h, c)

    def ahead(d):
        return ((qy + d // nx) % ny) * nx + (qx + d % nx) % nx

    def behind(d):
        return ((qy + ny - d // nx) % ny) * nx + (qx + nx - d % nx) % nx

    def rcopy(src, dst, ssem, rsem, dev):
        return pltpu.make_async_remote_copy(
            src_ref=src, dst_ref=dst, send_sem=ssem, recv_sem=rsem, device_id=dev, device_id_type=MESH
        )

    def u_out(d, s):
        return rcopy(
            u_ref.at[:, :, s * sw:(s + 1) * sw], us.at[r, s], u_send.at[d, s], u_recv.at[r, s],
            (behind(d) * 2 + h, c),
        )

    def u_side(s):
        return rcopy(u_ref.at[:, :, s * sw:(s + 1) * sw], us.at[r, s], u_sib.at[s], u_recv.at[r, s], sib)

    def u_forward(t, s, b):
        return rcopy(us.at[b, s], us.at[b, s], u_fwd.at[t, s], u_recv.at[b, s], sib)

    def p_up(b, s):
        return rcopy(ps.at[b, s], pr.at[b, s], p_send.at[b, s], p_recv.at[b, s], (r, c + 1))

    def lz_out(k):
        to = (c + k) % n_cols
        start = pl.multiple_of(to * wc + q * wq, wq)
        return rcopy(up_ref.at[0, h, pl.ds(start, wq), :], lz.at[c], lz_send.at[k], lz_recv.at[c], (r, to))

    def lg_out(d):
        return rcopy(lz, lg.at[h, q], lg_send.at[d], lg_recv.at[h, q], (behind(d) * 2 + h, c))

    def lg_side():
        return rcopy(lz, lg.at[h, q], lg_sib.at[0], lg_recv.at[h, q], sib)

    def lg_forward(d):
        b = ahead(d)
        return rcopy(lg.at[h, b], lg.at[h, b], lg_fwd.at[d], lg_recv.at[h, b], sib)

    def k_out(k):
        to = (c + k) % n_cols
        return rcopy(ks.at[k], kr.at[c], k_send.at[k], k_recv.at[c], (r, to))

    def e_out(k):
        return rcopy(eb.at[c], eb.at[c], e_send.at[k], e_recv.at[c], (r, (c + k) % n_cols))

    def each(first, last, body):
        lax.fori_loop(first, last, lambda i, z: (body(i), z)[1], 0)

    own = [
        pltpu.make_async_copy(u_ref.at[:, :, s * sw:(s + 1) * sw], us.at[r, s], u_loc.at[s]) for s in range(nsub)
    ]
    for copy in own:
        copy.start()
    mine = pl.multiple_of(c * wc + q * wq, wq)
    lz_own = pltpu.make_async_copy(up_ref.at[0, h, pl.ds(mine, wq), :], lz.at[c], lz_loc.at[0])
    lz_own.start()
    barrier = pltpu.get_barrier_semaphore()

    def signal(dev):
        pl.semaphore_signal(barrier, inc=1, device_id=dev, device_id_type=MESH)

    signal(sib)
    each(1, chips, lambda d: signal((behind(d) * 2 + h, c)))
    each(1, n_cols, lambda k: signal((r, (c + k) % n_cols)))
    pl.semaphore_wait(barrier, 1 + (chips - 1) + (n_cols - 1))

    @pl.when(q >= c)
    def _():
        for s in range(nsub):
            u_side(s).start()

        @pl.when(q > 0)
        def _():
            for s in range(nsub):
                each(1, chips, lambda d: u_out(d, s).start())

    each(1, n_cols, lambda k: lz_out(k).start())

    for i in range(tiles):
        for p in range(2):
            a, b = split(row_ref[i, p])
            at = pl.ds(p * half + i * ranks, ranks)
            xh[at, :] = a
            xl[at, :] = b

    pos = c * wc + lax.broadcasted_iota(jnp.int32, (wc, ranks), 0)
    parts = []
    for i in range(tiles):
        hit = pos == piv_ref[i:i + 1, :]
        for p in range(2):
            parts.append(jnp.sum(jnp.where(hit, col_ref[i, p], 0.0), axis=0, keepdims=True))
    parts.append(jnp.zeros((eb.shape[1] - 2 * tiles, ranks), jnp.float32))
    eb[c] = jnp.concatenate(parts, axis=0)
    each(1, n_cols, lambda k: e_out(k).start())
    for copy in own:
        copy.wait()

    near = chips * (nsub - 1)
    total = 2 * (near + chips + nsub - 1)
    spread_at = jnp.where(c == 0, 2, 0)
    final_at = jnp.where(c == 0, total - 1, 2 * (near + chips - 1 - c) + 1)

    def finish():
        def pass_on(d2):
            o = ahead(d2)
            rcopy(lz, lg.at[h, o], lg_send.at[d2], lg_recv.at[h, o], sib).wait_recv()
            lg_forward(d2).start()

        each(1, chips, pass_on)

        each(1, n_cols, lambda k: rcopy(
            eb.at[(c + k) % n_cols], eb.at[(c + k) % n_cols], e_send.at[k], e_recv.at[(c + k) % n_cols], sib
        ).wait_recv())
        entries = jnp.sum(eb[...], axis=0)
        lines = []
        levels = lax.broadcasted_iota(jnp.int32, (1, ranks), 1)
        for i in range(tiles):
            er, ei = entries[2 * i:2 * i + 1], entries[2 * i + 1:2 * i + 2]
            keep = (levels < RANK_STEP * rank_ref[i]).astype(jnp.float32)
            mag = jnp.maximum(er * er + ei * ei, 1.0)
            lines.append(keep * er / mag)
            lines.append(-keep * ei / mag)
        lines.append(jnp.zeros((128 - 2 * tiles, ranks), jnp.float32))
        turned = jnp.concatenate(lines, axis=0).T
        for i in range(tiles):
            fr, fi = turned[:, 2 * i:2 * i + 1], turned[:, 2 * i + 1:2 * i + 2]
            lr, li = i * ranks, half + i * ranks
            vr, vi = [], []
            for hh in range(2):
                for s in range(nsub):
                    vr.append(ps[2 * c + hh, s, lr:lr + ranks, :])
                    vi.append(ps[2 * c + hh, s, li:li + ranks, :])
            vr, vi = jnp.concatenate(vr, axis=1), jnp.concatenate(vi, axis=1)
            wr = vr * fr - vi * fi
            wi = vr * fi + vi * fr
            panel_ref[i, 0] = wr
            panel_ref[i, 1] = wi
            a, b = split(wr)
            ch[lr:lr + ranks, :] = a
            cl[lr:lr + ranks, :] = b
            a, b = split(wi)
            ch[li:li + ranks, :] = a
            cl[li:li + ranks, :] = b

        pltpu.make_async_copy(lz, lg.at[h, q], lg_loc.at[0]).wait()
        each(0, chips, lambda o: rcopy(
            lz, lg.at[1 - h, o], lg_sib.at[0], lg_recv.at[1 - h, o], sib
        ).wait_recv())

        def core(k0, carry):
            k = jnp.where(c == 0, n_cols - 1 - k0, (k0 + 1) % n_cols)
            j = (c + k) % n_cols
            lr = lg[0, :, j].reshape(wc, lz.shape[2])
            li = lg[1, :, j].reshape(wc, lz.shape[2])
            rank2 = lz.shape[2]
            uh, ul = split(jnp.concatenate([lr, li], axis=1))
            prod = dot3(ch[...], cl[...], uh, ul)
            real = prod[:half, :rank2] - prod[half:, rank2:]
            imag = prod[:half, rank2:] + prod[half:, :rank2]
            for i in range(tiles):
                ks[k, i, 0] = real[i * ranks:(i + 1) * ranks]
                ks[k, i, 1] = imag[i * ranks:(i + 1) * ranks]

            @pl.when(k > 0)
            def _():
                k_out(k).start()

            return carry

        lax.fori_loop(0, n_cols, core, 0)

    def unit(u, carry):
        slot = u // 2
        t = jnp.where(slot < near, ahead(slot % chips), jnp.maximum(near + chips - 1 - slot, 0))
        s = jnp.where(slot < near, slot // chips, jnp.where(slot < near + chips, nsub - 1, slot - near - chips))
        live = jnp.logical_and(t >= c, jnp.logical_or(slot >= near, t > 0))
        e = u % 2
        b = t * 2 + (h + e) % 2

        @pl.when(u == spread_at)
        def _():
            lz_own.wait()
            each(1, n_cols, lambda k: rcopy(
                lz.at[(c + k) % n_cols], lz.at[(c + k) % n_cols], lz_send.at[k], lz_recv.at[(c + k) % n_cols], sib
            ).wait_recv())
            lg_side().start()
            pltpu.make_async_copy(lz, lg.at[h, q], lg_loc.at[0]).start()
            each(1, chips, lambda d2: lg_out(d2).start())

            @pl.when(jnp.logical_and(q == 0, q >= c))
            def _():
                for s2 in range(nsub):
                    each(1, chips, lambda d2: u_out(d2, s2).start())

        @pl.when(live)
        def _():
            @pl.when(jnp.logical_or(t != q, e > 0))
            def _():
                u_forward(t, s, b).wait_recv()

            @pl.when(jnp.logical_and(t != q, e == 0))
            def _():
                u_forward(t, s, b).start()

            ur, ui = us[b, s, 0], us[b, s, 1]
            uh, ul = split(jnp.concatenate([ur, ui], axis=1))
            prod = dot3(xh[...], xl[...], uh, ul)
            fin[0:half] = prod[:half, :sw] - prod[half:, sw:]
            fin[half:2 * half] = prod[:half, sw:] + prod[half:, :sw]

            @pl.when(c > 0)
            def _():
                rcopy(ps.at[b, s], pr.at[b, s], p_send.at[b, s], p_recv.at[b, s], sib).wait_recv()
                ps[b, s] = fin[...] + pr[b, s]

            @pl.when(c == 0)
            def _():
                ps[b, s] = fin[...]

            @pl.when(t > c)
            def _():
                p_up(b, s).start()

        @pl.when(u == final_at)
        def _():
            finish()

        return carry

    lax.fori_loop(0, total, unit, 0)
    cores_ref[:, 0] = ks[0]

    def gather(k):
        o = (c + k) % n_cols
        rcopy(ks.at[k], kr.at[o], k_send.at[k], k_recv.at[o], sib).wait_recv()
        cores_ref[:, 0] = cores_ref[:, 0] + kr[o]

    each(1, n_cols, gather)

    @pl.when(q >= c)
    def _():
        for s in range(nsub):
            u_side(s).wait_send()

        def left(d):
            for s in range(nsub):
                u_out(d, s).wait_send()

        each(1, chips, left)

    def rest(d):
        t = ahead(d)

        @pl.when(jnp.logical_and(t >= c, d > 0))
        def _():
            for s in range(nsub):
                u_forward(t, s, t * 2 + h).wait_send()

        @pl.when(t > c)
        def _():
            for s in range(nsub):
                for e in range(2):
                    p_up(t * 2 + e, s).wait_send()

        @pl.when(d > 0)
        def _():
            lg_out(d).wait_send()
            lg_forward(d).wait_send()

    each(0, chips, rest)
    lg_side().wait_send()

    def tail(k):
        lz_out(k).wait_send()
        k_out(k).wait_send()
        e_out(k).wait_send()

    each(1, n_cols, tail)


def stacked(x, uh, ul):
    rows = x.shape[0] // 2
    high = jnp.dot(x, uh, preferred_element_type=jnp.float32)
    low = jnp.dot(x[:rows], ul, preferred_element_type=jnp.float32)
    return high[:rows] + (high[rows:] + low)


def paired_kernel(
    n_rows, n_cols,
    row_ref, u_ref, up_ref, col_ref, piv_ref, rank_ref,
    panel_ref, cores_ref,
    rows, cols, in_sem, xs, x0, cs, us, uc, lc, stg, ps, pr, pq, pin, lg, ks, ku, kd, eb,
    u_loc, nat_x, nat_y, nat_fwd, full1, near1, half1,
    lift, sc_send, sc_recv, full0, half0, lift_x, lift_y, lift_fx, lift_fy,
    side_send, side_recv, x_send, x_recv, p_send, p_recv, q_send, q_recv,
    l_loc, l_send, l_recv, g_send, g_recv, l_side, l_got,
    k_send, ku_recv, k_recv, e_send, e_recv,
):
    r, c = lax.axis_index("row"), lax.axis_index("col")
    chips = n_rows // 2
    nx = math.isqrt(chips)
    q, h = r // 2, r % 2
    qy, qx = q // nx, q % nx
    xn, yn, dn = qy * nx + 1 - qx, (1 - qy) * nx + qx, (1 - qy) * nx + 1 - qx
    tiles, _, ranks, wc = row_ref.shape
    nsub, sw = us.shape[1], us.shape[5]
    wq = wc // chips
    rank2 = lg.shape[3]
    width = n_cols - 2
    sib = (q * 2 + 1 - h, c)
    to_x, to_y = (xn * 2 + h, c), (yn * 2 + h, c)
    stages = 2 * nsub

    def ahead(d):
        return ((qy + d // nx) % nx) * nx + (qx + d % nx) % nx

    def rcopy(src, dst, ssem, rsem, dev):
        return pltpu.make_async_remote_copy(
            src_ref=src, dst_ref=dst, send_sem=ssem, recv_sem=rsem, device_id=dev, device_id_type=MESH
        )

    def each(first, last, body):
        lax.fori_loop(first, last, lambda i, z: (body(i), z)[1], 0)

    def ts(i):
        t = jnp.where(c == 0, 1 - i // nsub, n_cols - 1 - i % width)
        return t, jnp.where(c == 0, i % nsub, i // width)

    def active(i):
        return ts(i)[0] >= c

    def lifted(i):
        return jnp.logical_and(c < 2, ts(i)[0] > 0)

    def ucols(s):
        return u_ref.at[:, :, pl.ds(pl.multiple_of(s * sw, sw), sw)]

    def local_u(s):
        return pltpu.make_async_copy(ucols(s), us.at[r, s, 1], u_loc.at[s])

    def nat_out(s):
        return rcopy(ucols(s), us.at[r, s, 1], nat_x.at[s], full1.at[q, s], to_x)

    def nat_near(s, k):
        rows = slice(k * (wc // 2), (k + 1) * (wc // 2))
        src = u_ref.at[:, rows, pl.ds(pl.multiple_of(s * sw, sw), sw)]
        return rcopy(src, us.at[r, s, 1, :, rows, :], nat_y.at[s, k], near1.at[q, s, k], to_y)

    def nat_full(t, s):
        b = 2 * t + h
        return rcopy(us.at[b, s, 1], us.at[b, s, 1], nat_fwd.at[t, s, 0], full1.at[t, s], sib)

    def nat_half(t, s, k, got, dev=None):
        part = us.at[2 * t + h, s, 1, :, k * (wc // 2):(k + 1) * (wc // 2), :]
        return rcopy(part, part, nat_fwd.at[t, s, k], got.at[t, s, k], dev or to_x)

    def piece(b, s, g):
        return us.at[b, s, 0, :, pl.ds(pl.multiple_of(g * wq, wq), wq), :]

    def upiece(s, g):
        rows = pl.ds(pl.multiple_of(g * wq, wq), wq)
        return u_ref.at[:, rows, pl.ds(pl.multiple_of(s * sw, sw), sw)]

    def scatter(s, g):
        slot = stg.at[q % width, s]
        return rcopy(upiece(s, g), slot, sc_send.at[s, g], sc_recv.at[q % width, s], (g * 2 + h, c))

    def raised(t, s, src):
        return rcopy(src, piece(2 * t + h, s, q), lift.at[s, t], full0.at[t, s, q], (r, 1 - c))

    def lift_full(t, s, g, sem, dev):
        p = piece(2 * t + h, s, g)
        return rcopy(p, p, sem.at[t, s], full0.at[t, s, g], dev)

    def lift_half(t, s, g, k, sem, dev):
        rows = pl.ds(pl.multiple_of(g * wq + k * (wq // 2), wq // 2), wq // 2)
        p = us.at[2 * t + h, s, 0, :, rows, :]
        return rcopy(p, p, sem.at[t, s], half0.at[t, s, k], dev)

    def side(t, s, kk, b):
        return rcopy(us.at[b, s, kk], us.at[b, s, kk], side_send.at[t, s, kk], side_recv.at[t, s, kk], sib)

    def x_swap(m, p):
        return rcopy(row_ref.at[m, p], x0.at[m, p], x_send.at[m, p], x_recv.at[m, p], (r, 1 - c))

    def p_up(b, s, m):
        return rcopy(ps.at[b, s, m], pr.at[b, s, m], p_send.at[b, s, m], p_recv.at[b, s, m], (r, c + 1))

    def l_down(o):
        rows = pl.ds(pl.multiple_of(o * wc, wc), wc)
        return rcopy(up_ref.at[0, h, rows, :], lg.at[h, c], l_send.at[o], l_recv.at[c], (r, o))

    def l_part(j, g):
        return lg.at[h, j, pl.ds(pl.multiple_of(g * wq, wq), wq), :]

    def l_up(o):
        rows = pl.ds(pl.multiple_of(o * wc + q * wq, wq), wq)
        return rcopy(up_ref.at[0, h, rows, :], l_part(c, q), l_send.at[o], l_recv.at[c], (r, o))

    def g_out(j, d):
        return rcopy(l_part(j, q), l_part(j, q), g_send.at[j, d], g_recv.at[j, q], (ahead(d) * 2 + h, c))

    def l_sib(j, comp):
        return rcopy(lg.at[comp, j], lg.at[comp, j], l_side.at[j], l_got.at[j], sib)

    def l_own():
        rows = pl.ds(pl.multiple_of(c * wc, wc), wc)
        return pltpu.make_async_copy(up_ref.at[0, :, rows, :], lg.at[:, c], l_loc.at[0])

    def others(body):
        each(1, n_cols, lambda k: body((c + k) % n_cols))

    def q_up(m):
        return rcopy(pq.at[m], pin.at[m], q_send.at[m], q_recv.at[m], (r, 1))

    def k_out(j, m):
        return rcopy(ks.at[j, m], kd.at[c, m], k_send.at[j, m], k_recv.at[c, m], (r, j))

    def k_next(j, m):
        to = (r, jnp.where(c == 0, 1, n_cols - 2))
        return rcopy(ks.at[j, m], ku.at[j, m], k_send.at[j, m], ku_recv.at[j, m], to)

    def join(j, m):
        k_next(j, m).wait_recv()
        ks[j, m] = ks[j, m] + ku[j, m]

        @pl.when(j != c)
        def _():
            k_out(j, m).start()

    def e_out(k):
        return rcopy(eb.at[c], eb.at[c], e_send.at[k], e_recv.at[c], (r, (c + k) % n_cols))

    row_in = pltpu.make_async_copy(row_ref, rows, in_sem.at[0])
    col_in = pltpu.make_async_copy(col_ref, cols, in_sem.at[1])
    col_in.start()
    row_in.start()
    l_own().start()
    barrier = pltpu.get_barrier_semaphore()

    def signal(dev):
        pl.semaphore_signal(barrier, inc=1, device_id=dev, device_id_type=MESH)

    signal(sib)
    each(1, chips, lambda d: signal((ahead(d) * 2 + h, c)))
    each(1, n_cols, lambda k: signal((r, (c + k) % n_cols)))

    @pl.when(c < 2)
    def _():
        each(1, chips, lambda d: signal((ahead(d) * 2 + h, 1 - c)))

    pl.semaphore_wait(barrier, 1 + (chips - 1) + (n_cols - 1) + jnp.where(c < 2, chips - 1, 0))

    def native_x(i):
        t, s = ts(i)

        @pl.when(jnp.logical_and(active(i), q == t))
        def _():
            nat_out(s).start()
            local_u(s).start()

    def native_y(i):
        t, s = ts(i)

        @pl.when(jnp.logical_and(active(i), q == t))
        def _():
            for k in range(2):
                nat_near(s, k).start()

    def native_out(i):
        native_x(i)
        native_y(i)

    def lift_in(i):
        t, s = ts(i)

        @pl.when(lifted(i))
        def _():
            lift_full(t, s, q, lift_x, sib).wait_recv()
            lift_full(t, s, q, lift_x, to_x).start()
            lift_full(t, s, q, lift_y, to_y).start()

    def relay_x(i):
        t, s = ts(i)

        @pl.when(jnp.logical_and(c == 0, xn == t))
        def _():
            nat_full(t, s).wait_recv()
            nat_half(t, s, 0, half1, to_y).start()

            @pl.when(t == 0)
            def _():
                nat_half(t, s, 1, half1, to_y).start()

    def relay_native(i):
        t, s = ts(i)

        @pl.when(jnp.logical_and(active(i), yn == t))
        def _():
            nat_half(t, s, 0, near1).wait_recv()

            @pl.when(c > 0)
            def _():
                nat_half(t, s, 0, half1).start()

            nat_half(t, s, 1, near1).wait_recv()

            @pl.when(jnp.logical_or(c > 0, t > 0))
            def _():
                nat_half(t, s, 1, half1).start()

        @pl.when(jnp.asarray(i) < width)
        def _():
            relay_x(i)

    def relay_lift(i):
        t, s = ts(i)

        @pl.when(lifted(i))
        def _():
            lift_full(t, s, xn, lift_x, sib).wait_recv()
            lift_half(t, s, xn, 0, lift_fy, to_y).start()
            lift_full(t, s, yn, lift_x, sib).wait_recv()
            lift_half(t, s, yn, 1, lift_fx, to_x).start()

    def collect(i):
        t, s = ts(i)

        @pl.when(active(i))
        def _():
            @pl.when(dn == t)
            def _():
                for k in range(2):
                    nat_half(t, s, k, half1).wait_recv()

            @pl.when(q == t)
            def _():
                local_u(s).wait()

            @pl.when(jnp.logical_and(c > 0, xn == t))
            def _():
                nat_full(t, s).wait_recv()

            side(t, s, 1, 2 * t + h).start()

        @pl.when(lifted(i))
        def _():
            lift_half(t, s, dn, 0, lift_fy, sib).wait_recv()
            lift_half(t, s, dn, 1, lift_fx, sib).wait_recv()
            side(t, s, 0, 2 * t + h).start()

    source = jnp.where(c == 0, q > 1, jnp.logical_and(c == 1, q == 1))

    def scatters(s):
        @pl.when(source)
        def _():
            each(1, chips, lambda d: scatter(s, ahead(d)).start())

    for s in range(nsub):
        scatters(s)

    each(0, stages, lambda i: pl.when(jnp.logical_or(c > 1, i < width))(lambda: native_out(i)))

    def climb(t, s):
        @pl.when(q == t)
        def _():
            raised(t, s, upiece(s, q)).start()

        @pl.when(q != t)
        def _():
            rcopy(stg.at[t % width, s], stg.at[t % width, s], lift.at[s, t], sc_recv.at[t % width, s], sib).wait_recv()
            raised(t, s, stg.at[t % width, s]).start()

    @pl.when(c == 0)
    def _():
        for s in range(nsub):
            for t in range(n_cols - 1, 1, -1):
                climb(t, s)
            for p in range(2):
                x_swap(s, p).start()

    @pl.when(c == 1)
    def _():
        for s in range(nsub):
            climb(1, s)
        for m in range(tiles):
            for p in range(2):
                x_swap(m, p).start()

    each(c + 1, n_cols, lambda o: l_up(o).start())

    @pl.when(c == 1)
    def _():
        l_down(0).start()

    col_in.wait()
    pos = c * wc + lax.broadcasted_iota(jnp.int32, (wc, ranks), 0)
    parts = []
    for i in range(tiles):
        hit = pos == piv_ref[i:i + 1, :]
        for p in range(2):
            parts.append(jnp.sum(jnp.where(hit, cols[i, p], 0.0), axis=0, keepdims=True))
    parts.append(jnp.zeros((eb.shape[1] - 2 * tiles, ranks), jnp.float32))
    eb[c] = jnp.concatenate(parts, axis=0)
    each(1, n_cols, lambda k: e_out(k).start())

    def spread(j):
        rcopy(l_part(j, q), l_part(j, q), l_send.at[c], l_recv.at[j], sib).wait_recv()
        each(1, chips, lambda d: g_out(j, d).start())

    @pl.when(c < 2)
    def _():
        for i in range(width):
            lift_in(i)

            @pl.when(c == 0)
            def _():
                native_x(width + i)

        relay_native(0)

        @pl.when(c == 1)
        def _():
            relay_lift(0)

        @pl.when(c == 0)
        def _():
            relay_lift(0)
            relay_lift(1)
            relay_native(1)
            for i in range(width, stages):
                native_y(i)
            for i in range(width, stages):
                relay_x(i)

        @pl.when(c == 1)
        def _():
            for i in range(1, width):
                relay_native(i)
                relay_lift(i)
            for i in range(width, stages):
                native_out(i)

        for i in range(width):
            collect(i)

    @pl.when(c > 1)
    def _():
        each(0, stages, relay_native)
        each(0, c, lambda o: l_down(o).start())
        each(0, stages, collect)
        each(0, c, spread)


    row_in.wait()
    for m in range(tiles):
        for p in range(2):
            a, b = split(rows[m, p])
            xs[1, m, p * ranks:(p + 1) * ranks, :] = a
            xs[1, m, (p + 2) * ranks:(p + 3) * ranks, :] = b

    def gather():
        l_own().wait()

        def low(j):
            each(1, chips, lambda d: rcopy(
                l_part(j, ahead(d)), l_part(j, ahead(d)), g_send.at[j, d], g_recv.at[j, ahead(d)], sib
            ).wait_recv())
            l_sib(j, h).start()

        def high(j):
            rcopy(lg.at[h, j], lg.at[h, j], l_send.at[c], l_recv.at[j], sib).wait_recv()
            l_sib(j, h).start()

        each(0, c, low)
        each(c + 1, n_cols, high)

    def gathered():
        each(0, c, lambda j: l_sib(j, 1 - h).wait_recv())
        each(c + 1, n_cols, lambda j: l_sib(j, 1 - h).wait_recv())

    def entries_in():
        each(1, n_cols, lambda k: rcopy(
            eb.at[(c + k) % n_cols], eb.at[(c + k) % n_cols], e_send.at[k], e_recv.at[(c + k) % n_cols], sib
        ).wait_recv())

    def scaled(t, m):
        entries = jnp.sum(eb[...], axis=0)
        lines = []
        levels = lax.broadcasted_iota(jnp.int32, (1, ranks), 1)
        for i in range(tiles):
            er, ei = entries[2 * i:2 * i + 1], entries[2 * i + 1:2 * i + 2]
            keep = (levels < RANK_STEP * rank_ref[i]).astype(jnp.float32)
            mag = jnp.maximum(er * er + ei * ei, 1.0)
            lines.append(keep * er / mag)
            lines.append(-keep * ei / mag)
        factor_r, factor_i = lines[0], lines[1]
        for i in range(1, tiles):
            factor_r = jnp.where(m == i, lines[2 * i], factor_r)
            factor_i = jnp.where(m == i, lines[2 * i + 1], factor_i)
        pad = jnp.zeros((126, ranks), jnp.float32)
        turned = jnp.concatenate([factor_r, factor_i, pad], axis=0).T
        fr, fi = turned[:, 0:1], turned[:, 1:2]
        vr, vi = [], []
        for hh in range(2):
            for s in range(nsub):
                vr.append(ps[2 * t + hh, s, m, 0])
                vi.append(ps[2 * t + hh, s, m, 1])
        vr, vi = jnp.concatenate(vr, axis=1), jnp.concatenate(vi, axis=1)
        wr = vr * fr - vi * fi
        wi = vr * fi + vi * fr
        return wr, wi

    def finish_next(m):
        @pl.when(m == 0)
        def _():
            entries_in()

        wr, wi = scaled(c + 1, m)
        pq[m, 0] = wr
        pq[m, 1] = wi
        q_up(m).start()

    def finish(m):
        @pl.when(m == 0)
        def _():
            gathered()

            @pl.when(c > 0)
            def _():
                entries_in()

        @pl.when(c == 1)
        def _():
            q_up(m).wait_recv()
            panel_ref[m] = pin[m]

        @pl.when(c != 1)
        def _():
            wr, wi = scaled(c, m)
            panel_ref[m, 0] = wr
            panel_ref[m, 1] = wi

        for p in range(2):
            a, b = split(panel_ref[m, p])
            cs[p * ranks:(p + 1) * ranks, :] = a
            cs[(p + 2) * ranks:(p + 3) * ranks, :] = b

        def core(j, carry):
            @pl.when(m == 0)
            def _():
                for p in range(2):
                    uh, ul = split(lg[p, j])
                    lc[j, 0, :, p * rank2:(p + 1) * rank2] = uh
                    lc[j, 1, :, p * rank2:(p + 1) * rank2] = ul

            prod = stacked(cs[...], lc[j, 0], lc[j, 1])
            ks[j, m, 0] = prod[:ranks, :rank2] - prod[ranks:, rank2:]
            ks[j, m, 1] = prod[:ranks, rank2:] + prod[ranks:, :rank2]

            @pl.when(jnp.logical_and(c == 1, j > 0))
            def _():
                join(j, m)

            ends = jnp.logical_or(c == 0, c == n_cols - 1)

            @pl.when(jnp.logical_and(ends, j != c))
            def _():
                k_next(j, m).start()

            @pl.when(jnp.logical_or(jnp.logical_and(c == 1, j == 0), jnp.logical_and(c == n_cols - 2, j > c)))
            def _():
                k_out(j, m).start()

            return carry

        lax.fori_loop(0, n_cols, core, 0)

    half = width * tiles
    total = 2 * half
    final0 = jnp.where(c == 0, half + nsub - 1, (nsub - 1) * half + n_cols - 1 - c)
    final0 = jnp.where(c == 1, total, final0)

    def unit(u, carry):
        i = u // half * width + u % width
        m = u // width % tiles
        t, s = ts(i)

        @pl.when(jnp.logical_and(active(i), u < total))
        def _():
            @pl.when(jnp.logical_and(c < 2, jnp.logical_and(u < half, u % width == 0)))
            def _():
                for p in range(2):
                    x_swap(m, p).wait_recv()
                    a, b = split(x0[m, p])
                    xs[0, m, p * ranks:(p + 1) * ranks, :] = a
                    xs[0, m, (p + 2) * ranks:(p + 3) * ranks, :] = b

            for e in range(2):
                b = 2 * t + (h + e) % 2

                if e == 1:
                    @pl.when(m == 0)
                    def _():
                        side(t, s, 1, b).wait_recv()

                        @pl.when(lifted(i))
                        def _():
                            side(t, s, 0, b).wait_recv()

                def product(kk):
                    @pl.when(m == 0)
                    def _():
                        for p in range(2):
                            uh, ul = split(us[b, s, kk, p])
                            uc[i, e, kk, 0, :, p * sw:(p + 1) * sw] = uh
                            uc[i, e, kk, 1, :, p * sw:(p + 1) * sw] = ul

                    prod = stacked(xs[kk, m], uc[i, e, kk, 0], uc[i, e, kk, 1])
                    real = prod[:ranks, :sw] - prod[ranks:, sw:]
                    imag = prod[:ranks, sw:] + prod[ranks:, :sw]
                    return real, imag

                real, imag = product(1)

                @pl.when(lifted(i))
                def _():
                    real0, imag0 = product(0)
                    ps[b, s, m, 0] = real + real0
                    ps[b, s, m, 1] = imag + imag0

                @pl.when(jnp.logical_and(c == 0, t == 0))
                def _():
                    ps[b, s, m, 0] = real
                    ps[b, s, m, 1] = imag

                @pl.when(c > 1)
                def _():
                    p_up(b, s, m).wait_recv()
                    ps[b, s, m, 0] = real + pr[b, s, m, 0]
                    ps[b, s, m, 1] = imag + pr[b, s, m, 1]

                @pl.when(jnp.logical_and(t > c, c > 0))
                def _():
                    p_up(b, s, m).start()

        @pl.when(jnp.logical_and(c == 0, jnp.logical_and(u < half, u % width == width - 1)))
        def _():
            finish_next(m)

        @pl.when(jnp.logical_or(u == final0, u == final0 + width))
        def _():
            finish(m)

        @pl.when(jnp.logical_and(c == 0, jnp.logical_and(u >= width, u < half)))
        def _():
            relay_native(u)

        @pl.when(jnp.logical_and(c == n_cols - 2, u >= total - 2))
        def _():
            each(0, c + 1, lambda j: join(j, u - total + 2))

        @pl.when(u == jnp.where(c == 0, half, jnp.where(c == 1, total - 1, width - 1)))
        def _():
            gather()

        @pl.when(jnp.logical_and(c == 1, u == 0))
        def _():
            for i in range(width, stages):
                lift_in(i)

        @pl.when(jnp.logical_and(c == 1, u == width - 1))
        def _():
            for i in range(width, stages):
                relay_native(i)
                relay_lift(i)

        @pl.when(jnp.logical_and(c < 2, u == half - 1))
        def _():
            for i in range(width, stages):
                collect(i)
            each(0, jnp.where(c == 1, 1, 0), spread)

        return carry

    lax.fori_loop(0, jnp.where(c == 1, total + 2 * width - 1, total), unit, 0)

    @pl.when(c < 2)
    def _():
        for m in range(tiles):
            for p in range(2):
                x_swap(m, p).wait_send()
        for s in range(nsub):
            for t in range(1, n_cols):
                @pl.when(c == (0 if t > 1 else 1))
                def _():
                    raised(t, s, stg.at[t % width, s]).wait_send()

    @pl.when(c == 0)
    def _():
        for m in range(tiles):
            q_up(m).wait_send()

    @pl.when(source)
    def _():
        for s in range(nsub):
            each(1, chips, lambda d: scatter(s, ahead(d)).wait_send())

    def drain(i):
        t, s = ts(i)

        @pl.when(active(i))
        def _():
            @pl.when(q == t)
            def _():
                nat_out(s).wait_send()
                for k in range(2):
                    nat_near(s, k).wait_send()

            @pl.when(jnp.where(jnp.logical_and(c == 0, t == 0), xn == t, yn == t))
            def _():
                nat_half(t, s, 1, half1).wait_send()

            @pl.when(jnp.where(c == 0, xn == t, yn == t))
            def _():
                nat_half(t, s, 0, half1).wait_send()

            side(t, s, 1, 2 * t + h).wait_send()

            @pl.when(lifted(i))
            def _():
                lift_full(t, s, q, lift_x, sib).wait_send()
                lift_full(t, s, q, lift_y, sib).wait_send()
                lift_half(t, s, xn, 0, lift_fy, sib).wait_send()
                lift_half(t, s, yn, 1, lift_fx, sib).wait_send()
                side(t, s, 0, 2 * t + h).wait_send()

            @pl.when(jnp.logical_and(t > c, c > 0))
            def _():
                for m in range(tiles):
                    for e in range(2):
                        p_up(2 * t + e, s, m).wait_send()

    each(0, stages, drain)

    def tail_l(j):
        each(1, chips, lambda d: g_out(j, d).wait_send())
        l_down(j).wait_send()

    each(0, c, tail_l)
    each(c + 1, n_cols, lambda o: l_up(o).wait_send())

    def tail_k(j):
        l_sib(j, h).wait_send()
        for m in range(tiles):
            k_out(j, m).wait_send()

    others(tail_k)
    each(1, n_cols, lambda k: e_out(k).wait_send())

    for m in range(tiles):
        cores_ref[m, 0] = ks[c, m]

        def add(o):
            @pl.when(jnp.logical_and(o > 0, o < n_cols - 1))
            def _():
                rcopy(ks.at[c, m], kd.at[o, m], k_send.at[c, m], k_recv.at[o, m], sib).wait_recv()
                cores_ref[m, 0] = cores_ref[m, 0] + kd[o, m]

        others(add)


def paired(n_rows, n_cols, col_samples, row_samples, pivot_rows, rank_blocks, upper_inverse, upanel_left):
    tiles, _, ranks, wc = row_samples.shape
    wr = upper_inverse.shape[2]
    left_ranks = upanel_left.shape[3]
    chips = n_rows // 2
    nsub = wr // 128
    sw = wr // nsub
    f32, bf16 = jnp.float32, jnp.bfloat16
    dma = pltpu.SemaphoreType.DMA
    vmem = pl.BlockSpec(memory_space=pltpu.VMEM)
    hbm = pl.BlockSpec(memory_space=pl.ANY)
    sums = pltpu.VMEM((n_rows, nsub, tiles, 2, ranks, sw), f32)
    return pl.pallas_call(
        functools.partial(paired_kernel, n_rows, n_cols),
        out_shape=(
            jax.ShapeDtypeStruct((tiles, 2, ranks, wc), f32),
            jax.ShapeDtypeStruct((tiles, 1, 2, ranks, left_ranks), f32),
        ),
        in_specs=[hbm, hbm, hbm, hbm, vmem, pl.BlockSpec(memory_space=pltpu.SMEM)],
        out_specs=(vmem, vmem),
        scratch_shapes=[
            pltpu.VMEM(row_samples.shape, f32),
            pltpu.VMEM(col_samples.shape, f32),
            dma((2,)),
            pltpu.VMEM((2, tiles, 4 * ranks, wc), bf16),
            pltpu.VMEM((tiles, 2, ranks, wc), f32),
            pltpu.VMEM((4 * ranks, wc), bf16),
            pltpu.VMEM((n_rows, nsub, 2, 2, wc, sw), f32),
            pltpu.VMEM((2 * nsub, 2, 2, 2, wc, 2 * sw), bf16),
            pltpu.VMEM((n_cols, 2, wc, 2 * left_ranks), bf16),
            pltpu.VMEM((n_cols - 2, nsub, 2, wc // chips, sw), f32),
            sums,
            sums,
            pltpu.VMEM((tiles, 2, ranks, wc), f32),
            pltpu.VMEM((tiles, 2, ranks, wc), f32),
            pltpu.VMEM((2, n_cols, wc, left_ranks), f32),
            pltpu.VMEM((n_cols, tiles, 2, ranks, left_ranks), f32),
            pltpu.VMEM((n_cols, tiles, 2, ranks, left_ranks), f32),
            pltpu.VMEM((n_cols, tiles, 2, ranks, left_ranks), f32),
            pltpu.VMEM((n_cols, -(-2 * tiles // 8) * 8, ranks), f32),
            dma((nsub,)), dma((nsub,)), dma((nsub, 2)), dma((n_cols, nsub, 2)), dma((n_cols, nsub)),
            dma((n_cols, nsub, 2)), dma((n_cols, nsub, 2)),
            dma((nsub, n_cols)), dma((nsub, chips)), dma((n_cols - 2, nsub)),
            dma((n_cols, nsub, chips)), dma((n_cols, nsub, 2)),
            dma((n_cols, nsub)), dma((n_cols, nsub)), dma((n_cols, nsub)), dma((n_cols, nsub)),
            dma((n_cols, nsub, 2)), dma((n_cols, nsub, 2)), dma((tiles, 2)), dma((tiles, 2)),
            dma((n_rows, nsub, tiles)), dma((n_rows, nsub, tiles)), dma((tiles,)), dma((tiles,)),
            dma((1,)), dma((n_cols,)), dma((n_cols,)), dma((n_cols, chips)), dma((n_cols, chips)),
            dma((n_cols,)), dma((n_cols,)),
            dma((n_cols, tiles)), dma((n_cols, tiles)), dma((n_cols, tiles)), dma((n_cols,)), dma((n_cols,)),
        ],
        compiler_params=pltpu.CompilerParams(
            collective_id=0, has_side_effects=True, vmem_limit_bytes=60 * 1024 * 1024
        ),
    )(row_samples, upper_inverse, upanel_left, col_samples, pivot_rows, rank_blocks)


def on_device(n_rows, n_cols, col_samples, row_samples, pivot_rows, rank_blocks, upper_inverse, upanel_left):
    tiles, _, ranks, wc = row_samples.shape
    wr = upper_inverse.shape[2]
    left_ranks = upanel_left.shape[3]
    chips = n_rows // 2
    if chips != n_cols or wc != 2 * wr:
        raise ValueError("unsupported mesh")
    if chips == 4 and wr == 128 * (n_cols - 2):
        return paired(
            n_rows, n_cols, col_samples, row_samples, pivot_rows, rank_blocks, upper_inverse, upanel_left
        )
    nsub = max(wr // 128, 1)
    sw = wr // nsub
    wq = wc // chips
    m = 2 * tiles * ranks
    f32, bf16 = jnp.float32, jnp.bfloat16
    dma = pltpu.SemaphoreType.DMA
    vmem = pl.BlockSpec(memory_space=pltpu.VMEM)
    hbm = pl.BlockSpec(memory_space=pl.ANY)
    return pl.pallas_call(
        functools.partial(kernel, n_rows, n_cols),
        out_shape=(
            jax.ShapeDtypeStruct((tiles, 2, ranks, wc), f32),
            jax.ShapeDtypeStruct((tiles, 1, 2, ranks, left_ranks), f32),
        ),
        in_specs=[vmem, hbm, hbm, vmem, vmem, pl.BlockSpec(memory_space=pltpu.SMEM)],
        out_specs=(vmem, vmem),
        scratch_shapes=[
            pltpu.VMEM((m, wc), bf16),
            pltpu.VMEM((m, wc), bf16),
            pltpu.VMEM((m, wc), bf16),
            pltpu.VMEM((m, wc), bf16),
            pltpu.VMEM((n_rows, nsub, 2, wc, sw), f32),
            pltpu.VMEM((n_rows, nsub, m, sw), f32),
            pltpu.VMEM((n_rows, nsub, m, sw), f32),
            pltpu.VMEM((m, sw), f32),
            pltpu.VMEM((n_cols, wq, left_ranks), f32),
            pltpu.VMEM((2, chips, n_cols, wq, left_ranks), f32),
            pltpu.VMEM((n_cols, tiles, 2, ranks, left_ranks), f32),
            pltpu.VMEM((n_cols, tiles, 2, ranks, left_ranks), f32),
            pltpu.VMEM((n_cols, -(-2 * tiles // 8) * 8, ranks), f32),
            dma((nsub,)), dma((chips, nsub)), dma((nsub,)), dma((chips, nsub)), dma((n_rows, nsub)),
            dma((n_rows, nsub)), dma((n_rows, nsub)),
            dma((1,)), dma((n_cols,)), dma((n_cols,)), dma((1,)), dma((chips,)), dma((1,)), dma((chips,)),
            dma((2, chips)),
            dma((n_cols,)), dma((n_cols,)), dma((n_cols,)), dma((n_cols,)),
        ],
        compiler_params=pltpu.CompilerParams(
            collective_id=0, has_side_effects=True, vmem_limit_bytes=56 * 1024 * 1024
        ),
    )(row_samples, upper_inverse, upanel_left, col_samples, pivot_rows, rank_blocks)


def solution(mesh):
    in_specs = (
        P("row", None, "col", None),
        P("row", None, None, "col"),
        P("row", None),
        P("row"),
        P(None, "col", "row"),
        P("col", None, None, None),
    )
    out_specs = (P("row", None, None, "col"), P("row", "col", None, None, None))
    body = functools.partial(on_device, mesh.shape["row"], mesh.shape["col"])
    return jax.shard_map(body, mesh=mesh, in_specs=in_specs, out_specs=out_specs, check_vma=False)
```

```python
import functools
import math

import jax
import jax.numpy as jnp
from jax import lax
from jax.experimental import pallas as pl
from jax.experimental.pallas import tpu as pltpu
from jax.sharding import PartitionSpec as P

RANK_STEP = 16
MESH = pl.DeviceIdType.MESH


def split(x):
    high = x.astype(jnp.bfloat16)
    low = (x - high.astype(jnp.float32)).astype(jnp.bfloat16)
    return high, low


def dot3(xh, xl, uh, ul):
    def single(a, b):
        return jnp.dot(a, b, preferred_element_type=jnp.float32)

    return single(xh, uh) + (single(xh, ul) + single(xl, uh))


def kernel(
    n_rows, n_cols,
    row_ref, u_ref, up_ref, col_ref, piv_ref, rank_ref,
    panel_ref, cores_ref,
    xh, xl, ch, cl, us, ps, pr, fin, lz, lg, ks, kr, eb,
    u_loc, u_send, u_sib, u_fwd, u_recv,
    p_send, p_recv,
    lz_loc, lz_send, lz_recv, lg_loc, lg_send, lg_sib, lg_fwd, lg_recv,
    k_send, k_recv, e_send, e_recv,
):
    r, c = lax.axis_index("row"), lax.axis_index("col")
    chips = n_rows // 2
    nx = math.isqrt(chips)
    ny = chips // nx
    q, h = r // 2, r % 2
    qy, qx = q // nx, q % nx
    tiles, _, ranks, wc = row_ref.shape
    nsub, sw = us.shape[1], us.shape[4]
    wq = lz.shape[1]
    half = tiles * ranks
    sib = (q * 2 + 1 - h, c)

    def ahead(d):
        return ((qy + d // nx) % ny) * nx + (qx + d % nx) % nx

    def behind(d):
        return ((qy + ny - d // nx) % ny) * nx + (qx + nx - d % nx) % nx

    def rcopy(src, dst, ssem, rsem, dev):
        return pltpu.make_async_remote_copy(
            src_ref=src, dst_ref=dst, send_sem=ssem, recv_sem=rsem, device_id=dev, device_id_type=MESH
        )

    def u_out(d, s):
        return rcopy(
            u_ref.at[:, :, s * sw:(s + 1) * sw], us.at[r, s], u_send.at[d, s], u_recv.at[r, s],
            (behind(d) * 2 + h, c),
        )

    def u_side(s):
        return rcopy(u_ref.at[:, :, s * sw:(s + 1) * sw], us.at[r, s], u_sib.at[s], u_recv.at[r, s], sib)

    def u_forward(t, s, b):
        return rcopy(us.at[b, s], us.at[b, s], u_fwd.at[t, s], u_recv.at[b, s], sib)

    def p_up(b, s):
        return rcopy(ps.at[b, s], pr.at[b, s], p_send.at[b, s], p_recv.at[b, s], (r, c + 1))

    def lz_out(k):
        to = (c + k) % n_cols
        start = pl.multiple_of(to * wc + q * wq, wq)
        return rcopy(up_ref.at[0, h, pl.ds(start, wq), :], lz.at[c], lz_send.at[k], lz_recv.at[c], (r, to))

    def lg_out(d):
        return rcopy(lz, lg.at[h, q], lg_send.at[d], lg_recv.at[h, q], (behind(d) * 2 + h, c))

    def lg_side():
        return rcopy(lz, lg.at[h, q], lg_sib.at[0], lg_recv.at[h, q], sib)

    def lg_forward(d):
        b = ahead(d)
        return rcopy(lg.at[h, b], lg.at[h, b], lg_fwd.at[d], lg_recv.at[h, b], sib)

    def k_out(k):
        to = (c + k) % n_cols
        return rcopy(ks.at[k], kr.at[c], k_send.at[k], k_recv.at[c], (r, to))

    def e_out(k):
        return rcopy(eb.at[c], eb.at[c], e_send.at[k], e_recv.at[c], (r, (c + k) % n_cols))

    def each(first, last, body):
        lax.fori_loop(first, last, lambda i, z: (body(i), z)[1], 0)

    own = [
        pltpu.make_async_copy(u_ref.at[:, :, s * sw:(s + 1) * sw], us.at[r, s], u_loc.at[s]) for s in range(nsub)
    ]
    for copy in own:
        copy.start()
    mine = pl.multiple_of(c * wc + q * wq, wq)
    lz_own = pltpu.make_async_copy(up_ref.at[0, h, pl.ds(mine, wq), :], lz.at[c], lz_loc.at[0])
    lz_own.start()
    barrier = pltpu.get_barrier_semaphore()

    def signal(dev):
        pl.semaphore_signal(barrier, inc=1, device_id=dev, device_id_type=MESH)

    signal(sib)
    each(1, chips, lambda d: signal((behind(d) * 2 + h, c)))
    each(1, n_cols, lambda k: signal((r, (c + k) % n_cols)))
    pl.semaphore_wait(barrier, 1 + (chips - 1) + (n_cols - 1))

    @pl.when(q >= c)
    def _():
        for s in range(nsub):
            u_side(s).start()

        @pl.when(q > 0)
        def _():
            for s in range(nsub):
                each(1, chips, lambda d: u_out(d, s).start())

    each(1, n_cols, lambda k: lz_out(k).start())

    for i in range(tiles):
        for p in range(2):
            a, b = split(row_ref[i, p])
            at = pl.ds(p * half + i * ranks, ranks)
            xh[at, :] = a
            xl[at, :] = b

    pos = c * wc + lax.broadcasted_iota(jnp.int32, (wc, ranks), 0)
    parts = []
    for i in range(tiles):
        hit = pos == piv_ref[i:i + 1, :]
        for p in range(2):
            parts.append(jnp.sum(jnp.where(hit, col_ref[i, p], 0.0), axis=0, keepdims=True))
    parts.append(jnp.zeros((eb.shape[1] - 2 * tiles, ranks), jnp.float32))
    eb[c] = jnp.concatenate(parts, axis=0)
    each(1, n_cols, lambda k: e_out(k).start())
    for copy in own:
        copy.wait()

    near = chips * (nsub - 1)
    total = 2 * (near + chips + nsub - 1)
    spread_at = jnp.where(c == 0, 2, 0)
    final_at = jnp.where(c == 0, total - 1, 2 * (near + chips - 1 - c) + 1)

    def finish():
        def pass_on(d2):
            o = ahead(d2)
            rcopy(lz, lg.at[h, o], lg_send.at[d2], lg_recv.at[h, o], sib).wait_recv()
            lg_forward(d2).start()

        each(1, chips, pass_on)

        each(1, n_cols, lambda k: rcopy(
            eb.at[(c + k) % n_cols], eb.at[(c + k) % n_cols], e_send.at[k], e_recv.at[(c + k) % n_cols], sib
        ).wait_recv())
        entries = jnp.sum(eb[...], axis=0)
        lines = []
        levels = lax.broadcasted_iota(jnp.int32, (1, ranks), 1)
        for i in range(tiles):
            er, ei = entries[2 * i:2 * i + 1], entries[2 * i + 1:2 * i + 2]
            keep = (levels < RANK_STEP * rank_ref[i]).astype(jnp.float32)
            mag = jnp.maximum(er * er + ei * ei, 1.0)
            lines.append(keep * er / mag)
            lines.append(-keep * ei / mag)
        lines.append(jnp.zeros((128 - 2 * tiles, ranks), jnp.float32))
        turned = jnp.concatenate(lines, axis=0).T
        for i in range(tiles):
            fr, fi = turned[:, 2 * i:2 * i + 1], turned[:, 2 * i + 1:2 * i + 2]
            lr, li = i * ranks, half + i * ranks
            vr, vi = [], []
            for hh in range(2):
                for s in range(nsub):
                    vr.append(ps[2 * c + hh, s, lr:lr + ranks, :])
                    vi.append(ps[2 * c + hh, s, li:li + ranks, :])
            vr, vi = jnp.concatenate(vr, axis=1), jnp.concatenate(vi, axis=1)
            wr = vr * fr - vi * fi
            wi = vr * fi + vi * fr
            panel_ref[i, 0] = wr
            panel_ref[i, 1] = wi
            a, b = split(wr)
            ch[lr:lr + ranks, :] = a
            cl[lr:lr + ranks, :] = b
            a, b = split(wi)
            ch[li:li + ranks, :] = a
            cl[li:li + ranks, :] = b

        pltpu.make_async_copy(lz, lg.at[h, q], lg_loc.at[0]).wait()
        each(0, chips, lambda o: rcopy(
            lz, lg.at[1 - h, o], lg_sib.at[0], lg_recv.at[1 - h, o], sib
        ).wait_recv())

        def core(k0, carry):
            k = jnp.where(c == 0, n_cols - 1 - k0, (k0 + 1) % n_cols)
            j = (c + k) % n_cols
            lr = lg[0, :, j].reshape(wc, lz.shape[2])
            li = lg[1, :, j].reshape(wc, lz.shape[2])
            rank2 = lz.shape[2]
            uh, ul = split(jnp.concatenate([lr, li], axis=1))
            prod = dot3(ch[...], cl[...], uh, ul)
            real = prod[:half, :rank2] - prod[half:, rank2:]
            imag = prod[:half, rank2:] + prod[half:, :rank2]
            for i in range(tiles):
                ks[k, i, 0] = real[i * ranks:(i + 1) * ranks]
                ks[k, i, 1] = imag[i * ranks:(i + 1) * ranks]

            @pl.when(k > 0)
            def _():
                k_out(k).start()

            return carry

        lax.fori_loop(0, n_cols, core, 0)

    def unit(u, carry):
        slot = u // 2
        t = jnp.where(slot < near, ahead(slot % chips), jnp.maximum(near + chips - 1 - slot, 0))
        s = jnp.where(slot < near, slot // chips, jnp.where(slot < near + chips, nsub - 1, slot - near - chips))
        live = jnp.logical_and(t >= c, jnp.logical_or(slot >= near, t > 0))
        e = u % 2
        b = t * 2 + (h + e) % 2

        @pl.when(u == spread_at)
        def _():
            lz_own.wait()
            each(1, n_cols, lambda k: rcopy(
                lz.at[(c + k) % n_cols], lz.at[(c + k) % n_cols], lz_send.at[k], lz_recv.at[(c + k) % n_cols], sib
            ).wait_recv())
            lg_side().start()
            pltpu.make_async_copy(lz, lg.at[h, q], lg_loc.at[0]).start()
            each(1, chips, lambda d2: lg_out(d2).start())

            @pl.when(jnp.logical_and(q == 0, q >= c))
            def _():
                for s2 in range(nsub):
                    each(1, chips, lambda d2: u_out(d2, s2).start())

        @pl.when(live)
        def _():
            @pl.when(jnp.logical_or(t != q, e > 0))
            def _():
                u_forward(t, s, b).wait_recv()

            @pl.when(jnp.logical_and(t != q, e == 0))
            def _():
                u_forward(t, s, b).start()

            ur, ui = us[b, s, 0], us[b, s, 1]
            uh, ul = split(jnp.concatenate([ur, ui], axis=1))
            prod = dot3(xh[...], xl[...], uh, ul)
            fin[0:half] = prod[:half, :sw] - prod[half:, sw:]
            fin[half:2 * half] = prod[:half, sw:] + prod[half:, :sw]

            @pl.when(c > 0)
            def _():
                rcopy(ps.at[b, s], pr.at[b, s], p_send.at[b, s], p_recv.at[b, s], sib).wait_recv()
                ps[b, s] = fin[...] + pr[b, s]

            @pl.when(c == 0)
            def _():
                ps[b, s] = fin[...]

            @pl.when(t > c)
            def _():
                p_up(b, s).start()

        @pl.when(u == final_at)
        def _():
            finish()

        return carry

    lax.fori_loop(0, total, unit, 0)
    cores_ref[:, 0] = ks[0]

    def gather(k):
        o = (c + k) % n_cols
        rcopy(ks.at[k], kr.at[o], k_send.at[k], k_recv.at[o], sib).wait_recv()
        cores_ref[:, 0] = cores_ref[:, 0] + kr[o]

    each(1, n_cols, gather)

    @pl.when(q >= c)
    def _():
        for s in range(nsub):
            u_side(s).wait_send()

        def left(d):
            for s in range(nsub):
                u_out(d, s).wait_send()

        each(1, chips, left)

    def rest(d):
        t = ahead(d)

        @pl.when(jnp.logical_and(t >= c, d > 0))
        def _():
            for s in range(nsub):
                u_forward(t, s, t * 2 + h).wait_send()

        @pl.when(t > c)
        def _():
            for s in range(nsub):
                for e in range(2):
                    p_up(t * 2 + e, s).wait_send()

        @pl.when(d > 0)
        def _():
            lg_out(d).wait_send()
            lg_forward(d).wait_send()

    each(0, chips, rest)
    lg_side().wait_send()

    def tail(k):
        lz_out(k).wait_send()
        k_out(k).wait_send()
        e_out(k).wait_send()

    each(1, n_cols, tail)


def stacked(x, uh, ul):
    rows = x.shape[0] // 2
    high = jnp.dot(x, uh, preferred_element_type=jnp.float32)
    low = jnp.dot(x[:rows], ul, preferred_element_type=jnp.float32)
    return high[:rows] + (high[rows:] + low)


def paired_kernel(
    n_rows, n_cols,
    row_ref, u_ref, up_ref, col_ref, piv_ref, rank_ref,
    panel_ref, cores_ref,
    rows, cols, in_sem, xs, x0, cs, us, uc, lc, stg, ps, pr, pq, pin, lg, ks, ku, kd, eb,
    u_loc, nat_x, nat_y, nat_fwd, full1, near1, half1,
    lift, sc_send, sc_recv, full0, half0, lift_x, lift_y, lift_fx, lift_fy,
    side_send, side_recv, x_send, x_recv, p_send, p_recv, q_send, q_recv,
    l_loc, l_send, l_recv, g_send, g_recv, l_side, l_got,
    k_send, ku_recv, k_recv, e_send, e_recv,
):
    r, c = lax.axis_index("row"), lax.axis_index("col")
    chips = n_rows // 2
    nx = math.isqrt(chips)
    q, h = r // 2, r % 2
    qy, qx = q // nx, q % nx
    xn, yn, dn = qy * nx + 1 - qx, (1 - qy) * nx + qx, (1 - qy) * nx + 1 - qx
    tiles, _, ranks, wc = row_ref.shape
    nsub, sw = us.shape[1], us.shape[5]
    wq = wc // chips
    rank2 = lg.shape[3]
    width = n_cols - 2
    sib = (q * 2 + 1 - h, c)
    to_x, to_y = (xn * 2 + h, c), (yn * 2 + h, c)
    stages = 2 * nsub

    def ahead(d):
        return ((qy + d // nx) % nx) * nx + (qx + d % nx) % nx

    def rcopy(src, dst, ssem, rsem, dev):
        return pltpu.make_async_remote_copy(
            src_ref=src, dst_ref=dst, send_sem=ssem, recv_sem=rsem, device_id=dev, device_id_type=MESH
        )

    def each(first, last, body):
        lax.fori_loop(first, last, lambda i, z: (body(i), z)[1], 0)

    def ts(i):
        t = jnp.where(c == 0, 1 - i // nsub, n_cols - 1 - i % width)
        return t, jnp.where(c == 0, i % nsub, i // width)

    def active(i):
        return ts(i)[0] >= c

    def lifted(i):
        return jnp.logical_and(c < 2, ts(i)[0] > 0)

    def ucols(s):
        return u_ref.at[:, :, pl.ds(pl.multiple_of(s * sw, sw), sw)]

    def local_u(s):
        return pltpu.make_async_copy(ucols(s), us.at[r, s, 1], u_loc.at[s])

    def nat_out(s):
        return rcopy(ucols(s), us.at[r, s, 1], nat_x.at[s], full1.at[q, s], to_x)

    def nat_near(s, k):
        rows = slice(k * (wc // 2), (k + 1) * (wc // 2))
        src = u_ref.at[:, rows, pl.ds(pl.multiple_of(s * sw, sw), sw)]
        return rcopy(src, us.at[r, s, 1, :, rows, :], nat_y.at[s, k], near1.at[q, s, k], to_y)

    def nat_full(t, s):
        b = 2 * t + h
        return rcopy(us.at[b, s, 1], us.at[b, s, 1], nat_fwd.at[t, s, 0], full1.at[t, s], sib)

    def nat_half(t, s, k, got, dev=None):
        part = us.at[2 * t + h, s, 1, :, k * (wc // 2):(k + 1) * (wc // 2), :]
        return rcopy(part, part, nat_fwd.at[t, s, k], got.at[t, s, k], dev or to_x)

    def piece(b, s, g):
        return us.at[b, s, 0, :, pl.ds(pl.multiple_of(g * wq, wq), wq), :]

    def upiece(s, g):
        rows = pl.ds(pl.multiple_of(g * wq, wq), wq)
        return u_ref.at[:, rows, pl.ds(pl.multiple_of(s * sw, sw), sw)]

    def scatter(s, g):
        slot = stg.at[q % width, s]
        return rcopy(upiece(s, g), slot, sc_send.at[s, g], sc_recv.at[q % width, s], (g * 2 + h, c))

    def raised(t, s, src):
        return rcopy(src, piece(2 * t + h, s, q), lift.at[s, t], full0.at[t, s, q], (r, 1 - c))

    def lift_full(t, s, g, sem, dev):
        p = piece(2 * t + h, s, g)
        return rcopy(p, p, sem.at[t, s], full0.at[t, s, g], dev)

    def lift_half(t, s, g, k, sem, dev):
        rows = pl.ds(pl.multiple_of(g * wq + k * (wq // 2), wq // 2), wq // 2)
        p = us.at[2 * t + h, s, 0, :, rows, :]
        return rcopy(p, p, sem.at[t, s], half0.at[t, s, k], dev)

    def side(t, s, kk, b):
        return rcopy(us.at[b, s, kk], us.at[b, s, kk], side_send.at[t, s, kk], side_recv.at[t, s, kk], sib)

    def x_swap(m, p):
        return rcopy(row_ref.at[m, p], x0.at[m, p], x_send.at[m, p], x_recv.at[m, p], (r, 1 - c))

    def p_up(b, s, m):
        return rcopy(ps.at[b, s, m], pr.at[b, s, m], p_send.at[b, s, m], p_recv.at[b, s, m], (r, c + 1))

    def l_down(o):
        rows = pl.ds(pl.multiple_of(o * wc, wc), wc)
        return rcopy(up_ref.at[0, h, rows, :], lg.at[h, c], l_send.at[o], l_recv.at[c], (r, o))

    def l_part(j, g):
        return lg.at[h, j, pl.ds(pl.multiple_of(g * wq, wq), wq), :]

    def l_up(o):
        rows = pl.ds(pl.multiple_of(o * wc + q * wq, wq), wq)
        return rcopy(up_ref.at[0, h, rows, :], l_part(c, q), l_send.at[o], l_recv.at[c], (r, o))

    def g_out(j, d):
        return rcopy(l_part(j, q), l_part(j, q), g_send.at[j, d], g_recv.at[j, q], (ahead(d) * 2 + h, c))

    def l_sib(j, comp):
        return rcopy(lg.at[comp, j], lg.at[comp, j], l_side.at[j], l_got.at[j], sib)

    def l_own():
        rows = pl.ds(pl.multiple_of(c * wc, wc), wc)
        return pltpu.make_async_copy(up_ref.at[0, :, rows, :], lg.at[:, c], l_loc.at[0])

    def others(body):
        each(1, n_cols, lambda k: body((c + k) % n_cols))

    def q_up(m):
        return rcopy(pq.at[m], pin.at[m], q_send.at[m], q_recv.at[m], (r, 1))

    def k_out(j, m):
        return rcopy(ks.at[j, m], kd.at[c, m], k_send.at[j, m], k_recv.at[c, m], (r, j))

    def k_next(j, m):
        to = (r, jnp.where(c == 0, 1, n_cols - 2))
        return rcopy(ks.at[j, m], ku.at[j, m], k_send.at[j, m], ku_recv.at[j, m], to)

    def join(j, m):
        k_next(j, m).wait_recv()
        ks[j, m] = ks[j, m] + ku[j, m]

        @pl.when(j != c)
        def _():
            k_out(j, m).start()

    def e_out(k):
        return rcopy(eb.at[c], eb.at[c], e_send.at[k], e_recv.at[c], (r, (c + k) % n_cols))

    row_in = pltpu.make_async_copy(row_ref, rows, in_sem.at[0])
    col_in = pltpu.make_async_copy(col_ref, cols, in_sem.at[1])
    col_in.start()
    row_in.start()
    l_own().start()
    barrier = pltpu.get_barrier_semaphore()

    def signal(dev):
        pl.semaphore_signal(barrier, inc=1, device_id=dev, device_id_type=MESH)

    signal(sib)
    each(1, chips, lambda d: signal((ahead(d) * 2 + h, c)))
    each(1, n_cols, lambda k: signal((r, (c + k) % n_cols)))

    @pl.when(c < 2)
    def _():
        each(1, chips, lambda d: signal((ahead(d) * 2 + h, 1 - c)))

    pl.semaphore_wait(barrier, 1 + (chips - 1) + (n_cols - 1) + jnp.where(c < 2, chips - 1, 0))

    def native_x(i):
        t, s = ts(i)

        @pl.when(jnp.logical_and(active(i), q == t))
        def _():
            nat_out(s).start()
            local_u(s).start()

    def native_y(i):
        t, s = ts(i)

        @pl.when(jnp.logical_and(active(i), q == t))
        def _():
            for k in range(2):
                nat_near(s, k).start()

    def native_out(i):
        native_x(i)
        native_y(i)

    def lift_in(i):
        t, s = ts(i)

        @pl.when(lifted(i))
        def _():
            lift_full(t, s, q, lift_x, sib).wait_recv()
            lift_full(t, s, q, lift_x, to_x).start()
            lift_full(t, s, q, lift_y, to_y).start()

    def relay_x(i):
        t, s = ts(i)

        @pl.when(jnp.logical_and(c == 0, xn == t))
        def _():
            nat_full(t, s).wait_recv()
            nat_half(t, s, 0, half1, to_y).start()

            @pl.when(t == 0)
            def _():
                nat_half(t, s, 1, half1, to_y).start()

    def relay_native(i):
        t, s = ts(i)

        @pl.when(jnp.logical_and(active(i), yn == t))
        def _():
            nat_half(t, s, 0, near1).wait_recv()

            @pl.when(c > 0)
            def _():
                nat_half(t, s, 0, half1).start()

            nat_half(t, s, 1, near1).wait_recv()

            @pl.when(jnp.logical_or(c > 0, t > 0))
            def _():
                nat_half(t, s, 1, half1).start()

        @pl.when(jnp.asarray(i) < width)
        def _():
            relay_x(i)

    def relay_lift(i):
        t, s = ts(i)

        @pl.when(lifted(i))
        def _():
            lift_full(t, s, xn, lift_x, sib).wait_recv()
            lift_half(t, s, xn, 0, lift_fy, to_y).start()
            lift_full(t, s, yn, lift_x, sib).wait_recv()
            lift_half(t, s, yn, 1, lift_fx, to_x).start()

    def collect(i):
        t, s = ts(i)

        @pl.when(active(i))
        def _():
            @pl.when(dn == t)
            def _():
                for k in range(2):
                    nat_half(t, s, k, half1).wait_recv()

            @pl.when(q == t)
            def _():
                local_u(s).wait()

            @pl.when(jnp.logical_and(c > 0, xn == t))
            def _():
                nat_full(t, s).wait_recv()

            side(t, s, 1, 2 * t + h).start()

        @pl.when(lifted(i))
        def _():
            lift_half(t, s, dn, 0, lift_fy, sib).wait_recv()
            lift_half(t, s, dn, 1, lift_fx, sib).wait_recv()
            side(t, s, 0, 2 * t + h).start()

    source = jnp.where(c == 0, q > 1, jnp.logical_and(c == 1, q == 1))

    def scatters(s):
        @pl.when(source)
        def _():
            each(1, chips, lambda d: scatter(s, ahead(d)).start())

    for s in range(nsub):
        scatters(s)

    each(0, stages, lambda i: pl.when(jnp.logical_or(c > 1, i < width))(lambda: native_out(i)))

    def climb(t, s):
        @pl.when(q == t)
        def _():
            raised(t, s, upiece(s, q)).start()

        @pl.when(q != t)
        def _():
            rcopy(stg.at[t % width, s], stg.at[t % width, s], lift.at[s, t], sc_recv.at[t % width, s], sib).wait_recv()
            raised(t, s, stg.at[t % width, s]).start()

    @pl.when(c == 0)
    def _():
        for s in range(nsub):
            for t in range(n_cols - 1, 1, -1):
                climb(t, s)
            for p in range(2):
                x_swap(s, p).start()

    @pl.when(c == 1)
    def _():
        for s in range(nsub):
            climb(1, s)
        for m in range(tiles):
            for p in range(2):
                x_swap(m, p).start()

    each(c + 1, n_cols, lambda o: l_up(o).start())

    @pl.when(c == 1)
    def _():
        l_down(0).start()

    col_in.wait()
    pos = c * wc + lax.broadcasted_iota(jnp.int32, (wc, ranks), 0)
    parts = []
    for i in range(tiles):
        hit = pos == piv_ref[i:i + 1, :]
        for p in range(2):
            parts.append(jnp.sum(jnp.where(hit, cols[i, p], 0.0), axis=0, keepdims=True))
    parts.append(jnp.zeros((eb.shape[1] - 2 * tiles, ranks), jnp.float32))
    eb[c] = jnp.concatenate(parts, axis=0)
    each(1, n_cols, lambda k: e_out(k).start())

    def spread(j):
        rcopy(l_part(j, q), l_part(j, q), l_send.at[c], l_recv.at[j], sib).wait_recv()
        each(1, chips, lambda d: g_out(j, d).start())

    @pl.when(c < 2)
    def _():
        for i in range(width):
            lift_in(i)

            @pl.when(c == 0)
            def _():
                native_x(width + i)

        relay_native(0)

        @pl.when(c == 1)
        def _():
            relay_lift(0)

        @pl.when(c == 0)
        def _():
            relay_lift(0)
            relay_lift(1)
            relay_native(1)
            for i in range(width, stages):
                native_y(i)
            for i in range(width, stages):
                relay_x(i)

        @pl.when(c == 1)
        def _():
            for i in range(1, width):
                relay_native(i)
                relay_lift(i)
            for i in range(width, stages):
                native_out(i)

        collect(0)

        @pl.when(c == 0)
        def _():
            for i in range(1, width):
                collect(i)

    @pl.when(c > 1)
    def _():
        each(0, stages, relay_native)
        each(0, c, lambda o: l_down(o).start())
        each(0, stages, collect)
        each(0, c, spread)


    row_in.wait()
    for m in range(tiles):
        for p in range(2):
            a, b = split(rows[m, p])
            xs[1, m, p * ranks:(p + 1) * ranks, :] = a
            xs[1, m, (p + 2) * ranks:(p + 3) * ranks, :] = b

    def gather():
        l_own().wait()

        def low(j):
            each(1, chips, lambda d: rcopy(
                l_part(j, ahead(d)), l_part(j, ahead(d)), g_send.at[j, d], g_recv.at[j, ahead(d)], sib
            ).wait_recv())
            l_sib(j, h).start()

        def high(j):
            rcopy(lg.at[h, j], lg.at[h, j], l_send.at[c], l_recv.at[j], sib).wait_recv()
            l_sib(j, h).start()

        each(0, c, low)
        each(c + 1, n_cols, high)

    def gathered():
        each(0, c, lambda j: l_sib(j, 1 - h).wait_recv())
        each(c + 1, n_cols, lambda j: l_sib(j, 1 - h).wait_recv())

    def entries_in():
        each(1, n_cols, lambda k: rcopy(
            eb.at[(c + k) % n_cols], eb.at[(c + k) % n_cols], e_send.at[k], e_recv.at[(c + k) % n_cols], sib
        ).wait_recv())

    def scaled(t, m):
        entries = jnp.sum(eb[...], axis=0)
        lines = []
        levels = lax.broadcasted_iota(jnp.int32, (1, ranks), 1)
        for i in range(tiles):
            er, ei = entries[2 * i:2 * i + 1], entries[2 * i + 1:2 * i + 2]
            keep = (levels < RANK_STEP * rank_ref[i]).astype(jnp.float32)
            mag = jnp.maximum(er * er + ei * ei, 1.0)
            lines.append(keep * er / mag)
            lines.append(-keep * ei / mag)
        factor_r, factor_i = lines[0], lines[1]
        for i in range(1, tiles):
            factor_r = jnp.where(m == i, lines[2 * i], factor_r)
            factor_i = jnp.where(m == i, lines[2 * i + 1], factor_i)
        pad = jnp.zeros((126, ranks), jnp.float32)
        turned = jnp.concatenate([factor_r, factor_i, pad], axis=0).T
        fr, fi = turned[:, 0:1], turned[:, 1:2]
        vr, vi = [], []
        for hh in range(2):
            for s in range(nsub):
                vr.append(ps[2 * t + hh, s, m, 0])
                vi.append(ps[2 * t + hh, s, m, 1])
        vr, vi = jnp.concatenate(vr, axis=1), jnp.concatenate(vi, axis=1)
        wr = vr * fr - vi * fi
        wi = vr * fi + vi * fr
        return wr, wi

    def finish_next(m):
        @pl.when(m == 0)
        def _():
            entries_in()

        wr, wi = scaled(c + 1, m)
        pq[m, 0] = wr
        pq[m, 1] = wi
        q_up(m).start()

    def finish(m):
        @pl.when(m == 0)
        def _():
            gathered()

            @pl.when(c > 0)
            def _():
                entries_in()

        @pl.when(c == 1)
        def _():
            q_up(m).wait_recv()
            panel_ref[m] = pin[m]

        @pl.when(c != 1)
        def _():
            wr, wi = scaled(c, m)
            panel_ref[m, 0] = wr
            panel_ref[m, 1] = wi

        for p in range(2):
            a, b = split(panel_ref[m, p])
            cs[p * ranks:(p + 1) * ranks, :] = a
            cs[(p + 2) * ranks:(p + 3) * ranks, :] = b

        def core(index, carry):
            j = jnp.where(c == n_cols - 1, index, (n_cols - index) % n_cols)
            @pl.when(m == 0)
            def _():
                for p in range(2):
                    uh, ul = split(lg[p, j])
                    lc[j, 0, :, p * rank2:(p + 1) * rank2] = uh
                    lc[j, 1, :, p * rank2:(p + 1) * rank2] = ul

            prod = stacked(cs[...], lc[j, 0], lc[j, 1])
            ks[j, m, 0] = prod[:ranks, :rank2] - prod[ranks:, rank2:]
            ks[j, m, 1] = prod[:ranks, rank2:] + prod[ranks:, :rank2]

            @pl.when(jnp.logical_and(c == 1, j > 0))
            def _():
                join(j, m)

            ends = jnp.logical_or(c == 0, c == n_cols - 1)

            @pl.when(jnp.logical_and(ends, j != c))
            def _():
                k_next(j, m).start()

            @pl.when(jnp.logical_or(jnp.logical_and(c == 1, j == 0), jnp.logical_and(c == n_cols - 2, j > c)))
            def _():
                k_out(j, m).start()

            return carry

        lax.fori_loop(0, n_cols, core, 0)

    half = width * tiles
    total = 2 * half
    final0 = jnp.where(c == 0, half + nsub - 1, (nsub - 1) * half + n_cols - 1 - c)
    final0 = jnp.where(c == 1, total, final0)

    def unit(u, carry):
        i = u // half * width + u % width
        m = u // width % tiles
        t, s = ts(i)

        @pl.when(jnp.logical_and(active(i), u < total))
        def _():
            @pl.when(jnp.logical_and(c < 2, jnp.logical_and(u < half, u % width == 0)))
            def _():
                for p in range(2):
                    x_swap(m, p).wait_recv()
                    a, b = split(x0[m, p])
                    xs[0, m, p * ranks:(p + 1) * ranks, :] = a
                    xs[0, m, (p + 2) * ranks:(p + 3) * ranks, :] = b

            for e in range(2):
                b = 2 * t + (h + e) % 2

                if e == 1:
                    @pl.when(m == 0)
                    def _():
                        side(t, s, 1, b).wait_recv()

                        @pl.when(lifted(i))
                        def _():
                            side(t, s, 0, b).wait_recv()

                def product(kk):
                    @pl.when(m == 0)
                    def _():
                        for p in range(2):
                            uh, ul = split(us[b, s, kk, p])
                            uc[i, e, kk, 0, :, p * sw:(p + 1) * sw] = uh
                            uc[i, e, kk, 1, :, p * sw:(p + 1) * sw] = ul

                    prod = stacked(xs[kk, m], uc[i, e, kk, 0], uc[i, e, kk, 1])
                    real = prod[:ranks, :sw] - prod[ranks:, sw:]
                    imag = prod[:ranks, sw:] + prod[ranks:, :sw]
                    return real, imag

                real, imag = product(1)

                @pl.when(lifted(i))
                def _():
                    real0, imag0 = product(0)
                    ps[b, s, m, 0] = real + real0
                    ps[b, s, m, 1] = imag + imag0

                @pl.when(jnp.logical_and(c == 0, t == 0))
                def _():
                    ps[b, s, m, 0] = real
                    ps[b, s, m, 1] = imag

                @pl.when(c > 1)
                def _():
                    p_up(b, s, m).wait_recv()
                    ps[b, s, m, 0] = real + pr[b, s, m, 0]
                    ps[b, s, m, 1] = imag + pr[b, s, m, 1]

                @pl.when(jnp.logical_and(t > c, c > 0))
                def _():
                    p_up(b, s, m).start()

        @pl.when(jnp.logical_and(c == 0, jnp.logical_and(u < half, u % width == width - 1)))
        def _():
            finish_next(m)

        @pl.when(jnp.logical_or(u == final0, u == final0 + width))
        def _():
            finish(m)

        @pl.when(jnp.logical_and(c == 0, jnp.logical_and(u >= width, u < half)))
        def _():
            relay_native(u)

        @pl.when(jnp.logical_and(c == n_cols - 2, u >= total - 2))
        def _():
            each(0, c + 1, lambda j: join(j, u - total + 2))

        @pl.when(jnp.logical_and(c == 1, jnp.logical_or(u == 0, u == half)))
        def _():
            base = u // half * width
            for k in range(1, width):
                collect(base + k)

        @pl.when(u == jnp.where(c == 0, half, jnp.where(c == 1, total - 1, width - 1)))
        def _():
            gather()

        @pl.when(jnp.logical_and(c == 1, u == 0))
        def _():
            for i in range(width, stages):
                lift_in(i)

        @pl.when(jnp.logical_and(c == 1, u == width - 1))
        def _():
            for i in range(width, stages):
                relay_native(i)
                relay_lift(i)

        @pl.when(jnp.logical_and(c < 2, u == half - 1))
        def _():
            collect(width)

            @pl.when(c == 0)
            def _():
                for i in range(width + 1, stages):
                    collect(i)

            each(0, jnp.where(c == 1, 1, 0), spread)

        return carry

    lax.fori_loop(0, jnp.where(c == 1, total + 2 * width - 1, total), unit, 0)

    @pl.when(c < 2)
    def _():
        for m in range(tiles):
            for p in range(2):
                x_swap(m, p).wait_send()
        for s in range(nsub):
            for t in range(1, n_cols):
                @pl.when(c == (0 if t > 1 else 1))
                def _():
                    raised(t, s, stg.at[t % width, s]).wait_send()

    @pl.when(c == 0)
    def _():
        for m in range(tiles):
            q_up(m).wait_send()

    @pl.when(source)
    def _():
        for s in range(nsub):
            each(1, chips, lambda d: scatter(s, ahead(d)).wait_send())

    def drain(i):
        t, s = ts(i)

        @pl.when(active(i))
        def _():
            @pl.when(q == t)
            def _():
                nat_out(s).wait_send()
                for k in range(2):
                    nat_near(s, k).wait_send()

            @pl.when(jnp.where(jnp.logical_and(c == 0, t == 0), xn == t, yn == t))
            def _():
                nat_half(t, s, 1, half1).wait_send()

            @pl.when(jnp.where(c == 0, xn == t, yn == t))
            def _():
                nat_half(t, s, 0, half1).wait_send()

            side(t, s, 1, 2 * t + h).wait_send()

            @pl.when(lifted(i))
            def _():
                lift_full(t, s, q, lift_x, sib).wait_send()
                lift_full(t, s, q, lift_y, sib).wait_send()
                lift_half(t, s, xn, 0, lift_fy, sib).wait_send()
                lift_half(t, s, yn, 1, lift_fx, sib).wait_send()
                side(t, s, 0, 2 * t + h).wait_send()

            @pl.when(jnp.logical_and(t > c, c > 0))
            def _():
                for m in range(tiles):
                    for e in range(2):
                        p_up(2 * t + e, s, m).wait_send()

    each(0, stages, drain)

    def tail_l(j):
        each(1, chips, lambda d: g_out(j, d).wait_send())
        l_down(j).wait_send()

    each(0, c, tail_l)
    each(c + 1, n_cols, lambda o: l_up(o).wait_send())

    def tail_k(j):
        l_sib(j, h).wait_send()
        for m in range(tiles):
            k_out(j, m).wait_send()

    others(tail_k)
    each(1, n_cols, lambda k: e_out(k).wait_send())

    for m in range(tiles):
        cores_ref[m, 0] = ks[c, m]

        def add(o):
            @pl.when(jnp.logical_and(o > 0, o < n_cols - 1))
            def _():
                rcopy(ks.at[c, m], kd.at[o, m], k_send.at[c, m], k_recv.at[o, m], sib).wait_recv()
                cores_ref[m, 0] = cores_ref[m, 0] + kd[o, m]

        others(add)


def paired(n_rows, n_cols, col_samples, row_samples, pivot_rows, rank_blocks, upper_inverse, upanel_left):
    tiles, _, ranks, wc = row_samples.shape
    wr = upper_inverse.shape[2]
    left_ranks = upanel_left.shape[3]
    chips = n_rows // 2
    nsub = wr // 128
    sw = wr // nsub
    f32, bf16 = jnp.float32, jnp.bfloat16
    dma = pltpu.SemaphoreType.DMA
    vmem = pl.BlockSpec(memory_space=pltpu.VMEM)
    hbm = pl.BlockSpec(memory_space=pl.ANY)
    sums = pltpu.VMEM((n_rows, nsub, tiles, 2, ranks, sw), f32)
    return pl.pallas_call(
        functools.partial(paired_kernel, n_rows, n_cols),
        out_shape=(
            jax.ShapeDtypeStruct((tiles, 2, ranks, wc), f32),
            jax.ShapeDtypeStruct((tiles, 1, 2, ranks, left_ranks), f32),
        ),
        in_specs=[hbm, hbm, hbm, hbm, vmem, pl.BlockSpec(memory_space=pltpu.SMEM)],
        out_specs=(vmem, vmem),
        scratch_shapes=[
            pltpu.VMEM(row_samples.shape, f32),
            pltpu.VMEM(col_samples.shape, f32),
            dma((2,)),
            pltpu.VMEM((2, tiles, 4 * ranks, wc), bf16),
            pltpu.VMEM((tiles, 2, ranks, wc), f32),
            pltpu.VMEM((4 * ranks, wc), bf16),
            pltpu.VMEM((n_rows, nsub, 2, 2, wc, sw), f32),
            pltpu.VMEM((2 * nsub, 2, 2, 2, wc, 2 * sw), bf16),
            pltpu.VMEM((n_cols, 2, wc, 2 * left_ranks), bf16),
            pltpu.VMEM((n_cols - 2, nsub, 2, wc // chips, sw), f32),
            sums,
            sums,
            pltpu.VMEM((tiles, 2, ranks, wc), f32),
            pltpu.VMEM((tiles, 2, ranks, wc), f32),
            pltpu.VMEM((2, n_cols, wc, left_ranks), f32),
            pltpu.VMEM((n_cols, tiles, 2, ranks, left_ranks), f32),
            pltpu.VMEM((n_cols, tiles, 2, ranks, left_ranks), f32),
            pltpu.VMEM((n_cols, tiles, 2, ranks, left_ranks), f32),
            pltpu.VMEM((n_cols, -(-2 * tiles // 8) * 8, ranks), f32),
            dma((nsub,)), dma((nsub,)), dma((nsub, 2)), dma((n_cols, nsub, 2)), dma((n_cols, nsub)),
            dma((n_cols, nsub, 2)), dma((n_cols, nsub, 2)),
            dma((nsub, n_cols)), dma((nsub, chips)), dma((n_cols - 2, nsub)),
            dma((n_cols, nsub, chips)), dma((n_cols, nsub, 2)),
            dma((n_cols, nsub)), dma((n_cols, nsub)), dma((n_cols, nsub)), dma((n_cols, nsub)),
            dma((n_cols, nsub, 2)), dma((n_cols, nsub, 2)), dma((tiles, 2)), dma((tiles, 2)),
            dma((n_rows, nsub, tiles)), dma((n_rows, nsub, tiles)), dma((tiles,)), dma((tiles,)),
            dma((1,)), dma((n_cols,)), dma((n_cols,)), dma((n_cols, chips)), dma((n_cols, chips)),
            dma((n_cols,)), dma((n_cols,)),
            dma((n_cols, tiles)), dma((n_cols, tiles)), dma((n_cols, tiles)), dma((n_cols,)), dma((n_cols,)),
        ],
        compiler_params=pltpu.CompilerParams(
            collective_id=0, has_side_effects=True, vmem_limit_bytes=60 * 1024 * 1024
        ),
    )(row_samples, upper_inverse, upanel_left, col_samples, pivot_rows, rank_blocks)


def on_device(n_rows, n_cols, col_samples, row_samples, pivot_rows, rank_blocks, upper_inverse, upanel_left):
    tiles, _, ranks, wc = row_samples.shape
    wr = upper_inverse.shape[2]
    left_ranks = upanel_left.shape[3]
    chips = n_rows // 2
    if chips != n_cols or wc != 2 * wr:
        raise ValueError("unsupported mesh")
    if chips == 4 and wr == 128 * (n_cols - 2):
        return paired(
            n_rows, n_cols, col_samples, row_samples, pivot_rows, rank_blocks, upper_inverse, upanel_left
        )
    nsub = max(wr // 128, 1)
    sw = wr // nsub
    wq = wc // chips
    m = 2 * tiles * ranks
    f32, bf16 = jnp.float32, jnp.bfloat16
    dma = pltpu.SemaphoreType.DMA
    vmem = pl.BlockSpec(memory_space=pltpu.VMEM)
    hbm = pl.BlockSpec(memory_space=pl.ANY)
    return pl.pallas_call(
        functools.partial(kernel, n_rows, n_cols),
        out_shape=(
            jax.ShapeDtypeStruct((tiles, 2, ranks, wc), f32),
            jax.ShapeDtypeStruct((tiles, 1, 2, ranks, left_ranks), f32),
        ),
        in_specs=[vmem, hbm, hbm, vmem, vmem, pl.BlockSpec(memory_space=pltpu.SMEM)],
        out_specs=(vmem, vmem),
        scratch_shapes=[
            pltpu.VMEM((m, wc), bf16),
            pltpu.VMEM((m, wc), bf16),
            pltpu.VMEM((m, wc), bf16),
            pltpu.VMEM((m, wc), bf16),
            pltpu.VMEM((n_rows, nsub, 2, wc, sw), f32),
            pltpu.VMEM((n_rows, nsub, m, sw), f32),
            pltpu.VMEM((n_rows, nsub, m, sw), f32),
            pltpu.VMEM((m, sw), f32),
            pltpu.VMEM((n_cols, wq, left_ranks), f32),
            pltpu.VMEM((2, chips, n_cols, wq, left_ranks), f32),
            pltpu.VMEM((n_cols, tiles, 2, ranks, left_ranks), f32),
            pltpu.VMEM((n_cols, tiles, 2, ranks, left_ranks), f32),
            pltpu.VMEM((n_cols, -(-2 * tiles // 8) * 8, ranks), f32),
            dma((nsub,)), dma((chips, nsub)), dma((nsub,)), dma((chips, nsub)), dma((n_rows, nsub)),
            dma((n_rows, nsub)), dma((n_rows, nsub)),
            dma((1,)), dma((n_cols,)), dma((n_cols,)), dma((1,)), dma((chips,)), dma((1,)), dma((chips,)),
            dma((2, chips)),
            dma((n_cols,)), dma((n_cols,)), dma((n_cols,)), dma((n_cols,)),
        ],
        compiler_params=pltpu.CompilerParams(
            collective_id=0, has_side_effects=True, vmem_limit_bytes=56 * 1024 * 1024
        ),
    )(row_samples, upper_inverse, upanel_left, col_samples, pivot_rows, rank_blocks)


def solution(mesh):
    in_specs = (
        P("row", None, "col", None),
        P("row", None, None, "col"),
        P("row", None),
        P("row"),
        P(None, "col", "row"),
        P("col", None, None, None),
    )
    out_specs = (P("row", None, None, "col"), P("row", "col", None, None, None))
    body = functools.partial(on_device, mesh.shape["row"], mesh.shape["col"])
    return jax.shard_map(body, mesh=mesh, in_specs=in_specs, out_specs=out_specs, check_vma=False)
```
